32 devices in a mesh: dp: 16 (over z, y, core), mp: 2 (over x).
Axes of the slice: x: 2, y: 2, z: 4, core: 2. Of those that a mesh axis runs over, the one named last changes fastest.
Arguments:
- inputs: float32 [32, 1024, 1536], P('dp', 'mp'), may hold values from -6 to 6
- text_states: float32 [32, 64, 1536], P('dp', 'mp'), may hold values from -6 to 6
- cotangent: float32 [32, 1024, 1536], P('dp', 'mp'), may hold values from -6 to 6
- norm_params: float32 [1536, 6], P('dp'), as said below
- self_query_key: float32 [1536, 2, 1536], P('dp', None, 'mp')
- self_value: float32 [1536, 1536], P('dp', 'mp'), may hold values from -0.15625 to 0.15625
- self_output: float32 [1536, 1536], P('dp', 'mp'), may hold values from -1.25 to 1.25
- cross_query: float32 [1536, 1536], P('dp', 'mp')
- cross_key_value: float32 [1536, 2, 1536], P('dp', None, 'mp')
- cross_output: float32 [1536, 1536], P('dp', 'mp'), may hold values from -0.625 to 0.625
- hidden_in: float32 [1536, 6144], P('dp', 'mp'), may hold values from -0.15625 to 0.15625
- hidden_out: float32 [1536, 6144], P('dp', 'mp'), may hold values from -0.078125 to 0.078125
Outputs:
- output: float32 [32, 1024, 1536], P('dp', 'mp')
- grad_inputs: float32 [32, 1024, 1536], P('dp', 'mp')
- grad_text: float32 [32, 64, 1536], P('dp', 'mp')
- grad_norm_params: float32 [1536, 6], P('dp')
- grad_self_query_key: float32 [1536, 2, 1536], P('dp', None, 'mp')
- grad_self_value: float32 [1536, 1536], P('dp', 'mp')
- grad_self_output: float32 [1536, 1536], P('dp', 'mp')
- grad_cross_query: float32 [1536, 1536], P('dp', 'mp')
- grad_cross_key_value: float32 [1536, 2, 1536], P('dp', None, 'mp')
- grad_cross_output: float32 [1536, 1536], P('dp', 'mp')
- grad_hidden_in: float32 [1536, 6144], P('dp', 'mp')
- grad_hidden_out: float32 [1536, 6144], P('dp', 'mp')
- factors: float32 [2, 24], P(None, 'mp')
- clipped_self_query_key: float32 [1536, 2, 1536], P('dp', None, 'mp')
- clipped_cross_query: float32 [1536, 1536], P('dp', 'mp')
- clipped_cross_key: float32 [1536, 1536], P('dp', 'mp')
The draws below stay inside these ranges and needn't reach their ends.
Inputs may be any that keep to these rules, and one draw needn't show every extreme that they name: `norm_params`: columns hold gain, bias, gain, bias, gain, bias of the three norms.
All inputs are finite; a program needn't handle non-finite values.
Results may differ from the reference program's by a relative error of at most 0.029.
Values may be sent and summed in bfloat16 or wider, within the bound.
A program may use at most 384 MiB of HBM per device.

```python
import math
import jax
import jax.numpy as jnp
from jax import lax

D = 1536
HEADS = 24
FF = 6144
TEXT = 64
FRAMES = 1024
CLIPS = 32


def head_scaled(key, groups_count):
    noise_key, scale_key = jax.random.split(key)
    noise_rows = jax.random.truncated_normal(noise_key, -4.0, 4.0, (D, groups_count, D), jnp.float32) * D ** (-0.5)
    scales = jnp.exp(jax.random.uniform(scale_key, (groups_count, HEADS), jnp.float32, math.log(0.7), math.log(1.7)))
    return noise_rows * jnp.repeat(scales, D // HEADS, axis=1)[None, :, :]


def draw_norm_params(key, part):
    gain_key, bias_key = jax.random.split(key)
    gain_cols = 1.0 + 0.1 * jax.random.truncated_normal(gain_key, -4.0, 4.0, (D, 3), jnp.float32)
    biases = 0.3 * jax.random.truncated_normal(bias_key, -4.0, 4.0, (D, 3), jnp.float32)
    return jnp.stack([gain_cols, biases], axis=2).reshape(D, 6)


def draw_self_query_key(key, part):
    return head_scaled(key, 2)


def draw_cross_query(key, part):
    return head_scaled(key, 1)[:, 0, :]


def draw_cross_key_value(key, part):
    scaled = head_scaled(jax.random.fold_in(key, 1), 1)
    drawn_rows = jax.random.truncated_normal(jax.random.fold_in(key, 2), -4.0, 4.0, (D, 1, D), jnp.float32) * D ** (-0.5)
    return jnp.concatenate([scaled, drawn_rows], axis=1)


def block_levels(stream_key, shape, cuts, least, largest):
    factor_of, own = 1.0, jax.random.fold_in(stream_key, 6)
    for axis_at, parts in cuts:
        steps = jnp.exp(jax.random.uniform(jax.random.fold_in(own, axis_at), (parts,), jnp.float32, least / len(cuts), largest / len(cuts)))
        factor_of = factor_of * jnp.repeat(steps, shape[axis_at] // parts).reshape([-1 if axis == axis_at else 1 for axis in range(len(shape))])
    return factor_of


def normal_values(stream_key, dims, deviation, reach, shards=(), kind=jnp.bfloat16):
    level = block_levels(stream_key, dims, shards, -0.22, 0.18) if shards else 1.0
    values = jax.random.normal(stream_key, dims, jnp.float32) * deviation * level
    return jnp.minimum(jnp.maximum(values, -reach), reach).astype(kind)


def setup_inputs(seed: int = 0) -> dict:
    key_list = jax.random.split(jax.random.key(seed), 13)
    return {
        "inputs": normal_values(key_list[0], (CLIPS, FRAMES, D), 1.0, 6.0, ((0, 16), (1, 2)), jnp.float32),
        "text_states": normal_values(key_list[1], (CLIPS, TEXT, D), 1.0, 6.0, ((0, 16), (1, 2)), jnp.float32),
        "cotangent": normal_values(key_list[2], (CLIPS, FRAMES, D), 1.0, 6.0, ((0, 16), (1, 2)), jnp.float32),
        "norm_params": draw_norm_params(jax.random.fold_in(key_list[12], 71), 0),
        "self_query_key": draw_self_query_key(jax.random.fold_in(key_list[12], 71), 0),
        "self_value": normal_values(key_list[5], (D, D), D ** -0.5, 0.15625, ((0, 16), (1, 2)), jnp.float32),
        "self_output": normal_values(key_list[6], (D, D), (D // 64) ** -0.5, 1.25, ((0, 16), (1, 2)), jnp.float32),
        "cross_query": draw_cross_query(jax.random.fold_in(key_list[12], 71), 0),
        "cross_key_value": draw_cross_key_value(jax.random.fold_in(key_list[12], 71), 0),
        "cross_output": normal_values(key_list[9], (D, D), (D // 16) ** -0.5, 0.625, ((0, 16), (1, 2)), jnp.float32),
        "hidden_in": normal_values(key_list[10], (D, FF), D ** -0.5, 0.15625, ((0, 16), (1, 2)), jnp.float32),
        "hidden_out": normal_values(key_list[11], (D, FF), FF ** -0.5, 0.078125, ((0, 16), (1, 2)), jnp.float32),
    }


EPSILON = 1e-05
CLIP_LIMIT = 7.0
MASKED = -1e+30
HIGHEST = lax.Precision.HIGHEST

@jax.custom_vjp
def low(v):
    return lax.optimization_barrier(v.astype(jnp.bfloat16)).astype(jnp.float32)

@jax.custom_vjp
def low_back(v):
    return v

def low_keep(v):
    return (low(v), None)

def low_pass(kept, grad):
    return (grad,)

def back_keep(v):
    return (v, None)

def back_low(kept, grad):
    return (low(grad),)
low.defvjp(low_keep, low_pass)
low_back.defvjp(back_keep, back_low)

def layer_norm(stream_rows, gain_row, bias_row):
    center = stream_rows - lax.optimization_barrier(jnp.mean(stream_rows, axis=-1, keepdims=True))
    spread = lax.optimization_barrier(jnp.mean(center * center, axis=-1, keepdims=True))
    return center * lax.rsqrt(spread + EPSILON) * gain_row + bias_row

def gelu_exact(values):
    return 0.5 * values * (1.0 + lax.erf(values * 2.0 ** (-0.5)))

def softmax_rows(scores):
    highest = lax.optimization_barrier(jnp.max(scores, axis=-1, keepdims=True))
    exponents = jnp.exp(scores - highest)
    return exponents / lax.optimization_barrier(jnp.sum(exponents, axis=-1, keepdims=True))

def attend_clip(queries, keys_all, values_all, causal):
    scaling = (D // HEADS) ** (-0.5)
    scores = low_back(jnp.einsum('qhe,khe->hqk', queries, keys_all, precision=HIGHEST) * scaling)
    if causal:
        frame_count = queries.shape[0]
        allowed = jnp.arange(frame_count)[None, :] <= jnp.arange(frame_count)[:, None]
        scores = jnp.where(allowed[None], scores, MASKED)
    head_peaks = lax.optimization_barrier(jnp.max(scores, axis=(1, 2)))
    weights = softmax_rows(scores)
    mixed_heads = jnp.einsum('hqk,khe->qhe', low(weights), values_all, precision=HIGHEST)
    return (low(low_back(mixed_heads)), head_peaks)

def self_clip(queries, keys_all, values_all):
    return attend_clip(queries, keys_all, values_all, True)

def cross_clip(queries, keys_all, values_all):
    return attend_clip(queries, keys_all, values_all, False)

def by_clip(function, queries, keys_all, values_all):
    kept = jax.checkpoint(function)

    def single(triple):
        return kept(triple[0], triple[1], triple[2])
    return lax.map(single, (queries, keys_all, values_all))

def forward(weights, stream, states):
    norm_params, self_query_key, self_value, self_output, cross_query, cross_key_value, cross_output, hidden_in, hidden_out = [low(weight_item) for weight_item in weights]
    head_width = D // HEADS

    def split_heads(array):
        return array.reshape(array.shape[0], array.shape[1], HEADS, head_width)

    def merge_heads(array):
        return array.reshape(array.shape[0], array.shape[1], D)

    def project(array, matrix):
        return jnp.einsum('gld,de->gle', array, matrix, precision=HIGHEST)

    def unproject(array, matrix):
        return jnp.einsum('gle,de->gld', array, matrix, precision=HIGHEST)
    normed_self = low(layer_norm(stream, norm_params[:, 0], norm_params[:, 1]))
    queries = low(low_back(project(normed_self, self_query_key[:, 0])))
    self_keys = low(low_back(project(normed_self, self_query_key[:, 1])))
    values = low(low_back(project(normed_self, self_value)))
    mixed_self, self_peaks = by_clip(self_clip, split_heads(queries), split_heads(self_keys), split_heads(values))
    after_self = stream + low_back(unproject(merge_heads(mixed_self), self_output))
    normed_cross = low(layer_norm(after_self, norm_params[:, 2], norm_params[:, 3]))
    cross_queries = low(low_back(project(normed_cross, cross_query)))
    rounded_states = low(states)
    cross_keys = low(low_back(project(rounded_states, cross_key_value[:, 0])))
    cross_values = low(low_back(project(rounded_states, cross_key_value[:, 1])))
    mixed_cross, cross_peaks = by_clip(cross_clip, split_heads(cross_queries), split_heads(cross_keys), split_heads(cross_values))
    after_cross = after_self + low_back(unproject(merge_heads(mixed_cross), cross_output))
    normed_hidden = low(layer_norm(after_cross, norm_params[:, 4], norm_params[:, 5]))
    upward = low_back(project(normed_hidden, hidden_in))
    activated = low(gelu_exact(upward))
    result = after_cross + low_back(unproject(activated, hidden_out))
    return (result, (lax.optimization_barrier(jnp.max(self_peaks, axis=0)), lax.optimization_barrier(jnp.max(cross_peaks, axis=0))))

def reference(inputs, text_states, cotangent, norm_params, self_query_key, self_value, self_output, cross_query, cross_key_value, cross_output, hidden_in, hidden_out):
    weights = (norm_params, self_query_key, self_value, self_output, cross_query, cross_key_value, cross_output, hidden_in, hidden_out)
    group_size = math.gcd(CLIPS, 4)
    rounds = CLIPS // group_size
    blocks_in = (inputs.reshape(rounds, group_size, FRAMES, D), text_states.reshape(rounds, group_size, TEXT, D), cotangent.reshape(rounds, group_size, FRAMES, D))

    def advance(carried, block_inputs):
        totals, self_top, cross_top = carried
        stream, states, upstream = block_inputs
        result, pullback, head_peaks = jax.vjp(forward, weights, stream, states, has_aux=True)
        grad_weights, grad_stream, grad_states = pullback(upstream)
        totals = jax.tree.map(jnp.add, totals, grad_weights)
        return ((totals, jnp.maximum(self_top, head_peaks[0]), jnp.maximum(cross_top, head_peaks[1])), (result, grad_stream, grad_states))
    lowest = jnp.full((HEADS,), MASKED, dtype=jnp.float32)
    initial = (jax.tree.map(jnp.zeros_like, weights), lowest, lowest)
    (totals, self_top, cross_top), (results, grad_streams, grad_texts) = lax.scan(advance, initial, blocks_in)
    factors = CLIP_LIMIT / jnp.maximum(jnp.stack([self_top, cross_top]), CLIP_LIMIT)
    root_scales = jnp.repeat(jnp.sqrt(factors), D // HEADS, axis=1)
    clipped_self = self_query_key * root_scales[0][None, None, :]
    clipped_query = cross_query * root_scales[1][None, :]
    clipped_key = cross_key_value[:, 0] * root_scales[1][None, :]
    return (results.reshape(CLIPS, FRAMES, D), grad_streams.reshape(CLIPS, FRAMES, D), grad_texts.reshape(CLIPS, TEXT, D), totals[0], totals[1], totals[2], totals[3], totals[4], totals[5], totals[6], totals[7], totals[8], factors, clipped_self, clipped_query, clipped_key)
```

```python
import functools

import jax
import jax.numpy as jnp
from jax import lax
from jax.experimental import pallas as pl
from jax.experimental.pallas import tpu as pltpu
from jax.sharding import PartitionSpec as P

D = 1536
HEADS = 24


EPSILON = 1e-05
CLIP_LIMIT = 7.0
MASKED = -1e30


def layer_norm(stream_rows, gain_row, bias_row):
    center = stream_rows - jnp.mean(stream_rows, axis=-1, keepdims=True)
    spread = jnp.mean(center * center, axis=-1, keepdims=True)
    return center * lax.rsqrt(spread + EPSILON) * gain_row + bias_row


def gelu_exact(values):
    return 0.5 * values * (1.0 + lax.erf(values * 2.0 ** (-0.5)))


def rounded(values):
    return values.astype(jnp.bfloat16)


def project(array, matrix):
    return jnp.einsum("cld,de->cle", array, matrix, preferred_element_type=jnp.float32)


def unproject(array, matrix):
    return jnp.einsum("cle,de->cld", array, matrix, preferred_element_type=jnp.float32)


def outer_sum(left, right):
    return jnp.einsum("cld,cle->de", left, right, preferred_element_type=jnp.float32)


def widen(values):
    return lax.all_gather(values, "mp", axis=1, tiled=True)


def settle(partial_sum):
    return lax.psum_scatter(
        partial_sum.astype(jnp.bfloat16), "mp", scatter_dimension=1, tiled=True
    ).astype(jnp.float32)


def widen_grad(values):
    return lax.all_gather(values, "mp", axis=1, tiled=True)


def settle_grad(partial_sum):
    return lax.psum_scatter(
        partial_sum.astype(jnp.bfloat16), "mp", scatter_dimension=1, tiled=True
    ).astype(jnp.float32)


def self_forward(queries, keys_all, values_all):
    frame_count, head_count, head_width = (queries.shape[1], queries.shape[2], queries.shape[3])
    block_rows = min(512, frame_count)
    block_count = frame_count // block_rows
    scaling = head_width ** (-0.5)
    row_ids = jnp.arange(block_rows)
    col_ids = jnp.arange(frame_count)

    def per_clip(triple):
        clip_queries, clip_keys, clip_values = triple

        def per_block(block_index):
            offset = block_index * block_rows
            block_queries = lax.dynamic_slice_in_dim(clip_queries, offset, block_rows, 0)
            scores = (
                jnp.einsum(
                    "qhe,khe->hqk", block_queries, clip_keys, preferred_element_type=jnp.float32
                )
                * scaling
            )
            allowed = col_ids[None, :] <= (offset + row_ids)[:, None]
            scores = jnp.where(allowed[None], scores, MASKED)
            highest = jnp.max(scores, axis=2, keepdims=True)
            exponents = jnp.exp(scores - highest)
            row_sums = jnp.sum(exponents, axis=2, keepdims=True)
            mixed = jnp.einsum(
                "hqk,khe->qhe",
                rounded(exponents / row_sums),
                clip_values,
                preferred_element_type=jnp.float32,
            )
            return (
                mixed,
                (highest + jnp.log(row_sums))[:, :, 0],
                jnp.max(highest[:, :, 0], axis=1),
            )

        mixed, log_sums, block_peaks = lax.map(per_block, jnp.arange(block_count))
        return (
            mixed.reshape(frame_count, head_count, head_width),
            log_sums,
            jnp.max(block_peaks, axis=0),
        )

    mixed, log_sums, clip_peaks = lax.map(per_clip, (queries, keys_all, values_all))
    return (mixed, log_sums, jnp.max(clip_peaks, axis=0))


def self_backward(queries, keys_all, values_all, log_sums, grad_mixed):
    frame_count, head_count, head_width = (queries.shape[1], queries.shape[2], queries.shape[3])
    block_rows = min(512, frame_count)
    block_count = frame_count // block_rows
    scaling = head_width ** (-0.5)
    row_ids = jnp.arange(block_rows)
    col_ids = jnp.arange(frame_count)

    def per_clip(bundle):
        clip_queries, clip_keys, clip_values, clip_logs, clip_grads = bundle

        def per_block(carried, block_index):
            grad_keys, grad_values = carried
            offset = block_index * block_rows
            block_queries = lax.dynamic_slice_in_dim(clip_queries, offset, block_rows, 0)
            block_grads = lax.dynamic_slice_in_dim(clip_grads, offset, block_rows, 0)
            scores = (
                jnp.einsum(
                    "qhe,khe->hqk", block_queries, clip_keys, preferred_element_type=jnp.float32
                )
                * scaling
            )
            allowed = col_ids[None, :] <= (offset + row_ids)[:, None]
            scores = jnp.where(allowed[None], scores, MASKED)
            weights = jnp.exp(scores - clip_logs[block_index][:, :, None])
            grad_values = grad_values + jnp.einsum(
                "hqk,qhe->khe", rounded(weights), block_grads, preferred_element_type=jnp.float32
            )
            grad_weights = jnp.einsum(
                "qhe,khe->hqk", block_grads, clip_values, preferred_element_type=jnp.float32
            )
            centered = grad_weights - jnp.sum(weights * grad_weights, axis=2, keepdims=True)
            grad_scores = rounded(weights * centered)
            grad_queries = (
                jnp.einsum(
                    "hqk,khe->qhe", grad_scores, clip_keys, preferred_element_type=jnp.float32
                )
                * scaling
            )
            grad_keys = (
                grad_keys
                + jnp.einsum(
                    "hqk,qhe->khe", grad_scores, block_queries, preferred_element_type=jnp.float32
                )
                * scaling
            )
            return ((grad_keys, grad_values), grad_queries)

        zero_keys = jnp.zeros(clip_keys.shape, jnp.float32)
        (grad_keys, grad_values), grad_queries = lax.scan(
            per_block, (zero_keys, zero_keys), jnp.arange(block_count)
        )
        return (grad_queries.reshape(frame_count, head_count, head_width), grad_keys, grad_values)

    return lax.map(per_clip, (queries, keys_all, values_all, log_sums, grad_mixed))


def cross_forward(queries, keys_all, values_all):
    scaling = queries.shape[3] ** (-0.5)
    scores = (
        jnp.einsum("clhe,cshe->chls", queries, keys_all, preferred_element_type=jnp.float32)
        * scaling
    )
    highest = jnp.max(scores, axis=3, keepdims=True)
    exponents = jnp.exp(scores - highest)
    weights = exponents / jnp.sum(exponents, axis=3, keepdims=True)
    mixed = jnp.einsum(
        "chls,cshe->clhe", rounded(weights), values_all, preferred_element_type=jnp.float32
    )
    return (mixed, weights, jnp.max(highest, axis=(0, 2, 3)))


def cross_backward(queries, keys_all, values_all, weights, grad_mixed):
    scaling = queries.shape[3] ** (-0.5)
    grad_values = jnp.einsum(
        "chls,clhe->cshe", rounded(weights), grad_mixed, preferred_element_type=jnp.float32
    )
    grad_weights = jnp.einsum(
        "clhe,cshe->chls", grad_mixed, values_all, preferred_element_type=jnp.float32
    )
    centered = grad_weights - jnp.sum(weights * grad_weights, axis=3, keepdims=True)
    grad_scores = rounded(weights * centered)
    grad_queries = (
        jnp.einsum("chls,cshe->clhe", grad_scores, keys_all, preferred_element_type=jnp.float32)
        * scaling
    )
    grad_keys = (
        jnp.einsum("chls,clhe->cshe", grad_scores, queries, preferred_element_type=jnp.float32)
        * scaling
    )
    return (grad_queries, grad_keys, grad_values)


def per_device(
    inputs,
    text_states,
    cotangent,
    norm_params,
    self_query_key,
    self_value,
    self_output,
    cross_query,
    cross_key_value,
    cross_output,
    hidden_in,
    hidden_out,
):
    (
        full_norms,
        full_query_key,
        full_value,
        full_output,
        full_cross_query,
        full_cross_pair,
        full_cross_output,
        full_hidden_in,
        full_hidden_out,
    ) = (
        lax.all_gather(rounded(norm_params), "dp", axis=0, tiled=True),
        lax.all_gather(rounded(self_query_key), "dp", axis=0, tiled=True),
        lax.all_gather(rounded(self_value), "dp", axis=0, tiled=True),
        lax.all_gather(rounded(self_output), "dp", axis=0, tiled=True),
        lax.all_gather(rounded(cross_query), "dp", axis=0, tiled=True),
        lax.all_gather(rounded(cross_key_value), "dp", axis=0, tiled=True),
        lax.all_gather(rounded(cross_output), "dp", axis=0, tiled=True),
        lax.all_gather(rounded(hidden_in), "dp", axis=0, tiled=True),
        lax.all_gather(rounded(hidden_out), "dp", axis=0, tiled=True),
    )
    norm_rows = full_norms.astype(jnp.float32)
    head_width = D // HEADS
    head_count = full_value.shape[1] // head_width

    def split_heads(array):
        return array.reshape(array.shape[0], array.shape[1], head_count, head_width)

    def merge_heads(array):
        return array.reshape(array.shape[0], array.shape[1], head_count * head_width)

    normed, pull_self = jax.vjp(layer_norm, inputs, norm_rows[:, 0], norm_rows[:, 1])
    normed_self = widen(rounded(normed))
    query_key_rows = jnp.einsum(
        "cld,dte->clte", normed_self, full_query_key, preferred_element_type=jnp.float32
    )
    queries = rounded(query_key_rows[:, :, 0])
    self_keys = rounded(query_key_rows[:, :, 1])
    values = rounded(project(normed_self, full_value))
    mixed, log_sums, self_peaks = self_forward(
        split_heads(queries), split_heads(self_keys), split_heads(values)
    )
    mixed_self = rounded(merge_heads(mixed))
    after_self = inputs + settle(unproject(mixed_self, full_output))
    normed, pull_cross = jax.vjp(layer_norm, after_self, norm_rows[:, 2], norm_rows[:, 3])
    normed_cross = widen(rounded(normed))
    cross_queries = rounded(project(normed_cross, full_cross_query))
    states = lax.all_gather(rounded(text_states), "mp", axis=1, tiled=True)
    key_value_rows = jnp.einsum(
        "csd,dte->cste", states, full_cross_pair, preferred_element_type=jnp.float32
    )
    cross_keys = rounded(key_value_rows[:, :, 0])
    cross_values = rounded(key_value_rows[:, :, 1])
    attended, cross_weights, cross_peaks = cross_forward(
        split_heads(cross_queries), split_heads(cross_keys), split_heads(cross_values)
    )
    mixed_cross = rounded(merge_heads(attended))
    after_cross = after_self + settle(unproject(mixed_cross, full_cross_output))
    normed, pull_hidden = jax.vjp(layer_norm, after_cross, norm_rows[:, 4], norm_rows[:, 5])
    normed_hidden = widen(rounded(normed))
    upward = project(normed_hidden, full_hidden_in)
    activated, pull_gelu = jax.vjp(gelu_exact, upward)
    activated = rounded(activated)
    output = after_cross + settle(unproject(activated, full_hidden_out))
    self_top, cross_top = lax.pmax((self_peaks, cross_peaks), "dp")
    grad_branch = widen_grad(rounded(cotangent))
    grad_hidden_out = outer_sum(grad_branch, activated)
    grad_upward = rounded(pull_gelu(project(grad_branch, full_hidden_out))[0])
    grad_hidden_in = outer_sum(normed_hidden, grad_upward)
    grad_normed = settle_grad(unproject(grad_upward, full_hidden_in))
    back_stream, grad_gain_three, grad_bias_three = pull_hidden(grad_normed)
    grad_stream = cotangent + back_stream
    grad_branch = widen_grad(rounded(grad_stream))
    grad_cross_output = outer_sum(grad_branch, mixed_cross)
    grad_attended = rounded(project(grad_branch, full_cross_output))
    grad_queries, grad_keys, grad_values = cross_backward(
        split_heads(cross_queries),
        split_heads(cross_keys),
        split_heads(cross_values),
        cross_weights,
        split_heads(grad_attended),
    )
    grad_queries = rounded(merge_heads(grad_queries))
    grad_pair = rounded(jnp.stack([merge_heads(grad_keys), merge_heads(grad_values)], axis=2))
    grad_cross_query = outer_sum(normed_cross, grad_queries)
    grad_cross_pair = jnp.einsum(
        "csd,cste->dte", states, grad_pair, preferred_element_type=jnp.float32
    )
    grad_text = lax.psum_scatter(
        jnp.einsum(
            "cste,dte->csd", grad_pair, full_cross_pair, preferred_element_type=jnp.float32
        ).astype(jnp.bfloat16),
        "mp",
        scatter_dimension=1,
        tiled=True,
    ).astype(jnp.float32)
    grad_normed = settle_grad(unproject(grad_queries, full_cross_query))
    back_stream, grad_gain_two, grad_bias_two = pull_cross(grad_normed)
    grad_stream = grad_stream + back_stream
    grad_branch = widen_grad(rounded(grad_stream))
    grad_self_output = outer_sum(grad_branch, mixed_self)
    grad_mixed = rounded(project(grad_branch, full_output))
    grad_queries, grad_keys, grad_values = self_backward(
        split_heads(queries),
        split_heads(self_keys),
        split_heads(values),
        log_sums,
        split_heads(grad_mixed),
    )
    grad_pair = rounded(jnp.stack([merge_heads(grad_queries), merge_heads(grad_keys)], axis=2))
    grad_values = rounded(merge_heads(grad_values))
    grad_self_pair = jnp.einsum(
        "cld,clte->dte", normed_self, grad_pair, preferred_element_type=jnp.float32
    )
    grad_self_value = outer_sum(normed_self, grad_values)
    grad_normed = settle_grad(
        jnp.einsum("clte,dte->cld", grad_pair, full_query_key, preferred_element_type=jnp.float32)
        + unproject(grad_values, full_value)
    )
    back_stream, grad_gain_one, grad_bias_one = pull_self(grad_normed)
    grad_inputs = grad_stream + back_stream
    grad_norm_rows = lax.psum(
        jnp.stack(
            [
                grad_gain_one,
                grad_bias_one,
                grad_gain_two,
                grad_bias_two,
                grad_gain_three,
                grad_bias_three,
            ],
            axis=1,
        ).astype(jnp.bfloat16),
        "mp",
    )
    (
        shard_norms,
        shard_self_pair,
        shard_self_value,
        shard_self_output,
        shard_cross_query,
        shard_cross_pair,
        shard_cross_output,
        shard_hidden_in,
        shard_hidden_out,
    ) = (
        lax.psum_scatter(grad_norm_rows, "dp", scatter_dimension=0, tiled=True).astype(jnp.float32),
        lax.psum_scatter(
            grad_self_pair.astype(jnp.bfloat16), "dp", scatter_dimension=0, tiled=True
        ).astype(jnp.float32),
        lax.psum_scatter(
            grad_self_value.astype(jnp.bfloat16), "dp", scatter_dimension=0, tiled=True
        ).astype(jnp.float32),
        lax.psum_scatter(
            grad_self_output.astype(jnp.bfloat16), "dp", scatter_dimension=0, tiled=True
        ).astype(jnp.float32),
        lax.psum_scatter(
            grad_cross_query.astype(jnp.bfloat16), "dp", scatter_dimension=0, tiled=True
        ).astype(jnp.float32),
        lax.psum_scatter(
            grad_cross_pair.astype(jnp.bfloat16), "dp", scatter_dimension=0, tiled=True
        ).astype(jnp.float32),
        lax.psum_scatter(
            grad_cross_output.astype(jnp.bfloat16), "dp", scatter_dimension=0, tiled=True
        ).astype(jnp.float32),
        lax.psum_scatter(
            grad_hidden_in.astype(jnp.bfloat16), "dp", scatter_dimension=0, tiled=True
        ).astype(jnp.float32),
        lax.psum_scatter(
            grad_hidden_out.astype(jnp.bfloat16), "dp", scatter_dimension=0, tiled=True
        ).astype(jnp.float32),
    )
    factors = CLIP_LIMIT / jnp.maximum(jnp.stack([self_top, cross_top]), CLIP_LIMIT)
    root_scales = jnp.repeat(jnp.sqrt(factors), head_width, axis=1)
    clipped_self = self_query_key * root_scales[0][None, None, :]
    clipped_query = cross_query * root_scales[1][None, :]
    clipped_key = cross_key_value[:, 0] * root_scales[1][None, :]
    return (
        output,
        grad_inputs,
        grad_text,
        shard_norms,
        shard_self_pair,
        shard_self_value,
        shard_self_output,
        shard_cross_query,
        shard_cross_pair,
        shard_cross_output,
        shard_hidden_in,
        shard_hidden_out,
        factors,
        clipped_self,
        clipped_query,
        clipped_key,
    )


NT = (((1,), (1,)), ((), ()))
TN = (((0,), (0,)), ((), ()))
NN = (((1,), (0,)), ((), ()))
f32 = jnp.float32
bf16 = jnp.bfloat16
LANES = 128
MESH = pl.DeviceIdType.MESH
Z, Y, CORES = 4, 2, 2


def dotf(a, b, dims):
    return lax.dot_general(a, b, dims, preferred_element_type=f32)


def head_masks():
    lane = lax.broadcasted_iota(jnp.int32, (1, LANES), 1)
    return [lane < 64, lane >= 64]


def self_forward_kernel(rows_at_once, q_ref, k_ref, v_ref, o_ref, lse_ref, peak_ref):
    frames, size = q_ref.shape[0], rows_at_once
    masks = head_masks()
    key_row = lax.broadcasted_iota(jnp.int32, (size, size), 0)
    query_col = lax.broadcasted_iota(jnp.int32, (size, size), 1)
    allowed = key_row <= query_col
    zero = jnp.zeros((), bf16)
    peaks = [None, None]
    values = [jnp.where(mask, v_ref[...], zero) for mask in masks]
    for block in range(frames // size):
        first = block * size
        rows = slice(first, first + size)
        q = q_ref[rows, :] * jnp.asarray(0.125, bf16)
        mixed = None
        for h in range(2):
            qh = jnp.where(masks[h], q, zero)
            diagonal = jnp.where(allowed, dotf(k_ref[rows, :], qh, NT), MASKED)
            top = jnp.max(diagonal, axis=0, keepdims=True)
            if first:
                full = dotf(k_ref[0:first, :], qh, NT)
                top = jnp.maximum(top, jnp.max(full, axis=0, keepdims=True))
            diagonal = jnp.exp(diagonal - top)
            total = jnp.sum(diagonal, axis=0, keepdims=True)
            part = dotf(diagonal.astype(bf16), values[h][rows, :], TN)
            if first:
                full = jnp.exp(full - top)
                total = total + jnp.sum(full, axis=0, keepdims=True)
                part = part + dotf(full.astype(bf16), values[h][0:first, :], TN)
            lse_ref[h : h + 1, rows] = top + jnp.log(total)
            part = part * (1.0 / total).reshape(size, 1)
            mixed = part if mixed is None else mixed + part
            peaks[h] = top if peaks[h] is None else jnp.maximum(peaks[h], top)
        o_ref[rows, :] = mixed.astype(bf16)
    for h in range(2):
        peak_ref[h : h + 1, :] = jnp.broadcast_to(
            jnp.max(peaks[h], axis=1, keepdims=True), (1, LANES)
        )


def self_attend(qkv, width):
    frames, pairs = qkv.shape[1], width // LANES
    at = lambda offset: pl.BlockSpec((None, frames, LANES), lambda m, i: (m, 0, offset + i))
    stat = lambda n: pl.BlockSpec((None, None, 8, n), lambda m, i: (m, i, 0, 0))
    return pl.pallas_call(
        functools.partial(self_forward_kernel, 512),
        grid=(2, pairs),
        out_shape=(
            jax.ShapeDtypeStruct((2, frames, width), bf16),
            jax.ShapeDtypeStruct((2, pairs, 8, frames), f32),
            jax.ShapeDtypeStruct((2, pairs, 8, LANES), f32),
        ),
        in_specs=[at(0), at(pairs), at(2 * pairs)],
        out_specs=(at(0), stat(frames), stat(LANES)),
        compiler_params=pltpu.CompilerParams(vmem_limit_bytes=40 << 20),
        cost_estimate=pl.CostEstimate(
            flops=16 * frames * frames * width,
            bytes_accessed=16 * frames * width,
            transcendentals=0,
        ),
    )(qkv, qkv, qkv)


def self_backward_kernel(
    rows_at_once, q_ref, k_ref, v_ref, g_ref, lse_ref, dq_ref, dk_ref, dv_ref, dk_sum, dv_sum
):
    frames, size = q_ref.shape[0], rows_at_once
    masks = head_masks()
    key_row = lax.broadcasted_iota(jnp.int32, (size, size), 0)
    query_col = lax.broadcasted_iota(jnp.int32, (size, size), 1)
    allowed = key_row <= query_col
    zero = jnp.zeros((), bf16)
    keys = [jnp.where(mask, k_ref[...], zero) for mask in masks]
    blocks = frames // size
    for block in reversed(range(blocks)):
        first = block * size
        spans = [(slice(first, first + size), True)]
        if first:
            spans.append((slice(0, first), False))
        rows = spans[0][0]
        q = q_ref[rows, :] * jnp.asarray(0.125, bf16)
        g = g_ref[rows, :]
        dq = None
        dk, dv = [None] * len(spans), [None] * len(spans)
        for h in range(2):
            qh, gh = jnp.where(masks[h], q, zero), jnp.where(masks[h], g, zero)
            lse = lse_ref[h : h + 1, rows]
            weights, grads, center = [], [], None
            for span, masked in spans:
                scores = dotf(k_ref[span, :], qh, NT)
                if masked:
                    scores = jnp.where(allowed, scores, MASKED)
                weights.append(jnp.exp(scores - lse))
                grads.append(dotf(v_ref[span, :], gh, NT))
                part = jnp.sum(weights[-1] * grads[-1], axis=0, keepdims=True)
                center = part if center is None else center + part
            for i, (span, _) in enumerate(spans):
                ds = (weights[i] * (grads[i] - center)).astype(bf16)
                a = dotf(weights[i].astype(bf16), gh, NN)
                b = dotf(ds, qh, NN)
                c = dotf(ds, keys[h][span, :], TN)
                dv[i] = a if dv[i] is None else dv[i] + a
                dk[i] = b if dk[i] is None else dk[i] + b
                dq = c if dq is None else dq + c
        dq_ref[rows, :] = (dq * 0.125).astype(bf16)
        for i, (span, _) in enumerate(spans):
            if block == blocks - 1:
                dk_sum[span, :] = dk[i]
                dv_sum[span, :] = dv[i]
            else:
                dk_sum[span, :] += dk[i]
                dv_sum[span, :] += dv[i]
    dk_ref[...] = dk_sum[...].astype(bf16)
    dv_ref[...] = dv_sum[...].astype(bf16)


class Hop:
    def __init__(self, kind, group):
        self.kind, self.group = kind, group
        rows, width = group.rows // 2, group.width
        self.chunk = (rows, width)
        self.count = {"x1": 8, "y1": 8, "y2": 4, "x2": 4, "za": 3, "zb": 3}[kind]
        self.lead = {"x1": (Z, Y), "y1": (2, Z), "y2": (Z,), "x2": (Z,), "za": (3,), "zb": (3,)}[kind]
        self.names = {
            "x1": ["own", "there"],
            "y1": ["own", "there"],
            "y2": ["own", "there", "x1"],
            "x2": ["own", "there", "y1"],
            "za": ["own", "there", "x1", "y2"],
            "zb": ["own", "there", "y1", "x2"],
        }[kind]

    def shape(self):
        return jax.ShapeDtypeStruct(self.lead + self.chunk, bf16)

    def scratch(self):
        return [
            pltpu.VMEM((self.count, len(self.names)) + self.chunk, bf16),
            pltpu.VMEM((self.count,) + self.chunk, bf16),
            pltpu.SemaphoreType.DMA((self.count, len(self.names))),
            pltpu.SemaphoreType.DMA((self.count,)),
            pltpu.SemaphoreType.DMA((self.count,)),
        ]

    def bind(self, sources, target, scratch):
        self.sources, self.target = sources, target
        self.loads, self.sent, self.load_sem, self.send_sem, self.recv_sem = scratch

    def index(self, t):
        half = self.chunk[0]
        low, high = pl.ds(0, half), pl.ds(half, half)
        if self.kind == "x1":
            at = (1, t // 2, t % 2, low)
            return [at, at], (t // 2, t % 2)
        if self.kind == "y1":
            at = (t // 4, t % 4, 1, high)
            return [at, at], (t // 4, t % 4)
        if self.kind == "y2":
            at = (0, t, 1, low)
            return [at, at, (t, 1)], (t,)
        if self.kind == "x2":
            at = (1, t, 0, high)
            return [at, at, (1, t)], (t,)
        z = (lax.axis_index("dp") // (Y * CORES) + t + 1) % Z
        if self.kind == "za":
            at = (0, z, 0, low)
            return [at, at, (z, 0), (z,)], (t,)
        at = (0, z, 0, high)
        return [at, at, (0, z), (z,)], (t,)

    def partner(self, t):
        dp, mp = lax.axis_index("dp"), lax.axis_index("mp")
        if self.kind in ("x1", "x2"):
            return (dp, 1 - mp)
        if self.kind in ("y1", "y2"):
            return (dp + CORES - 2 * CORES * ((dp // CORES) % Y), mp)
        group = Y * CORES
        return (((dp // group + t + 1) % Z) * group + dp % group, mp)

    def partners(self):
        return [self.partner(t) for t in range(3 if self.kind in ("za", "zb") else 1)]

    def load(self, t):
        return [
            pltpu.make_async_copy(source.at[at], self.loads.at[t, i], self.load_sem.at[t, i])
            for i, (source, at) in enumerate(zip(self.sources, self.index(t)[0]))
        ]

    def send(self, t):
        return pltpu.make_async_remote_copy(
            src_ref=self.sent.at[t],
            dst_ref=self.target.at[self.index(t)[1]],
            send_sem=self.send_sem.at[t],
            recv_sem=self.recv_sem.at[t],
            device_id=self.partner(t),
            device_id_type=MESH,
        )

    def begin(self):
        for t in range(self.count):
            for copy in self.load(t):
                copy.start()

    def each(self, steps):
        return self.count if steps < 3 else -(-self.count // 2)

    def work(self, step, steps, j):
        t = step * self.each(steps) + j

        @pl.when(t < self.count)
        def _():
            for copy in self.load(t):
                copy.wait()
            total = self.loads[t, 0].astype(f32)
            for i in range(1, len(self.names)):
                total = total + self.loads[t, i].astype(f32)
            self.sent[t] = total.astype(bf16)
            self.send(t).start()

    def finish(self):
        for t in range(self.count):
            self.send(t).wait()


class Group:
    def __init__(self, own, there):
        self.arrays = {"own": own, "there": there}
        self.rows, self.width = own.shape[3], own.shape[4]

    def result(self, z):
        a = self.arrays
        half = self.rows // 2
        take = lambda array, at=0: lax.dynamic_index_in_dim(array, z, at, keepdims=False)
        total = take(a["own"][0, :, 0]).astype(f32) + take(a["there"][0, :, 0]).astype(f32)
        low = take(a["x1"][:, 0]).astype(f32) + take(a["y2"]).astype(f32)
        high = take(a["y1"][0]).astype(f32) + take(a["x2"]).astype(f32)
        for k in range(3):
            low = low + a["za"][k].astype(f32)
            high = high + a["zb"][k].astype(f32)
        return total + jnp.concatenate([low, high], axis=0)


def meet(partners):
    barrier = pltpu.get_barrier_semaphore()
    for partner in partners:
        pl.semaphore_signal(barrier, inc=1, device_id=partner, device_id_type=MESH)
    pl.semaphore_wait(barrier, len(partners))


def core_partner():
    dp = lax.axis_index("dp")
    return (dp + 1 - 2 * (dp % CORES), lax.axis_index("mp"))


def hosted(body, number, grid, args, in_specs, out_shape, out_specs, scratch, plan, flops, core=False):
    hops = [Hop(kind, group) for kind, group in plan]
    arrays, places = [], {}
    for hop in hops:
        for name in hop.names:
            key = (id(hop.group), name)
            if key not in places:
                places[key] = len(arrays)
                arrays.append(hop.group.arrays[name])
    steps = 1
    for n in grid:
        steps *= n
    kinds = set(hop.kind[0] for hop in hops)

    def kernel(*refs):
        counts = [len(args), len(arrays), len(out_shape), len(hops), len(scratch)]
        parts, at = [], 0
        for n in counts:
            parts.append(refs[at : at + n])
            at += n
        for k, hop in enumerate(hops):
            sources = [parts[1][places[(id(hop.group), name)]] for name in hop.names]
            hop.bind(sources, parts[3][k], refs[at : at + 5])
            at += 5
        step = 0
        for axis, n in enumerate(grid):
            step = step * n + pl.program_id(axis)

        @pl.when(step == 0)
        def _():
            partners = [core_partner()] if core else []
            for kind in sorted(kinds):
                partners += [hop for hop in hops if hop.kind[0] == kind][0].partners()
            if partners:
                meet(partners)
            for hop in hops:
                hop.begin()

        for j in range(max([hop.each(steps) for hop in hops], default=0)):
            for hop in hops:
                if j < hop.each(steps):
                    hop.work(step, steps, j)
        body(*parts[0], *parts[2], *parts[4])

        @pl.when(step == steps - 1)
        def _():
            for hop in hops:
                hop.finish()

    hbm = pl.BlockSpec(memory_space=pl.ANY)
    extra = [s for hop in hops for s in hop.scratch()]
    outs = pl.pallas_call(
        kernel,
        grid=grid,
        in_specs=list(in_specs) + [hbm] * len(arrays),
        out_specs=tuple(out_specs) + (hbm,) * len(hops),
        out_shape=tuple(out_shape) + tuple(hop.shape() for hop in hops),
        scratch_shapes=list(scratch) + extra,
        compiler_params=pltpu.CompilerParams(
            vmem_limit_bytes=56 << 20,
            **(dict(collective_id=number, has_side_effects=True) if hops or core else {}),
        ),
        cost_estimate=pl.CostEstimate(flops=flops, bytes_accessed=flops // 500, transcendentals=0),
    )(*args, *arrays)
    for hop, array in zip(hops, outs[len(out_shape) :]):
        hop.group.arrays[hop.kind] = array
    return outs[: len(out_shape)]


def self_attend_back(number, plan, qkv, grad, lse, width, begin, end):
    frames, pairs = qkv.shape[1], width // LANES
    at = lambda offset: pl.BlockSpec((None, frames, LANES), lambda m, i: (m, 0, offset + i))
    out = jax.ShapeDtypeStruct((2, frames, (end - begin) * LANES), bf16)
    return hosted(
        functools.partial(self_backward_kernel, 256),
        number,
        (2, end - begin),
        [qkv, qkv, qkv, grad, lse],
        [
            at(begin),
            at(pairs + begin),
            at(2 * pairs + begin),
            at(begin),
            pl.BlockSpec((None, None, 8, frames), lambda m, i: (m, begin + i, 0, 0)),
        ],
        [out] * 3,
        [at(0)] * 3,
        [pltpu.VMEM((frames, LANES), f32)] * 2,
        plan,
        16 * frames * frames * LANES * (end - begin),
    )


def half_spec(array, half):
    if array.ndim == 2:
        return pl.BlockSpec(array.shape, lambda *grid: (0, 0), pipeline_mode=pl.Buffered(1))
    return pl.BlockSpec(
        (None,) + array.shape[1:], lambda *grid: (half, 0, 0), pipeline_mode=pl.Buffered(1)
    )


def exchanged_grad(number, plan, xs, tiles, rows):
    depth = xs[0].shape[1]
    specs = [pl.BlockSpec(x.shape, lambda j, m: (0, 0), pipeline_mode=pl.Buffered(1)) for x in xs]
    args, halves = list(xs), []
    for _, arrays in tiles:
        halves.append([])
        for half in range(2):
            halves[-1].append(range(len(args), len(args) + len(arrays)))
            args += arrays
            specs += [half_spec(array, half) for array in arrays]
    tile = sum(array.shape[2] for array in tiles[0][1])
    count = len(tiles)
    steps = 2 * count
    longest = max(x.shape[0] for x in xs)
    shape = jax.ShapeDtypeStruct((2, Z, Y, rows, count * tile), bf16)
    hbm = pl.BlockSpec(memory_space=pl.ANY)

    def body(*refs):
        own_ref, there_ref = refs[len(args) : len(args) + 2]
        turned, own, other, own_sem, send_sem, recv_sem = refs[len(args) + 2 :]
        dp, mp = lax.axis_index("dp"), lax.axis_index("mp")
        core, across = dp % CORES, (dp // CORES) % Y
        j, m = pl.program_id(0), pl.program_id(1)
        step = 2 * j + m

        def place(step):
            column = (step // 2) * tile
            column = column if isinstance(column, int) else pl.multiple_of(column, LANES)
            every = slice(None)
            return ((step + mp) % 2, every, every, every, pl.ds(column, tile))

        def kept(step):
            slot = step % 2
            return pltpu.make_async_copy(own.at[slot], own_ref.at[place(step)], own_sem.at[slot])

        def sent(step):
            return pltpu.make_async_remote_copy(
                src_ref=other.at[step % 2],
                dst_ref=there_ref.at[place(step)],
                send_sem=send_sem.at[step],
                recv_sem=recv_sem.at[step],
                device_id=core_partner(),
                device_id_type=MESH,
            )

        @pl.when(step >= 2)
        def _():
            kept(step - 2).wait()
            sent(step - 2).wait_send()

        for k, (source, _) in enumerate(tiles):
            frames = xs[source].shape[0]

            if k == 0 or tiles[k - 1][0] != source:

                @pl.when((j == k) & (m == 0))
                def _(source=source, frames=frames):
                    turned[:, 0:frames] = refs[source][...].T

            for half in range(2):

                @pl.when((j == k) & (m == half))
                def _(k=k, half=half, frames=frames):
                    pieces = [refs[i][...] for i in halves[k][half]]
                    y = pieces[0] if len(pieces) == 1 else jnp.concatenate(pieces, axis=1)
                    for z in range(Z):
                        span = slice(z * Y * CORES * rows, (z + 1) * Y * CORES * rows)
                        part = dotf(turned[span, 0:frames], y, NN).astype(bf16)
                        for i in range(Y):
                            first = part[2 * i * rows : (2 * i + 1) * rows]
                            second = part[(2 * i + 1) * rows : (2 * i + 2) * rows]
                            own[m, z, (i + across) % 2] = jnp.where(core == 0, first, second)
                            other[m, z, (i + across) % 2] = jnp.where(core == 0, second, first)

        kept(step).start()
        sent(step).start()

        @pl.when(step == steps - 1)
        def _():
            for t in (steps - 2, steps - 1):
                kept(t).wait()
                sent(t).wait_send()
            for t in range(steps):
                sent(t).wait_recv()

    outs = hosted(
        body,
        number,
        (count, 2),
        args,
        specs,
        [shape, shape],
        [hbm, hbm],
        [
            pltpu.VMEM((depth, longest), bf16),
            pltpu.VMEM((2, Z, Y, rows, tile), bf16),
            pltpu.VMEM((2, Z, Y, rows, tile), bf16),
            pltpu.SemaphoreType.DMA((2,)),
            pltpu.SemaphoreType.DMA((steps,)),
            pltpu.SemaphoreType.DMA((steps,)),
        ],
        plan,
        4 * longest * depth * count * tile,
        core=True,
    )
    return Group(*outs)


def project_kernel(x_ref, w_ref, o_ref):
    step = x_ref.shape[0] // 4
    for i in range(4):
        rows = slice(i * step, (i + 1) * step)
        o_ref[rows, :] = dotf(x_ref[rows, :], w_ref[...], NN).astype(o_ref.dtype)


def project_both(x, whole, begin, width, tile=768):
    (frames, depth), first = x.shape, begin // tile
    return pl.pallas_call(
        project_kernel,
        grid=(2, width // tile),
        in_specs=[
            pl.BlockSpec((frames, depth), lambda m, j: (0, 0)),
            pl.BlockSpec((None, depth, tile), lambda m, j: (m, 0, first + j)),
        ],
        out_specs=pl.BlockSpec((None, frames, tile), lambda m, j: (m, 0, j)),
        out_shape=jax.ShapeDtypeStruct((2, frames, width), bf16),
        compiler_params=pltpu.CompilerParams(vmem_limit_bytes=40 << 20),
        cost_estimate=pl.CostEstimate(
            flops=4 * frames * depth * width,
            bytes_accessed=4 * (frames + depth) * width,
            transcendentals=0,
        ),
    )(x, whole)


def unproject_both(number, plan, pieces, whole, begin, width, base=None):
    frames, depth, tile = pieces[0][0].shape[-2], whole.shape[1], 256
    first, direct = begin // width, len(pieces) == 2
    bases = [] if base is None else [base]

    def body(*refs):
        n = len(pieces)
        w_refs, refs_left = refs[n : n + 2], refs[n + 2 :]
        o_ref = refs_left[len(bases)]

        if not direct:
            joint = refs_left[-1]

            @pl.when(pl.program_id(0) == 0)
            def _():
                for ref, (_, half, column) in zip(refs, pieces):
                    joint[half, :, column : column + ref.shape[1]] = ref[...]

        for i in range(4):
            rows = slice(i * frames // 4, (i + 1) * frames // 4)
            ys = [refs[m][rows, :] if direct else joint[m, rows, :] for m in range(2)]
            total = dotf(ys[0], w_refs[0][...], NT) + dotf(ys[1], w_refs[1][...], NT)
            o_ref[rows, :] = refs_left[0][rows, :] + total if bases else total

    weights = lambda m: pl.BlockSpec((None, tile, width), lambda j: (m, j, first))
    across = pl.BlockSpec((frames, tile), lambda j: (0, j))
    return hosted(
        body,
        number,
        (depth // tile,),
        [p[0] for p in pieces] + [whole, whole] + bases,
        [half_spec(array, half) for array, half, _ in pieces] + [weights(0), weights(1)] + [across] * len(bases),
        [jax.ShapeDtypeStruct((frames, depth), f32)],
        [across],
        [] if direct else [pltpu.VMEM((2, frames, width), bf16)],
        plan,
        4 * frames * depth * width,
    )[0]


def halves_of(array):
    return [(array, 0, 0), (array, 1, 0)]


def relay(number, plan, value):
    def body(value_ref, total_ref, sums, got, send_sem, recv_sem):
        dp, mp = lax.axis_index("dp"), lax.axis_index("mp")
        group = Y * CORES
        z, rest = dp // group, dp % group
        partners = [core_partner(), (dp, 1 - mp), (dp + CORES - 2 * CORES * ((dp // CORES) % Y), mp)]
        partners.append(((z + 1 - 2 * (z % 2)) * group + rest, mp))
        partners.append((((z + 2) % Z) * group + rest, mp))
        sums[0] = value_ref[...]
        for i, partner in enumerate(partners):
            copy = pltpu.make_async_remote_copy(
                src_ref=sums.at[i],
                dst_ref=got.at[i],
                send_sem=send_sem.at[i],
                recv_sem=recv_sem.at[i],
                device_id=partner,
                device_id_type=MESH,
            )
            copy.start()
            copy.wait()
            sums[i + 1] = sums[i] + got[i]
        total_ref[...] = sums[5]

    whole = pl.BlockSpec(value.shape, lambda i: (0, 0))
    return hosted(
        body,
        number,
        (1,),
        [value],
        [whole],
        [jax.ShapeDtypeStruct(value.shape, f32)],
        [whole],
        [
            pltpu.VMEM((6,) + value.shape, f32),
            pltpu.VMEM((5,) + value.shape, f32),
            pltpu.SemaphoreType.DMA((5,)),
            pltpu.SemaphoreType.DMA((5,)),
        ],
        plan,
        10**9,
        core=True,
    )[0]


def last_hop(number, plan):
    hosted(lambda: None, number, (1,), [], [], [], [], [], plan, 10**9)


def pair_rows(array, masks):
    zero = jnp.zeros((), bf16)
    return jnp.concatenate([jnp.where(mask, array, zero) for mask in masks], axis=0)


def cross_weights_of(q, keys, masks):
    scores = dotf(q * jnp.asarray(0.125, bf16), keys, NT)
    tops = [jnp.max(jnp.where(mask, scores, MASKED), axis=1, keepdims=True) for mask in masks]
    exponents = jnp.exp(scores - jnp.where(masks[0], tops[0], tops[1]))
    sums = [jnp.sum(jnp.where(mask, exponents, 0.0), axis=1, keepdims=True) for mask in masks]
    return exponents * jnp.where(masks[0], 1.0 / sums[0], 1.0 / sums[1]), tops


def cross_forward_kernel(q_ref, k_ref, v_ref, o_ref, peak_ref):
    masks = head_masks()
    weights, tops = cross_weights_of(q_ref[...], pair_rows(k_ref[...], masks), masks)
    o_ref[...] = dotf(weights.astype(bf16), pair_rows(v_ref[...], masks), NN).astype(bf16)
    for h in range(2):
        peak_ref[h : h + 1, :] = jnp.broadcast_to(
            jnp.max(tops[h], axis=0, keepdims=True), (1, LANES)
        )


def cross_specs(frames, text, pairs):
    at = lambda n, offset: pl.BlockSpec((None, n, LANES), lambda m, i: (m, 0, offset + i))
    return at(frames, 0), at(text, 0), at(text, pairs)


def cross_attend(q, kv, width):
    frames, text, pairs = q.shape[1], kv.shape[1], width // LANES
    long, keys, values = cross_specs(frames, text, pairs)
    return pl.pallas_call(
        cross_forward_kernel,
        grid=(2, pairs),
        out_shape=(
            jax.ShapeDtypeStruct((2, frames, width), bf16),
            jax.ShapeDtypeStruct((2, pairs, 8, LANES), f32),
        ),
        in_specs=[long, keys, values],
        out_specs=(long, pl.BlockSpec((None, None, 8, LANES), lambda m, i: (m, i, 0, 0))),
        compiler_params=pltpu.CompilerParams(vmem_limit_bytes=32 << 20),
        cost_estimate=pl.CostEstimate(
            flops=32 * frames * LANES * width, bytes_accessed=8 * frames * width, transcendentals=0
        ),
    )(q, kv, kv)


def cross_backward_kernel(q_ref, k_ref, v_ref, g_ref, dq_ref, dk_ref, dv_ref):
    masks = head_masks()
    text = k_ref.shape[0]
    keys, values = pair_rows(k_ref[...], masks), pair_rows(v_ref[...], masks)
    q, g = q_ref[...], g_ref[...]
    weights, _ = cross_weights_of(q, keys, masks)
    grads = dotf(g, values, NT)
    products = weights * grads
    centers = [jnp.sum(jnp.where(mask, products, 0.0), axis=1, keepdims=True) for mask in masks]
    ds = (weights * (grads - jnp.where(masks[0], centers[0], centers[1]))).astype(bf16)
    dq_ref[...] = (dotf(ds, keys, NN) * 0.125).astype(bf16)
    dk = dotf(ds, q, TN) * 0.125
    dv = dotf(weights.astype(bf16), g, TN)
    dk_ref[...] = jnp.where(masks[0], dk[:text], dk[text:]).astype(bf16)
    dv_ref[...] = jnp.where(masks[0], dv[:text], dv[text:]).astype(bf16)


def cross_attend_back(q, kv, grad, width):
    frames, text, pairs = q.shape[1], kv.shape[1], width // LANES
    long, keys, values = cross_specs(frames, text, pairs)
    return pl.pallas_call(
        cross_backward_kernel,
        grid=(2, pairs),
        out_shape=(
            jax.ShapeDtypeStruct((2, frames, width), bf16),
            jax.ShapeDtypeStruct((2, text, width), bf16),
            jax.ShapeDtypeStruct((2, text, width), bf16),
        ),
        in_specs=[long, keys, values, long],
        out_specs=(long, keys, keys),
        compiler_params=pltpu.CompilerParams(vmem_limit_bytes=32 << 20),
        cost_estimate=pl.CostEstimate(
            flops=64 * frames * LANES * width, bytes_accessed=12 * frames * width, transcendentals=0
        ),
    )(q, kv, kv, grad)


def weight_grad_whole_kernel(x_ref, y0_ref, y1_ref, *refs):
    half, tile = pl.program_id(0), pl.program_id(1)
    o_ref, turned = refs[-2:]

    @pl.when((half == 0) & (tile == 0))
    def _():
        turned[...] = x_ref[...].T

    for m, y_ref in enumerate((y0_ref, y1_ref)):

        @pl.when(half == m)
        def _(y_ref=y_ref):
            step = o_ref.shape[0] // 4
            for i in range(4):
                rows = slice(i * step, (i + 1) * step)
                o_ref[rows, :] = dotf(turned[rows, :], y_ref[...], NN).astype(bf16)


def weight_grad_whole(x, ys, tile, columns, begin, into=None):
    frames, depth = x.shape
    width = ys[0].shape[1]
    tiles, first = width // tile, begin // tile
    given = [] if into is None else [into]
    return pl.pallas_call(
        weight_grad_whole_kernel,
        grid=(2, tiles),
        in_specs=[
            pl.BlockSpec((frames, depth), lambda m, j: (0, 0)),
            pl.BlockSpec((frames, tile), lambda m, j: (0, jnp.where(m == 0, j, tiles - 1))),
            pl.BlockSpec((frames, tile), lambda m, j: (0, jnp.where(m == 0, 0, j))),
        ]
        + [pl.BlockSpec(memory_space=pl.ANY)] * len(given),
        out_specs=pl.BlockSpec((None, depth, tile), lambda m, j: (m, 0, first + j)),
        scratch_shapes=[pltpu.VMEM((depth, frames), bf16)],
        out_shape=jax.ShapeDtypeStruct((2, depth, columns), bf16),
        input_output_aliases={3: 0} if given else {},
        compiler_params=pltpu.CompilerParams(vmem_limit_bytes=40 << 20),
        cost_estimate=pl.CostEstimate(
            flops=4 * frames * depth * width,
            bytes_accessed=4 * (depth + frames) * width + 2 * frames * depth,
            transcendentals=0,
        ),
    )(x, *ys, *given)


def swap(values, axis_name, pairs):
    return lax.ppermute(values, axis_name, pairs)


MP_PAIRS = [(0, 1), (1, 0)]
CORE_PAIRS = [(i, i ^ 1) for i in range(Z * Y * CORES)]


def over_all(value, join):
    value = join(value, swap(value, "dp", CORE_PAIRS))
    value = join(value, swap(value, "mp", MP_PAIRS))
    for bit in (2, 4, 8):
        pairs = [(i, i ^ bit) for i in range(Z * Y * CORES)]
        value = join(value, swap(value, "dp", pairs))
    return value


def joined(arrays):
    return jnp.concatenate(arrays, axis=1)


def norm_rows_of(stream):
    center = stream - jnp.mean(stream, axis=-1, keepdims=True)
    inverse = lax.rsqrt(jnp.mean(center * center, axis=-1, keepdims=True) + EPSILON)
    return center * inverse, inverse


def norm_back(stream, gain, grad):
    rows, inverse = norm_rows_of(stream)
    scaled = grad * gain
    back = inverse * (
        scaled
        - jnp.mean(scaled, axis=-1, keepdims=True)
        - rows * jnp.mean(scaled * rows, axis=-1, keepdims=True)
    )
    return back, jnp.sum(grad * rows, axis=0), jnp.sum(grad, axis=0)


def clip_per_device(
    inputs,
    text_states,
    cotangent,
    norm_params,
    self_query_key,
    self_value,
    self_output,
    cross_query,
    cross_key_value,
    cross_output,
    hidden_in,
    hidden_out,
):
    dp, mp = lax.axis_index("dp"), lax.axis_index("mp")
    z = dp // (Y * CORES)
    rows, width = self_value.shape
    both = range(2)

    def gathered(pieces):
        shard = jnp.concatenate([rounded(p).reshape(rows, -1) for p in pieces], axis=1)
        whole = lax.all_gather(shard, ("mp", "dp"), axis=0, tiled=True)
        return whole.reshape(2, D, shard.shape[1])

    def to_clip(array, kind):
        own = lax.dynamic_index_in_dim(array, mp, 0, keepdims=False)
        sent = rounded(lax.dynamic_index_in_dim(array, 1 - mp, 0, keepdims=False))
        own, got = own.astype(kind), swap(sent, "mp", MP_PAIRS).astype(kind)
        return jnp.where(
            mp == 0, jnp.concatenate([own, got], axis=0), jnp.concatenate([got, own], axis=0)
        )

    def to_frames(array):
        count = array.shape[0] // 2
        own = lax.dynamic_slice_in_dim(array, mp * count, count, 0)
        sent = rounded(lax.dynamic_slice_in_dim(array, (1 - mp) * count, count, 0))
        got = swap(sent, "mp", MP_PAIRS).astype(f32)
        return jnp.where(mp == 0, jnp.stack([own, got]), jnp.stack([got, own]))

    norms_padded = jnp.pad(norm_params, ((0, 0), (0, LANES - norm_params.shape[1])))
    hidden = hidden_in.shape[1]
    self_all = gathered([self_query_key, self_value, self_output, norms_padded])
    cross_all = gathered([cross_query, cross_key_value, cross_output, hidden_in])
    out_all = gathered([hidden_out])
    norms = self_all[0, :, 4 * width : 4 * width + norm_params.shape[1]].astype(f32).T
    self_o = [self_all[m, :, 3 * width : 4 * width] for m in both]
    cross_q = [cross_all[m, :, :width] for m in both]
    cross_kv = [cross_all[m, :, width : 3 * width] for m in both]
    cross_o = [cross_all[m, :, 3 * width : 4 * width] for m in both]
    in_w = [cross_all[m, :, 4 * width :] for m in both]

    def times(array, matrix):
        return dotf(array, matrix, NN)

    def times_turned(arrays, matrices):
        return dotf(arrays[0], matrices[0], NT) + dotf(arrays[1], matrices[1], NT)

    stream = to_clip(inputs, f32)
    states = to_clip(text_states, bf16)
    normed_self = rounded(norm_rows_of(stream)[0] * norms[0] + norms[1])
    qkv = project_both(normed_self, self_all, 0, 3 * width)
    qkv, cotangent = lax.optimization_barrier((qkv, cotangent))
    upstream = to_clip(cotangent, f32)
    mixed_self, lse, self_peaks = self_attend(qkv, width)
    after_self = unproject_both(0, [], halves_of(mixed_self), self_all, 3 * width, width, stream)
    normed_cross = rounded(norm_rows_of(after_self)[0] * norms[2] + norms[3])
    queries = project_both(normed_cross, cross_all, 0, width)
    text_kv = jnp.stack([rounded(times(states, cross_kv[m])) for m in both])
    mixed_cross, cross_peaks = cross_attend(queries, text_kv, width)
    after_cross = unproject_both(0, [], halves_of(mixed_cross), cross_all, 3 * width, width, after_self)
    normed_hidden = rounded(norm_rows_of(after_cross)[0] * norms[4] + norms[5])
    upward = [times(normed_hidden, in_w[m]) for m in both]
    activated, pulls = zip(*[jax.vjp(gelu_exact, up) for up in upward])
    activated = [rounded(a) for a in activated]

    branch = rounded(upstream)
    hidden_grad = weight_grad_whole(branch, activated, 512, 2 * hidden, hidden)
    def peaks_of(peaks):
        return peaks[:, :, :2, 0].reshape(2, -1)

    tops = over_all(jnp.stack([peaks_of(self_peaks), peaks_of(cross_peaks)]), jnp.maximum)
    tops = lax.dynamic_index_in_dim(tops, mp, 1, keepdims=False)
    factors = CLIP_LIMIT / jnp.maximum(tops, CLIP_LIMIT)
    root_scales = jnp.repeat(jnp.sqrt(factors), D // HEADS, axis=1)
    clipped = (
        self_query_key * root_scales[0][None, None, :],
        cross_query * root_scales[1][None, :],
        cross_key_value[:, 0] * root_scales[1][None, :],
    )
    out_all, hidden_grad, clipped = lax.optimization_barrier((out_all, hidden_grad, clipped))
    grad_up = [rounded(pulls[m](times(branch, out_all[m]))[0]) for m in both]
    hidden_grad = weight_grad_whole(normed_hidden, grad_up, 512, 2 * hidden, 0, hidden_grad)
    grad_up, hidden_grad = lax.optimization_barrier((grad_up, hidden_grad))
    shard_hidden = lax.psum_scatter(
        hidden_grad.reshape(2 * D, 2 * hidden), ("mp", "dp"), scatter_dimension=0, tiled=True
    ).astype(f32)
    back, gain_three, bias_three = norm_back(
        after_cross, norms[4], times_turned(grad_up, in_w)
    )
    grad_stream = upstream + back

    branch_cross = rounded(grad_stream)
    grad_mixed = project_both(branch_cross, cross_all, 3 * width, width)
    dq, dk, dv = cross_attend_back(queries, text_kv, grad_mixed, width)
    grad_normed = unproject_both(0, [], halves_of(dq), cross_all, 0, width)
    back, gain_two, bias_two = norm_back(after_self, norms[2], grad_normed)
    dkv = [joined([dk[m], dv[m]]) for m in both]
    grad_text = to_frames(times_turned(dkv, cross_kv))
    grad_stream = grad_stream + back
    branch_self = rounded(grad_stream)
    group_pair = exchanged_grad(1, [], [normed_cross, states], [(0, [dq]), (1, [dk]), (1, [dv])], rows)
    group_out = exchanged_grad(
        2, [], [branch_cross, branch_self], [(0, [mixed_cross]), (1, [mixed_self])], rows
    )
    grad_mixed = project_both(branch_self, self_all, 3 * width, width)
    cut = width // 2 // LANES
    early = self_attend_back(
        3, [("x1", group_pair), ("y1", group_pair)], qkv, grad_mixed, lse, width, 0, cut
    )
    activated, early = lax.optimization_barrier((activated, early))
    output = unproject_both(
        4, [("x1", group_out), ("y1", group_out)], [(a, m, 0) for m, a in enumerate(activated)], out_all, 0, hidden, after_cross
    )
    output = to_frames(output)
    group_early = exchanged_grad(
        5, [("x2", group_pair), ("y2", group_pair)], [normed_self], [(0, list(early))], rows
    )
    late = self_attend_back(
        6,
        [("x2", group_out), ("y2", group_out), ("za", group_pair), ("zb", group_pair)],
        qkv,
        grad_mixed,
        lse,
        width,
        cut,
        2 * cut,
    )
    late, output, grad_text = lax.optimization_barrier((late, output, grad_text))
    group_late = exchanged_grad(
        7, [("x1", group_early), ("y1", group_early)], [normed_self], [(0, list(late))], rows
    )
    pieces = []
    for half in both:
        for part, arrays in enumerate((early, late)):
            pieces += [(a, half, i * width + part * cut * LANES) for i, a in enumerate(arrays)]
    grad_normed = unproject_both(
        8,
        [
            ("x1", group_late),
            ("y1", group_late),
            ("x2", group_early),
            ("y2", group_early),
            ("za", group_out),
            ("zb", group_out),
        ],
        pieces,
        self_all,
        0,
        3 * width,
    )
    back, gain_one, bias_one = norm_back(stream, norms[0], grad_normed)
    norm_grads = jnp.stack([gain_one, bias_one, gain_two, bias_two, gain_three, bias_three])
    grad_inputs, norm_grads = lax.optimization_barrier((grad_stream + back, norm_grads))
    grad_inputs = to_frames(grad_inputs)
    norm_grads = relay(
        9,
        [("x2", group_late), ("y2", group_late), ("za", group_early), ("zb", group_early)],
        jnp.pad(norm_grads, ((0, 2), (0, 0))),
    )[:6]
    last_hop(10, [("za", group_late), ("zb", group_late)])
    shard_pair, shard_outs = group_pair.result(z), group_out.result(z)
    halves = [group_early.result(z), group_late.result(z)]
    half = width // 2
    shard_self = [joined([h[:, i * half : (i + 1) * half] for h in halves]) for i in range(3)]

    shard_norms = lax.dynamic_slice_in_dim(norm_grads, dp * rows, rows, 1).T

    return (
        output,
        grad_inputs,
        grad_text,
        shard_norms,
        jnp.stack(shard_self[:2], axis=1),
        shard_self[2],
        shard_outs[:, width:],
        shard_pair[:, :width],
        shard_pair[:, width:].reshape(rows, 2, width),
        shard_outs[:, :width],
        shard_hidden[:, :hidden],
        shard_hidden[:, hidden:],
        factors,
        *clipped,
    )


def solution(mesh):
    in_specs = (
        P("dp", "mp", None),
        P("dp", "mp", None),
        P("dp", "mp", None),
        P("dp", None),
        P("dp", None, "mp"),
        P("dp", "mp"),
        P("dp", "mp"),
        P("dp", "mp"),
        P("dp", None, "mp"),
        P("dp", "mp"),
        P("dp", "mp"),
        P("dp", "mp"),
    )
    out_specs = (
        P("dp", "mp", None),
        P("dp", "mp", None),
        P("dp", "mp", None),
        P("dp", None),
        P("dp", None, "mp"),
        P("dp", "mp"),
        P("dp", "mp"),
        P("dp", "mp"),
        P("dp", None, "mp"),
        P("dp", "mp"),
        P("dp", "mp"),
        P("dp", "mp"),
        P(None, "mp"),
        P("dp", None, "mp"),
        P("dp", "mp"),
        P("dp", "mp"),
    )
    by_clip = mesh.shape["mp"] == 2 and mesh.shape["dp"] == 16
    return jax.shard_map(
        clip_per_device if by_clip else per_device, mesh=mesh, in_specs=in_specs, out_specs=out_specs, check_vma=False
    )
```

```python
import functools
import math

import jax
import jax.numpy as jnp
from jax import lax
from jax.experimental import pallas as pl
from jax.experimental.pallas import tpu as pltpu
from jax.sharding import PartitionSpec as P

D = 1536
HEADS = 24


EPSILON = 1e-05
CLIP_LIMIT = 7.0
MASKED = -1e30


def layer_norm(stream_rows, gain_row, bias_row):
    center = stream_rows - jnp.mean(stream_rows, axis=-1, keepdims=True)
    spread = jnp.mean(center * center, axis=-1, keepdims=True)
    return center * lax.rsqrt(spread + EPSILON) * gain_row + bias_row


def gelu_exact(values):
    return 0.5 * values * (1.0 + lax.erf(values * 2.0 ** (-0.5)))


def rounded(values):
    return values.astype(jnp.bfloat16)


def project(array, matrix):
    return jnp.einsum("cld,de->cle", array, matrix, preferred_element_type=jnp.float32)


def unproject(array, matrix):
    return jnp.einsum("cle,de->cld", array, matrix, preferred_element_type=jnp.float32)


def outer_sum(left, right):
    return jnp.einsum("cld,cle->de", left, right, preferred_element_type=jnp.float32)


def widen(values):
    return lax.all_gather(values, "mp", axis=1, tiled=True)


def settle(partial_sum):
    return lax.psum_scatter(
        partial_sum.astype(jnp.bfloat16), "mp", scatter_dimension=1, tiled=True
    ).astype(jnp.float32)


def widen_grad(values):
    return lax.all_gather(values, "mp", axis=1, tiled=True)


def settle_grad(partial_sum):
    return lax.psum_scatter(
        partial_sum.astype(jnp.bfloat16), "mp", scatter_dimension=1, tiled=True
    ).astype(jnp.float32)


def self_forward(queries, keys_all, values_all):
    frame_count, head_count, head_width = (queries.shape[1], queries.shape[2], queries.shape[3])
    block_rows = min(512, frame_count)
    block_count = frame_count // block_rows
    scaling = head_width ** (-0.5)
    row_ids = jnp.arange(block_rows)
    col_ids = jnp.arange(frame_count)

    def per_clip(triple):
        clip_queries, clip_keys, clip_values = triple

        def per_block(block_index):
            offset = block_index * block_rows
            block_queries = lax.dynamic_slice_in_dim(clip_queries, offset, block_rows, 0)
            scores = (
                jnp.einsum(
                    "qhe,khe->hqk", block_queries, clip_keys, preferred_element_type=jnp.float32
                )
                * scaling
            )
            allowed = col_ids[None, :] <= (offset + row_ids)[:, None]
            scores = jnp.where(allowed[None], scores, MASKED)
            highest = jnp.max(scores, axis=2, keepdims=True)
            exponents = jnp.exp(scores - highest)
            row_sums = jnp.sum(exponents, axis=2, keepdims=True)
            mixed = jnp.einsum(
                "hqk,khe->qhe",
                rounded(exponents / row_sums),
                clip_values,
                preferred_element_type=jnp.float32,
            )
            return (
                mixed,
                (highest + jnp.log(row_sums))[:, :, 0],
                jnp.max(highest[:, :, 0], axis=1),
            )

        mixed, log_sums, block_peaks = lax.map(per_block, jnp.arange(block_count))
        return (
            mixed.reshape(frame_count, head_count, head_width),
            log_sums,
            jnp.max(block_peaks, axis=0),
        )

    mixed, log_sums, clip_peaks = lax.map(per_clip, (queries, keys_all, values_all))
    return (mixed, log_sums, jnp.max(clip_peaks, axis=0))


def self_backward(queries, keys_all, values_all, log_sums, grad_mixed):
    frame_count, head_count, head_width = (queries.shape[1], queries.shape[2], queries.shape[3])
    block_rows = min(512, frame_count)
    block_count = frame_count // block_rows
    scaling = head_width ** (-0.5)
    row_ids = jnp.arange(block_rows)
    col_ids = jnp.arange(frame_count)

    def per_clip(bundle):
        clip_queries, clip_keys, clip_values, clip_logs, clip_grads = bundle

        def per_block(carried, block_index):
            grad_keys, grad_values = carried
            offset = block_index * block_rows
            block_queries = lax.dynamic_slice_in_dim(clip_queries, offset, block_rows, 0)
            block_grads = lax.dynamic_slice_in_dim(clip_grads, offset, block_rows, 0)
            scores = (
                jnp.einsum(
                    "qhe,khe->hqk", block_queries, clip_keys, preferred_element_type=jnp.float32
                )
                * scaling
            )
            allowed = col_ids[None, :] <= (offset + row_ids)[:, None]
            scores = jnp.where(allowed[None], scores, MASKED)
            weights = jnp.exp(scores - clip_logs[block_index][:, :, None])
            grad_values = grad_values + jnp.einsum(
                "hqk,qhe->khe", rounded(weights), block_grads, preferred_element_type=jnp.float32
            )
            grad_weights = jnp.einsum(
                "qhe,khe->hqk", block_grads, clip_values, preferred_element_type=jnp.float32
            )
            centered = grad_weights - jnp.sum(weights * grad_weights, axis=2, keepdims=True)
            grad_scores = rounded(weights * centered)
            grad_queries = (
                jnp.einsum(
                    "hqk,khe->qhe", grad_scores, clip_keys, preferred_element_type=jnp.float32
                )
                * scaling
            )
            grad_keys = (
                grad_keys
                + jnp.einsum(
                    "hqk,qhe->khe", grad_scores, block_queries, preferred_element_type=jnp.float32
                )
                * scaling
            )
            return ((grad_keys, grad_values), grad_queries)

        zero_keys = jnp.zeros(clip_keys.shape, jnp.float32)
        (grad_keys, grad_values), grad_queries = lax.scan(
            per_block, (zero_keys, zero_keys), jnp.arange(block_count)
        )
        return (grad_queries.reshape(frame_count, head_count, head_width), grad_keys, grad_values)

    return lax.map(per_clip, (queries, keys_all, values_all, log_sums, grad_mixed))


def cross_forward(queries, keys_all, values_all):
    scaling = queries.shape[3] ** (-0.5)
    scores = (
        jnp.einsum("clhe,cshe->chls", queries, keys_all, preferred_element_type=jnp.float32)
        * scaling
    )
    highest = jnp.max(scores, axis=3, keepdims=True)
    exponents = jnp.exp(scores - highest)
    weights = exponents / jnp.sum(exponents, axis=3, keepdims=True)
    mixed = jnp.einsum(
        "chls,cshe->clhe", rounded(weights), values_all, preferred_element_type=jnp.float32
    )
    return (mixed, weights, jnp.max(highest, axis=(0, 2, 3)))


def cross_backward(queries, keys_all, values_all, weights, grad_mixed):
    scaling = queries.shape[3] ** (-0.5)
    grad_values = jnp.einsum(
        "chls,clhe->cshe", rounded(weights), grad_mixed, preferred_element_type=jnp.float32
    )
    grad_weights = jnp.einsum(
        "clhe,cshe->chls", grad_mixed, values_all, preferred_element_type=jnp.float32
    )
    centered = grad_weights - jnp.sum(weights * grad_weights, axis=3, keepdims=True)
    grad_scores = rounded(weights * centered)
    grad_queries = (
        jnp.einsum("chls,cshe->clhe", grad_scores, keys_all, preferred_element_type=jnp.float32)
        * scaling
    )
    grad_keys = (
        jnp.einsum("chls,clhe->cshe", grad_scores, queries, preferred_element_type=jnp.float32)
        * scaling
    )
    return (grad_queries, grad_keys, grad_values)


def per_device(
    inputs,
    text_states,
    cotangent,
    norm_params,
    self_query_key,
    self_value,
    self_output,
    cross_query,
    cross_key_value,
    cross_output,
    hidden_in,
    hidden_out,
):
    (
        full_norms,
        full_query_key,
        full_value,
        full_output,
        full_cross_query,
        full_cross_pair,
        full_cross_output,
        full_hidden_in,
        full_hidden_out,
    ) = (
        lax.all_gather(rounded(norm_params), "dp", axis=0, tiled=True),
        lax.all_gather(rounded(self_query_key), "dp", axis=0, tiled=True),
        lax.all_gather(rounded(self_value), "dp", axis=0, tiled=True),
        lax.all_gather(rounded(self_output), "dp", axis=0, tiled=True),
        lax.all_gather(rounded(cross_query), "dp", axis=0, tiled=True),
        lax.all_gather(rounded(cross_key_value), "dp", axis=0, tiled=True),
        lax.all_gather(rounded(cross_output), "dp", axis=0, tiled=True),
        lax.all_gather(rounded(hidden_in), "dp", axis=0, tiled=True),
        lax.all_gather(rounded(hidden_out), "dp", axis=0, tiled=True),
    )
    norm_rows = full_norms.astype(jnp.float32)
    head_width = D // HEADS
    head_count = full_value.shape[1] // head_width

    def split_heads(array):
        return array.reshape(array.shape[0], array.shape[1], head_count, head_width)

    def merge_heads(array):
        return array.reshape(array.shape[0], array.shape[1], head_count * head_width)

    normed, pull_self = jax.vjp(layer_norm, inputs, norm_rows[:, 0], norm_rows[:, 1])
    normed_self = widen(rounded(normed))
    query_key_rows = jnp.einsum(
        "cld,dte->clte", normed_self, full_query_key, preferred_element_type=jnp.float32
    )
    queries = rounded(query_key_rows[:, :, 0])
    self_keys = rounded(query_key_rows[:, :, 1])
    values = rounded(project(normed_self, full_value))
    mixed, log_sums, self_peaks = self_forward(
        split_heads(queries), split_heads(self_keys), split_heads(values)
    )
    mixed_self = rounded(merge_heads(mixed))
    after_self = inputs + settle(unproject(mixed_self, full_output))
    normed, pull_cross = jax.vjp(layer_norm, after_self, norm_rows[:, 2], norm_rows[:, 3])
    normed_cross = widen(rounded(normed))
    cross_queries = rounded(project(normed_cross, full_cross_query))
    states = lax.all_gather(rounded(text_states), "mp", axis=1, tiled=True)
    key_value_rows = jnp.einsum(
        "csd,dte->cste", states, full_cross_pair, preferred_element_type=jnp.float32
    )
    cross_keys = rounded(key_value_rows[:, :, 0])
    cross_values = rounded(key_value_rows[:, :, 1])
    attended, cross_weights, cross_peaks = cross_forward(
        split_heads(cross_queries), split_heads(cross_keys), split_heads(cross_values)
    )
    mixed_cross = rounded(merge_heads(attended))
    after_cross = after_self + settle(unproject(mixed_cross, full_cross_output))
    normed, pull_hidden = jax.vjp(layer_norm, after_cross, norm_rows[:, 4], norm_rows[:, 5])
    normed_hidden = widen(rounded(normed))
    upward = project(normed_hidden, full_hidden_in)
    activated, pull_gelu = jax.vjp(gelu_exact, upward)
    activated = rounded(activated)
    output = after_cross + settle(unproject(activated, full_hidden_out))
    self_top, cross_top = lax.pmax((self_peaks, cross_peaks), "dp")
    grad_branch = widen_grad(rounded(cotangent))
    grad_hidden_out = outer_sum(grad_branch, activated)
    grad_upward = rounded(pull_gelu(project(grad_branch, full_hidden_out))[0])
    grad_hidden_in = outer_sum(normed_hidden, grad_upward)
    grad_normed = settle_grad(unproject(grad_upward, full_hidden_in))
    back_stream, grad_gain_three, grad_bias_three = pull_hidden(grad_normed)
    grad_stream = cotangent + back_stream
    grad_branch = widen_grad(rounded(grad_stream))
    grad_cross_output = outer_sum(grad_branch, mixed_cross)
    grad_attended = rounded(project(grad_branch, full_cross_output))
    grad_queries, grad_keys, grad_values = cross_backward(
        split_heads(cross_queries),
        split_heads(cross_keys),
        split_heads(cross_values),
        cross_weights,
        split_heads(grad_attended),
    )
    grad_queries = rounded(merge_heads(grad_queries))
    grad_pair = rounded(jnp.stack([merge_heads(grad_keys), merge_heads(grad_values)], axis=2))
    grad_cross_query = outer_sum(normed_cross, grad_queries)
    grad_cross_pair = jnp.einsum(
        "csd,cste->dte", states, grad_pair, preferred_element_type=jnp.float32
    )
    grad_text = lax.psum_scatter(
        jnp.einsum(
            "cste,dte->csd", grad_pair, full_cross_pair, preferred_element_type=jnp.float32
        ).astype(jnp.bfloat16),
        "mp",
        scatter_dimension=1,
        tiled=True,
    ).astype(jnp.float32)
    grad_normed = settle_grad(unproject(grad_queries, full_cross_query))
    back_stream, grad_gain_two, grad_bias_two = pull_cross(grad_normed)
    grad_stream = grad_stream + back_stream
    grad_branch = widen_grad(rounded(grad_stream))
    grad_self_output = outer_sum(grad_branch, mixed_self)
    grad_mixed = rounded(project(grad_branch, full_output))
    grad_queries, grad_keys, grad_values = self_backward(
        split_heads(queries),
        split_heads(self_keys),
        split_heads(values),
        log_sums,
        split_heads(grad_mixed),
    )
    grad_pair = rounded(jnp.stack([merge_heads(grad_queries), merge_heads(grad_keys)], axis=2))
    grad_values = rounded(merge_heads(grad_values))
    grad_self_pair = jnp.einsum(
        "cld,clte->dte", normed_self, grad_pair, preferred_element_type=jnp.float32
    )
    grad_self_value = outer_sum(normed_self, grad_values)
    grad_normed = settle_grad(
        jnp.einsum("clte,dte->cld", grad_pair, full_query_key, preferred_element_type=jnp.float32)
        + unproject(grad_values, full_value)
    )
    back_stream, grad_gain_one, grad_bias_one = pull_self(grad_normed)
    grad_inputs = grad_stream + back_stream
    grad_norm_rows = lax.psum(
        jnp.stack(
            [
                grad_gain_one,
                grad_bias_one,
                grad_gain_two,
                grad_bias_two,
                grad_gain_three,
                grad_bias_three,
            ],
            axis=1,
        ).astype(jnp.bfloat16),
        "mp",
    )
    (
        shard_norms,
        shard_self_pair,
        shard_self_value,
        shard_self_output,
        shard_cross_query,
        shard_cross_pair,
        shard_cross_output,
        shard_hidden_in,
        shard_hidden_out,
    ) = (
        lax.psum_scatter(grad_norm_rows, "dp", scatter_dimension=0, tiled=True).astype(jnp.float32),
        lax.psum_scatter(
            grad_self_pair.astype(jnp.bfloat16), "dp", scatter_dimension=0, tiled=True
        ).astype(jnp.float32),
        lax.psum_scatter(
            grad_self_value.astype(jnp.bfloat16), "dp", scatter_dimension=0, tiled=True
        ).astype(jnp.float32),
        lax.psum_scatter(
            grad_self_output.astype(jnp.bfloat16), "dp", scatter_dimension=0, tiled=True
        ).astype(jnp.float32),
        lax.psum_scatter(
            grad_cross_query.astype(jnp.bfloat16), "dp", scatter_dimension=0, tiled=True
        ).astype(jnp.float32),
        lax.psum_scatter(
            grad_cross_pair.astype(jnp.bfloat16), "dp", scatter_dimension=0, tiled=True
        ).astype(jnp.float32),
        lax.psum_scatter(
            grad_cross_output.astype(jnp.bfloat16), "dp", scatter_dimension=0, tiled=True
        ).astype(jnp.float32),
        lax.psum_scatter(
            grad_hidden_in.astype(jnp.bfloat16), "dp", scatter_dimension=0, tiled=True
        ).astype(jnp.float32),
        lax.psum_scatter(
            grad_hidden_out.astype(jnp.bfloat16), "dp", scatter_dimension=0, tiled=True
        ).astype(jnp.float32),
    )
    factors = CLIP_LIMIT / jnp.maximum(jnp.stack([self_top, cross_top]), CLIP_LIMIT)
    root_scales = jnp.repeat(jnp.sqrt(factors), head_width, axis=1)
    clipped_self = self_query_key * root_scales[0][None, None, :]
    clipped_query = cross_query * root_scales[1][None, :]
    clipped_key = cross_key_value[:, 0] * root_scales[1][None, :]
    return (
        output,
        grad_inputs,
        grad_text,
        shard_norms,
        shard_self_pair,
        shard_self_value,
        shard_self_output,
        shard_cross_query,
        shard_cross_pair,
        shard_cross_output,
        shard_hidden_in,
        shard_hidden_out,
        factors,
        clipped_self,
        clipped_query,
        clipped_key,
    )


NT = (((1,), (1,)), ((), ()))
TN = (((0,), (0,)), ((), ()))
NN = (((1,), (0,)), ((), ()))
f32 = jnp.float32
bf16 = jnp.bfloat16
LANES = 128
MESH = pl.DeviceIdType.MESH
Z, Y, CORES = 4, 2, 2


def dotf(a, b, dims):
    return lax.dot_general(a, b, dims, preferred_element_type=f32)


def head_masks():
    lane = lax.broadcasted_iota(jnp.int32, (1, LANES), 1)
    return [lane < 64, lane >= 64]


def self_forward_kernel(rows_at_once, q_ref, k_ref, v_ref, o_ref, lse_ref, peak_ref):
    frames, size = q_ref.shape[0], rows_at_once
    masks = head_masks()
    key_row = lax.broadcasted_iota(jnp.int32, (size, size), 0)
    query_col = lax.broadcasted_iota(jnp.int32, (size, size), 1)
    allowed = key_row <= query_col
    zero = jnp.zeros((), bf16)
    peaks = [None, None]
    values = [jnp.where(mask, v_ref[...], zero) for mask in masks]
    for block in range(frames // size):
        first = block * size
        rows = slice(first, first + size)
        q = q_ref[rows, :] * jnp.asarray(0.125, bf16)
        mixed = None
        for h in range(2):
            qh = jnp.where(masks[h], q, zero)
            diagonal = jnp.where(allowed, dotf(k_ref[rows, :], qh, NT), MASKED)
            top = jnp.max(diagonal, axis=0, keepdims=True)
            if first:
                full = dotf(k_ref[0:first, :], qh, NT)
                top = jnp.maximum(top, jnp.max(full, axis=0, keepdims=True))
            diagonal = jnp.exp(diagonal - top)
            total = jnp.sum(diagonal, axis=0, keepdims=True)
            part = dotf(diagonal.astype(bf16), values[h][rows, :], TN)
            if first:
                full = jnp.exp(full - top)
                total = total + jnp.sum(full, axis=0, keepdims=True)
                part = part + dotf(full.astype(bf16), values[h][0:first, :], TN)
            lse_ref[h : h + 1, rows] = top + jnp.log(total)
            part = part * (1.0 / total).reshape(size, 1)
            mixed = part if mixed is None else mixed + part
            peaks[h] = top if peaks[h] is None else jnp.maximum(peaks[h], top)
        o_ref[rows, :] = mixed.astype(bf16)
    for h in range(2):
        peak_ref[h : h + 1, :] = jnp.broadcast_to(
            jnp.max(peaks[h], axis=1, keepdims=True), (1, LANES)
        )


def self_attend(qkv, width):
    frames, pairs = qkv.shape[1], width // LANES
    at = lambda offset: pl.BlockSpec((None, frames, LANES), lambda m, i: (m, 0, offset + i))
    stat = lambda n: pl.BlockSpec((None, None, 8, n), lambda m, i: (m, i, 0, 0))
    return pl.pallas_call(
        functools.partial(self_forward_kernel, 512),
        grid=(2, pairs),
        out_shape=(
            jax.ShapeDtypeStruct((2, frames, width), bf16),
            jax.ShapeDtypeStruct((2, pairs, 8, frames), f32),
            jax.ShapeDtypeStruct((2, pairs, 8, LANES), f32),
        ),
        in_specs=[at(0), at(pairs), at(2 * pairs)],
        out_specs=(at(0), stat(frames), stat(LANES)),
        compiler_params=pltpu.CompilerParams(vmem_limit_bytes=40 << 20),
        cost_estimate=pl.CostEstimate(
            flops=16 * frames * frames * width,
            bytes_accessed=16 * frames * width,
            transcendentals=0,
        ),
    )(qkv, qkv, qkv)


def self_backward_kernel(
    rows_at_once, q_ref, k_ref, v_ref, g_ref, lse_ref, dq_ref, dk_ref, dv_ref, dk_sum, dv_sum
):
    frames, size = q_ref.shape[0], rows_at_once
    masks = head_masks()
    key_row = lax.broadcasted_iota(jnp.int32, (size, size), 0)
    query_col = lax.broadcasted_iota(jnp.int32, (size, size), 1)
    allowed = key_row <= query_col
    zero = jnp.zeros((), bf16)
    keys = [jnp.where(mask, k_ref[...], zero) for mask in masks]
    blocks = frames // size
    for block in reversed(range(blocks)):
        first = block * size
        spans = [(slice(first, first + size), True)]
        if first:
            spans.append((slice(0, first), False))
        rows = spans[0][0]
        q = q_ref[rows, :] * jnp.asarray(0.125, bf16)
        g = g_ref[rows, :]
        dq = None
        dk, dv = [None] * len(spans), [None] * len(spans)
        for h in range(2):
            qh, gh = jnp.where(masks[h], q, zero), jnp.where(masks[h], g, zero)
            lse = lse_ref[h : h + 1, rows]
            weights, grads, center = [], [], None
            for span, masked in spans:
                scores = dotf(k_ref[span, :], qh, NT)
                if masked:
                    scores = jnp.where(allowed, scores, MASKED)
                weights.append(jnp.exp(scores - lse))
                grads.append(dotf(v_ref[span, :], gh, NT))
                part = jnp.sum(weights[-1] * grads[-1], axis=0, keepdims=True)
                center = part if center is None else center + part
            for i, (span, _) in enumerate(spans):
                ds = (weights[i] * (grads[i] - center)).astype(bf16)
                a = dotf(weights[i].astype(bf16), gh, NN)
                b = dotf(ds, qh, NN)
                c = dotf(ds, keys[h][span, :], TN)
                dv[i] = a if dv[i] is None else dv[i] + a
                dk[i] = b if dk[i] is None else dk[i] + b
                dq = c if dq is None else dq + c
        dq_ref[rows, :] = (dq * 0.125).astype(bf16)
        for i, (span, _) in enumerate(spans):
            if block == blocks - 1:
                dk_sum[span, :] = dk[i]
                dv_sum[span, :] = dv[i]
            else:
                dk_sum[span, :] += dk[i]
                dv_sum[span, :] += dv[i]
    dk_ref[...] = dk_sum[...].astype(bf16)
    dv_ref[...] = dv_sum[...].astype(bf16)


class Hop:
    def __init__(self, kind, group):
        self.kind, self.group = kind, group
        rows, width = group.rows // 2, group.width
        self.chunk = (rows, width)
        self.count = {"x1": 8, "y1": 8, "y2": 4, "x2": 4, "za": 3, "zb": 3}[kind]
        self.lead = {"x1": (Z, Y), "y1": (2, Z), "y2": (Z,), "x2": (Z,), "za": (3,), "zb": (3,)}[kind]
        self.names = {
            "x1": ["own", "there"],
            "y1": ["own", "there"],
            "y2": ["own", "there", "x1"],
            "x2": ["own", "there", "y1"],
            "za": ["own", "there", "x1", "y2"],
            "zb": ["own", "there", "y1", "x2"],
        }[kind]

    def shape(self):
        return jax.ShapeDtypeStruct(self.lead + self.chunk, bf16)

    def scratch(self):
        return [
            pltpu.VMEM((self.count, len(self.names)) + self.chunk, bf16),
            pltpu.VMEM((self.count,) + self.chunk, bf16),
            pltpu.SemaphoreType.DMA((self.count, len(self.names))),
            pltpu.SemaphoreType.DMA((self.count,)),
            pltpu.SemaphoreType.DMA((self.count,)),
        ]

    def bind(self, sources, target, scratch):
        self.sources, self.target = sources, target
        self.loads, self.sent, self.load_sem, self.send_sem, self.recv_sem = scratch

    def index(self, t):
        half = self.chunk[0]
        low, high = pl.ds(0, half), pl.ds(half, half)
        if self.kind == "x1":
            at = (1, t // 2, t % 2, low)
            return [at, at], (t // 2, t % 2)
        if self.kind == "y1":
            at = (t // 4, t % 4, 1, high)
            return [at, at], (t // 4, t % 4)
        if self.kind == "y2":
            at = (0, t, 1, low)
            return [at, at, (t, 1)], (t,)
        if self.kind == "x2":
            at = (1, t, 0, high)
            return [at, at, (1, t)], (t,)
        z = (lax.axis_index("dp") // (Y * CORES) + t + 1) % Z
        if self.kind == "za":
            at = (0, z, 0, low)
            return [at, at, (z, 0), (z,)], (t,)
        at = (0, z, 0, high)
        return [at, at, (0, z), (z,)], (t,)

    def partner(self, t):
        dp, mp = lax.axis_index("dp"), lax.axis_index("mp")
        if self.kind in ("x1", "x2"):
            return (dp, 1 - mp)
        if self.kind in ("y1", "y2"):
            return (dp + CORES - 2 * CORES * ((dp // CORES) % Y), mp)
        group = Y * CORES
        return (((dp // group + t + 1) % Z) * group + dp % group, mp)

    def partners(self):
        return [self.partner(t) for t in range(3 if self.kind in ("za", "zb") else 1)]

    def load(self, t):
        return [
            pltpu.make_async_copy(source.at[at], self.loads.at[t, i], self.load_sem.at[t, i])
            for i, (source, at) in enumerate(zip(self.sources, self.index(t)[0]))
        ]

    def send(self, t):
        return pltpu.make_async_remote_copy(
            src_ref=self.sent.at[t],
            dst_ref=self.target.at[self.index(t)[1]],
            send_sem=self.send_sem.at[t],
            recv_sem=self.recv_sem.at[t],
            device_id=self.partner(t),
            device_id_type=MESH,
        )

    def begin(self):
        for t in range(self.count):
            for copy in self.load(t):
                copy.start()

    def each(self, steps):
        return self.count if steps < 3 else -(-self.count // 2)

    def work(self, step, steps, j):
        t = step * self.each(steps) + j

        @pl.when(t < self.count)
        def _():
            for copy in self.load(t):
                copy.wait()
            total = self.loads[t, 0].astype(f32)
            for i in range(1, len(self.names)):
                total = total + self.loads[t, i].astype(f32)
            self.sent[t] = total.astype(bf16)
            self.send(t).start()

    def finish(self):
        for t in range(self.count):
            self.send(t).wait()


class Swap:
    kind, names = "x0", ["sent"]

    def __init__(self, holder):
        self.group = holder

    def shape(self):
        sent = self.group.arrays["sent"]
        return jax.ShapeDtypeStruct(sent.shape, sent.dtype)

    def scratch(self):
        return [pltpu.SemaphoreType.DMA((1,)), pltpu.SemaphoreType.DMA((1,))]

    def bind(self, sources, target, scratch):
        self.source, self.target = sources[0], target
        self.send_sem, self.recv_sem = scratch

    def partners(self):
        return [(lax.axis_index("dp"), 1 - lax.axis_index("mp"))]

    def copy(self):
        return pltpu.make_async_remote_copy(
            src_ref=self.source,
            dst_ref=self.target,
            send_sem=self.send_sem.at[0],
            recv_sem=self.recv_sem.at[0],
            device_id=self.partners()[0],
            device_id_type=MESH,
        )

    def each(self, steps):
        return 1

    def begin(self):
        pass

    def work(self, step, steps, j):
        @pl.when(step == 0)
        def _():
            self.copy().start()

    def finish(self):
        self.copy().wait()


class Total:
    kind = "total"
    names = ["own", "there", "x1", "y2", "y1", "x2", "za", "zb"]

    def __init__(self, group):
        self.group = group
        low = group.rows // 2
        self.low, self.high = pl.ds(0, low), pl.ds(low, group.rows - low)

    def shape(self):
        return jax.ShapeDtypeStruct((self.group.rows, self.group.width), f32)

    def scratch(self):
        half, width = self.group.rows // 2, self.group.width
        return [
            pltpu.VMEM((2, 7, half, width), bf16),
            pltpu.VMEM((2 * half, width), f32),
            pltpu.SemaphoreType.DMA((2, 7)),
            pltpu.SemaphoreType.DMA(()),
        ]

    def bind(self, sources, target, scratch):
        self.sources, self.target = dict(zip(self.names, sources)), target
        self.terms, self.sum, self.load_sem, self.store_sem = scratch

    def partners(self):
        return []

    def loads(self):
        z = lax.axis_index("dp") // (Y * CORES)
        a = self.sources
        low = [a["own"].at[0, z, 0, self.low], a["there"].at[0, z, 0, self.low], a["x1"].at[z, 0]]
        low += [a["y2"].at[z]] + [a["za"].at[k] for k in range(3)]
        high = [a["own"].at[0, z, 0, self.high], a["there"].at[0, z, 0, self.high]]
        high += [a["y1"].at[0, z], a["x2"].at[z]] + [a["zb"].at[k] for k in range(3)]
        return [
            pltpu.make_async_copy(source, self.terms.at[p, i], self.load_sem.at[p, i])
            for p, part in enumerate((low, high))
            for i, source in enumerate(part)
        ]

    def each(self, steps):
        return 0

    def begin(self):
        for copy in self.loads():
            copy.start()

    def finish(self):
        for copy in self.loads():
            copy.wait()
        half = self.group.rows // 2
        for p in range(2):
            total = self.terms[p, 0].astype(f32)
            for i in range(1, 7):
                total = total + self.terms[p, i].astype(f32)
            self.sum[p * half : (p + 1) * half, :] = total
        copy = pltpu.make_async_copy(self.sum, self.target, self.store_sem)
        copy.start()
        copy.wait()


class Holder:
    def __init__(self, sent):
        self.arrays = {"sent": sent}

    def got(self):
        return self.arrays["x0"]


class Group:
    def __init__(self, own, there):
        self.arrays = {"own": own, "there": there}
        self.rows, self.width = own.shape[3], own.shape[4]

    def result(self, z):
        a = self.arrays
        half = self.rows // 2
        take = lambda array, at=0: lax.dynamic_index_in_dim(array, z, at, keepdims=False)
        total = take(a["own"][0, :, 0]).astype(f32) + take(a["there"][0, :, 0]).astype(f32)
        low = take(a["x1"][:, 0]).astype(f32) + take(a["y2"]).astype(f32)
        high = take(a["y1"][0]).astype(f32) + take(a["x2"]).astype(f32)
        for k in range(3):
            low = low + a["za"][k].astype(f32)
            high = high + a["zb"][k].astype(f32)
        return total + jnp.concatenate([low, high], axis=0)


def meet(partners):
    barrier = pltpu.get_barrier_semaphore()
    for partner in partners:
        pl.semaphore_signal(barrier, inc=1, device_id=partner, device_id_type=MESH)
    pl.semaphore_wait(barrier, len(partners))


def core_partner():
    dp = lax.axis_index("dp")
    return (dp + 1 - 2 * (dp % CORES), lax.axis_index("mp"))


def hosted(body, number, grid, args, in_specs, out_shape, out_specs, scratch, plan, flops, core=False):
    special = {"x0": Swap, "total": Total}
    hops = [special[k](group) if k in special else Hop(k, group) for k, group in plan]
    arrays, places = [], {}
    for hop in hops:
        for name in hop.names:
            key = (id(hop.group), name)
            if key not in places:
                places[key] = len(arrays)
                arrays.append(hop.group.arrays[name])
    steps = 1
    for n in grid:
        steps *= n
    kinds = set(hop.kind[0] for hop in hops if hop.kind != "total")

    def kernel(*refs):
        counts = [len(args), len(arrays), len(out_shape), len(hops), len(scratch)]
        parts, at = [], 0
        for n in counts:
            parts.append(refs[at : at + n])
            at += n
        for k, hop in enumerate(hops):
            sources = [parts[1][places[(id(hop.group), name)]] for name in hop.names]
            taken = len(hop.scratch())
            hop.bind(sources, parts[3][k], refs[at : at + taken])
            at += taken
        step = 0
        for axis, n in enumerate(grid):
            step = step * n + pl.program_id(axis)

        @pl.when(step == 0)
        def _():
            partners = [core_partner()] if core else []
            for kind in sorted(kinds):
                partners += [hop for hop in hops if hop.kind[0] == kind][0].partners()
            if partners:
                meet(partners)
            for hop in hops:
                hop.begin()

        for j in range(max([hop.each(steps) for hop in hops], default=0)):
            for hop in hops:
                if j < hop.each(steps):
                    hop.work(step, steps, j)
        body(*parts[0], *parts[2], *parts[4])

        @pl.when(step == steps - 1)
        def _():
            for hop in sorted(hops, key=lambda hop: hop.kind != "total"):
                hop.finish()

    hbm = pl.BlockSpec(memory_space=pl.ANY)
    extra = [s for hop in hops for s in hop.scratch()]
    outs = pl.pallas_call(
        kernel,
        grid=grid,
        in_specs=list(in_specs) + [hbm] * len(arrays),
        out_specs=tuple(out_specs) + (hbm,) * len(hops),
        out_shape=tuple(out_shape) + tuple(hop.shape() for hop in hops),
        scratch_shapes=list(scratch) + extra,
        compiler_params=pltpu.CompilerParams(
            vmem_limit_bytes=56 << 20,
            **(dict(collective_id=number, has_side_effects=True) if hops or core else {}),
        ),
        cost_estimate=pl.CostEstimate(flops=flops, bytes_accessed=flops // 500, transcendentals=0),
    )(*args, *arrays)
    for hop, array in zip(hops, outs[len(out_shape) :]):
        hop.group.arrays[hop.kind] = array
    return outs[: len(out_shape)]


def self_attend_back(number, plan, qkv, grad, lse, width, begin, end):
    frames, pairs = qkv.shape[1], width // LANES
    at = lambda offset: pl.BlockSpec((None, frames, LANES), lambda m, i: (m, 0, offset + i))
    out = jax.ShapeDtypeStruct((2, frames, (end - begin) * LANES), bf16)
    return hosted(
        functools.partial(self_backward_kernel, 256),
        number,
        (2, end - begin),
        [qkv, qkv, qkv, grad, lse],
        [
            at(begin),
            at(pairs + begin),
            at(2 * pairs + begin),
            at(begin),
            pl.BlockSpec((None, None, 8, frames), lambda m, i: (m, begin + i, 0, 0)),
        ],
        [out] * 3,
        [at(0)] * 3,
        [pltpu.VMEM((frames, LANES), f32)] * 2,
        plan,
        16 * frames * frames * LANES * (end - begin),
    )


def half_spec(array, half):
    if array.ndim == 2:
        return pl.BlockSpec(array.shape, lambda *grid: (0, 0), pipeline_mode=pl.Buffered(1))
    return pl.BlockSpec(
        (None,) + array.shape[1:], lambda *grid: (half, 0, 0), pipeline_mode=pl.Buffered(1)
    )


def exchanged_grad(number, plan, xs, tiles, rows):
    depth = xs[0].shape[1]
    specs = [pl.BlockSpec(x.shape, lambda j, m: (0, 0), pipeline_mode=pl.Buffered(1)) for x in xs]
    args, halves = list(xs), []
    for _, arrays in tiles:
        halves.append([])
        for half in range(2):
            halves[-1].append(range(len(args), len(args) + len(arrays)))
            args += arrays
            specs += [half_spec(array, half) for array in arrays]
    tile = sum(array.shape[2] for array in tiles[0][1])
    count = len(tiles)
    steps = 2 * count
    longest = max(x.shape[0] for x in xs)
    shape = jax.ShapeDtypeStruct((2, Z, Y, rows, count * tile), bf16)
    hbm = pl.BlockSpec(memory_space=pl.ANY)

    def body(*refs):
        own_ref, there_ref = refs[len(args) : len(args) + 2]
        turned, own, other, own_sem, send_sem, recv_sem = refs[len(args) + 2 :]
        dp, mp = lax.axis_index("dp"), lax.axis_index("mp")
        core, across = dp % CORES, (dp // CORES) % Y
        j, m = pl.program_id(0), pl.program_id(1)
        step = 2 * j + m

        def place(step):
            column = (step // 2) * tile
            column = column if isinstance(column, int) else pl.multiple_of(column, LANES)
            every = slice(None)
            return ((step + mp) % 2, every, every, every, pl.ds(column, tile))

        def kept(step):
            slot = step % 2
            return pltpu.make_async_copy(own.at[slot], own_ref.at[place(step)], own_sem.at[slot])

        def sent(step):
            return pltpu.make_async_remote_copy(
                src_ref=other.at[step % 2],
                dst_ref=there_ref.at[place(step)],
                send_sem=send_sem.at[step],
                recv_sem=recv_sem.at[step],
                device_id=core_partner(),
                device_id_type=MESH,
            )

        @pl.when(step >= 2)
        def _():
            kept(step - 2).wait()
            sent(step - 2).wait_send()

        for k, (source, _) in enumerate(tiles):
            frames = xs[source].shape[0]

            if k == 0 or tiles[k - 1][0] != source:

                @pl.when((j == k) & (m == 0))
                def _(source=source, frames=frames):
                    turned[:, 0:frames] = refs[source][...].T

            for half in range(2):

                @pl.when((j == k) & (m == half))
                def _(k=k, half=half, frames=frames):
                    pieces = [refs[i][...] for i in halves[k][half]]
                    y = pieces[0] if len(pieces) == 1 else jnp.concatenate(pieces, axis=1)
                    for z in range(Z):
                        span = slice(z * Y * CORES * rows, (z + 1) * Y * CORES * rows)
                        part = dotf(turned[span, 0:frames], y, NN).astype(bf16)
                        for i in range(Y):
                            first = part[2 * i * rows : (2 * i + 1) * rows]
                            second = part[(2 * i + 1) * rows : (2 * i + 2) * rows]
                            own[m, z, (i + across) % 2] = jnp.where(core == 0, first, second)
                            other[m, z, (i + across) % 2] = jnp.where(core == 0, second, first)

        kept(step).start()
        sent(step).start()

        @pl.when(step == steps - 1)
        def _():
            for t in (steps - 2, steps - 1):
                kept(t).wait()
                sent(t).wait_send()
            for t in range(steps):
                sent(t).wait_recv()

    outs = hosted(
        body,
        number,
        (count, 2),
        args,
        specs,
        [shape, shape],
        [hbm, hbm],
        [
            pltpu.VMEM((depth, longest), bf16),
            pltpu.VMEM((2, Z, Y, rows, tile), bf16),
            pltpu.VMEM((2, Z, Y, rows, tile), bf16),
            pltpu.SemaphoreType.DMA((2,)),
            pltpu.SemaphoreType.DMA((steps,)),
            pltpu.SemaphoreType.DMA((steps,)),
        ],
        plan,
        4 * longest * depth * count * tile,
        core=True,
    )
    return Group(*outs)


def gather_kernel(parts, swaps, *refs):
    shard_ref, sent_refs = refs[0], refs[1 : 1 + swaps]
    whole_ref, got_refs = refs[1 + swaps], refs[2 + swaps : 2 + 2 * swaps]
    own_sem, swap_send, swap_recv, send_sem, recv_sem = refs[2 + 2 * swaps :]
    dp, x = lax.axis_index("dp"), lax.axis_index("mp")
    group = Y * CORES
    z, rest = dp // group, dp % group
    across = rest + CORES - 2 * CORES * (rest // CORES)
    rows, columns = shard_ref.shape
    x_peer, y_peer, core_peer = (dp, 1 - x), (z * group + across, x), core_partner()
    z_peers = [(((z + k) % Z) * group + rest, x) for k in range(1, Z)]
    cut = 5 * rows // 6
    low, high, every = pl.ds(0, cut), pl.ds(cut, rows - cut), slice(None)
    meet([x_peer, y_peer, core_peer] + z_peers)
    started = []

    def send(part, slot, source, at, peer):
        copy = pltpu.make_async_remote_copy(
            src_ref=source,
            dst_ref=whole_ref.at[at],
            send_sem=send_sem.at[part, slot],
            recv_sem=recv_sem.at[part, slot],
            device_id=peer,
            device_id_type=MESH,
        )
        copy.start()
        started.append(copy)
        return copy

    def pass_on(part, slot, at, peer):
        return send(part, slot, whole_ref.at[at], at, peer)

    def columns_of(part):
        begin, end = parts[part]
        return pl.ds(begin, end - begin)

    swapped = []
    for i in range(swaps):
        copy = pltpu.make_async_remote_copy(
            src_ref=sent_refs[i],
            dst_ref=got_refs[i],
            send_sem=swap_send.at[i],
            recv_sem=swap_recv.at[i],
            device_id=x_peer,
            device_id_type=MESH,
        )
        copy.start()
        swapped.append(copy)
    own = pltpu.make_async_copy(shard_ref, whole_ref.at[x, z, rest], own_sem)
    own.start()
    along, over, turned, late = {}, {}, {}, []
    for part in range(len(parts)):
        cut = columns_of(part)
        at = (x, z, rest, every, cut)
        along[part] = [
            send(part, k, shard_ref.at[every, cut], at, peer) for k, peer in enumerate(z_peers)
        ]
        late.append(send(part, 3, shard_ref.at[every, cut], at, core_peer))
    own.wait()

    def first(part):
        cut = columns_of(part)
        for copy in along[part]:
            copy.wait_recv()
        over[part] = [
            pass_on(part, 4, (x, every, rest, low, cut), x_peer),
            pass_on(part, 5, (x, every, rest, high, cut), y_peer),
        ]
        for k in range(1, Z):
            late.append(pass_on(part, 5 + k, (x, (z + k) % Z, rest, every, cut), core_peer))

    def second(part):
        cut = columns_of(part)
        for copy in over[part]:
            copy.wait_recv()
        turned[part] = [
            pass_on(part, 9, (0, every, rest, low, cut), y_peer),
            pass_on(part, 10, (x, every, rest, high, cut), x_peer),
            pass_on(part, 11, (1, every, rest, low, cut), y_peer),
            pass_on(part, 12, (x, every, across, high, cut), x_peer),
        ]
        late.append(pass_on(part, 13, (1 - x, every, rest, low, cut), core_peer))
        late.append(pass_on(part, 14, (x, every, across, high, cut), core_peer))

    def third(part):
        cut = columns_of(part)
        for copy in turned[part]:
            copy.wait_recv()
        late.append(pass_on(part, 15, (0, every, across, low, cut), core_peer))
        late.append(pass_on(part, 16, (1, every, across, low, cut), core_peer))
        late.append(pass_on(part, 17, (1 - x, every, rest, high, cut), core_peer))
        late.append(pass_on(part, 18, (1 - x, every, across, high, cut), core_peer))

    first(0)
    for part in range(len(parts)):
        second(part)
        if part + 1 < len(parts):
            first(part + 1)
        if part:
            third(part - 1)
    third(len(parts) - 1)
    for copy in late:
        copy.wait_recv()
    for copy in started:
        copy.wait_send()
    for copy in swapped:
        copy.wait()


def gather_now(number, shard, swaps):
    rows, columns = shard.shape
    tiles = columns // LANES
    cuts = [0, tiles // 3 * LANES, 2 * tiles // 3 * LANES, columns]
    parts = list(zip(cuts[:-1], cuts[1:]))
    hbm = pl.BlockSpec(memory_space=pl.ANY)
    outs = pl.pallas_call(
        functools.partial(gather_kernel, parts, len(swaps)),
        in_specs=[hbm] * (1 + len(swaps)),
        out_specs=(hbm,) * (1 + len(swaps)),
        out_shape=(jax.ShapeDtypeStruct((2, Z, Y * CORES, rows, columns), shard.dtype),)
        + tuple(jax.ShapeDtypeStruct(a.shape, a.dtype) for a in swaps),
        scratch_shapes=[
            pltpu.SemaphoreType.DMA(()),
            pltpu.SemaphoreType.DMA((len(swaps),)),
            pltpu.SemaphoreType.DMA((len(swaps),)),
            pltpu.SemaphoreType.DMA((len(parts), 19)),
            pltpu.SemaphoreType.DMA((len(parts), 19)),
        ],
        compiler_params=pltpu.CompilerParams(collective_id=number, has_side_effects=True),
        cost_estimate=pl.CostEstimate(flops=10**9, bytes_accessed=10**8, transcendentals=0),
    )(shard, *swaps)
    return outs[0], outs[1:]


def project_kernel(x_ref, w_ref, o_ref):
    step = x_ref.shape[0] // 4
    for i in range(4):
        rows = slice(i * step, (i + 1) * step)
        o_ref[rows, :] = dotf(x_ref[rows, :], w_ref[...], NN).astype(o_ref.dtype)


def project_both(x, whole, begin, width, tile=768):
    (frames, depth), first = x.shape, begin // tile
    return pl.pallas_call(
        project_kernel,
        grid=(2, width // tile),
        in_specs=[
            pl.BlockSpec((frames, depth), lambda m, j: (0, 0)),
            pl.BlockSpec((None, depth, tile), lambda m, j: (m, 0, first + j)),
        ],
        out_specs=pl.BlockSpec((None, frames, tile), lambda m, j: (m, 0, j)),
        out_shape=jax.ShapeDtypeStruct((2, frames, width), bf16),
        compiler_params=pltpu.CompilerParams(vmem_limit_bytes=40 << 20),
        cost_estimate=pl.CostEstimate(
            flops=4 * frames * depth * width,
            bytes_accessed=4 * (frames + depth) * width,
            transcendentals=0,
        ),
    )(x, whole)


def unproject_both(number, plan, pieces, whole, begin, width, base=None):
    frames, depth, tile = pieces[0][0].shape[-2], whole.shape[1], 256
    first, direct = begin // width, len(pieces) == 2
    bases = [] if base is None else [base]

    def body(*refs):
        n = len(pieces)
        w_refs, refs_left = refs[n : n + 2], refs[n + 2 :]
        o_ref = refs_left[len(bases)]

        if not direct:
            joint = refs_left[-1]

            @pl.when(pl.program_id(0) == 0)
            def _():
                for ref, (_, half, column) in zip(refs, pieces):
                    joint[half, :, column : column + ref.shape[1]] = ref[...]

        for i in range(4):
            rows = slice(i * frames // 4, (i + 1) * frames // 4)
            ys = [refs[m][rows, :] if direct else joint[m, rows, :] for m in range(2)]
            total = dotf(ys[0], w_refs[0][...], NT) + dotf(ys[1], w_refs[1][...], NT)
            o_ref[rows, :] = refs_left[0][rows, :] + total if bases else total

    weights = lambda m: pl.BlockSpec((None, tile, width), lambda j: (m, j, first))
    across = pl.BlockSpec((frames, tile), lambda j: (0, j))
    return hosted(
        body,
        number,
        (depth // tile,),
        [p[0] for p in pieces] + [whole, whole] + bases,
        [half_spec(array, half) for array, half, _ in pieces] + [weights(0), weights(1)] + [across] * len(bases),
        [jax.ShapeDtypeStruct((frames, depth), f32)],
        [across],
        [] if direct else [pltpu.VMEM((2, frames, width), bf16)],
        plan,
        4 * frames * depth * width,
    )[0]


def halves_of(array):
    return [(array, 0, 0), (array, 1, 0)]


def relay(number, plan, value):
    def body(value_ref, total_ref, sums, got, send_sem, recv_sem):
        dp, mp = lax.axis_index("dp"), lax.axis_index("mp")
        group = Y * CORES
        z, rest = dp // group, dp % group
        partners = [core_partner(), (dp, 1 - mp), (dp + CORES - 2 * CORES * ((dp // CORES) % Y), mp)]
        partners.append(((z + 1 - 2 * (z % 2)) * group + rest, mp))
        partners.append((((z + 2) % Z) * group + rest, mp))
        sums[0] = value_ref[...]
        for i, partner in enumerate(partners):
            copy = pltpu.make_async_remote_copy(
                src_ref=sums.at[i],
                dst_ref=got.at[i],
                send_sem=send_sem.at[i],
                recv_sem=recv_sem.at[i],
                device_id=partner,
                device_id_type=MESH,
            )
            copy.start()
            copy.wait()
            sums[i + 1] = sums[i] + got[i]
        total_ref[...] = sums[5]

    whole = pl.BlockSpec(value.shape, lambda i: (0, 0))
    return hosted(
        body,
        number,
        (1,),
        [value],
        [whole],
        [jax.ShapeDtypeStruct(value.shape, f32)],
        [whole],
        [
            pltpu.VMEM((6,) + value.shape, f32),
            pltpu.VMEM((5,) + value.shape, f32),
            pltpu.SemaphoreType.DMA((5,)),
            pltpu.SemaphoreType.DMA((5,)),
        ],
        plan,
        10**9,
        core=True,
    )[0]


def last_hop(number, plan):
    hosted(lambda: None, number, (1,), [], [], [], [], [], plan, 10**9)


def pair_rows(array, masks):
    zero = jnp.zeros((), bf16)
    return jnp.concatenate([jnp.where(mask, array, zero) for mask in masks], axis=0)


def cross_weights_of(q, keys, masks):
    scores = dotf(q * jnp.asarray(0.125, bf16), keys, NT)
    tops = [jnp.max(jnp.where(mask, scores, MASKED), axis=1, keepdims=True) for mask in masks]
    exponents = jnp.exp(scores - jnp.where(masks[0], tops[0], tops[1]))
    sums = [jnp.sum(jnp.where(mask, exponents, 0.0), axis=1, keepdims=True) for mask in masks]
    return exponents * jnp.where(masks[0], 1.0 / sums[0], 1.0 / sums[1]), tops


def cross_forward_kernel(q_ref, k_ref, v_ref, o_ref, peak_ref):
    masks = head_masks()
    weights, tops = cross_weights_of(q_ref[...], pair_rows(k_ref[...], masks), masks)
    o_ref[...] = dotf(weights.astype(bf16), pair_rows(v_ref[...], masks), NN).astype(bf16)
    for h in range(2):
        peak_ref[h : h + 1, :] = jnp.broadcast_to(
            jnp.max(tops[h], axis=0, keepdims=True), (1, LANES)
        )


def cross_specs(frames, text, pairs):
    at = lambda n, offset: pl.BlockSpec((None, n, LANES), lambda m, i: (m, 0, offset + i))
    return at(frames, 0), at(text, 0), at(text, pairs)


def cross_attend(q, kv, width):
    frames, text, pairs = q.shape[1], kv.shape[1], width // LANES
    long, keys, values = cross_specs(frames, text, pairs)
    return pl.pallas_call(
        cross_forward_kernel,
        grid=(2, pairs),
        out_shape=(
            jax.ShapeDtypeStruct((2, frames, width), bf16),
            jax.ShapeDtypeStruct((2, pairs, 8, LANES), f32),
        ),
        in_specs=[long, keys, values],
        out_specs=(long, pl.BlockSpec((None, None, 8, LANES), lambda m, i: (m, i, 0, 0))),
        compiler_params=pltpu.CompilerParams(vmem_limit_bytes=32 << 20),
        cost_estimate=pl.CostEstimate(
            flops=32 * frames * LANES * width, bytes_accessed=8 * frames * width, transcendentals=0
        ),
    )(q, kv, kv)


def cross_backward_kernel(q_ref, k_ref, v_ref, g_ref, dq_ref, dk_ref, dv_ref):
    masks = head_masks()
    text = k_ref.shape[0]
    keys, values = pair_rows(k_ref[...], masks), pair_rows(v_ref[...], masks)
    q, g = q_ref[...], g_ref[...]
    weights, _ = cross_weights_of(q, keys, masks)
    grads = dotf(g, values, NT)
    products = weights * grads
    centers = [jnp.sum(jnp.where(mask, products, 0.0), axis=1, keepdims=True) for mask in masks]
    ds = (weights * (grads - jnp.where(masks[0], centers[0], centers[1]))).astype(bf16)
    dq_ref[...] = (dotf(ds, keys, NN) * 0.125).astype(bf16)
    dk = dotf(ds, q, TN) * 0.125
    dv = dotf(weights.astype(bf16), g, TN)
    dk_ref[...] = jnp.where(masks[0], dk[:text], dk[text:]).astype(bf16)
    dv_ref[...] = jnp.where(masks[0], dv[:text], dv[text:]).astype(bf16)


def cross_attend_back(q, kv, grad, width):
    frames, text, pairs = q.shape[1], kv.shape[1], width // LANES
    long, keys, values = cross_specs(frames, text, pairs)
    return pl.pallas_call(
        cross_backward_kernel,
        grid=(2, pairs),
        out_shape=(
            jax.ShapeDtypeStruct((2, frames, width), bf16),
            jax.ShapeDtypeStruct((2, text, width), bf16),
            jax.ShapeDtypeStruct((2, text, width), bf16),
        ),
        in_specs=[long, keys, values, long],
        out_specs=(long, keys, keys),
        compiler_params=pltpu.CompilerParams(vmem_limit_bytes=32 << 20),
        cost_estimate=pl.CostEstimate(
            flops=64 * frames * LANES * width, bytes_accessed=12 * frames * width, transcendentals=0
        ),
    )(q, kv, kv, grad)


def weight_grad_whole_kernel(x_ref, y0_ref, y1_ref, *refs):
    half, tile = pl.program_id(0), pl.program_id(1)
    o_ref, turned = refs[-2:]

    @pl.when((half == 0) & (tile == 0))
    def _():
        turned[...] = x_ref[...].T

    for m, y_ref in enumerate((y0_ref, y1_ref)):

        @pl.when(half == m)
        def _(y_ref=y_ref):
            step = o_ref.shape[0] // 4
            for i in range(4):
                rows = slice(i * step, (i + 1) * step)
                o_ref[rows, :] = dotf(turned[rows, :], y_ref[...], NN).astype(bf16)


def weight_grad_whole(x, ys, tile, columns, begin, into=None):
    frames, depth = x.shape
    width = ys[0].shape[1]
    tiles, first = width // tile, begin // tile
    given = [] if into is None else [into]
    return pl.pallas_call(
        weight_grad_whole_kernel,
        grid=(2, tiles),
        in_specs=[
            pl.BlockSpec((frames, depth), lambda m, j: (0, 0)),
            pl.BlockSpec((frames, tile), lambda m, j: (0, jnp.where(m == 0, j, tiles - 1))),
            pl.BlockSpec((frames, tile), lambda m, j: (0, jnp.where(m == 0, 0, j))),
        ]
        + [pl.BlockSpec(memory_space=pl.ANY)] * len(given),
        out_specs=pl.BlockSpec((None, depth, tile), lambda m, j: (m, 0, first + j)),
        scratch_shapes=[pltpu.VMEM((depth, frames), bf16)],
        out_shape=jax.ShapeDtypeStruct((2, depth, columns), bf16),
        input_output_aliases={3: 0} if given else {},
        compiler_params=pltpu.CompilerParams(vmem_limit_bytes=40 << 20),
        cost_estimate=pl.CostEstimate(
            flops=4 * frames * depth * width,
            bytes_accessed=4 * (depth + frames) * width + 2 * frames * depth,
            transcendentals=0,
        ),
    )(x, *ys, *given)


def swap(values, axis_name, pairs):
    return lax.ppermute(values, axis_name, pairs)


MP_PAIRS = [(0, 1), (1, 0)]
CORE_PAIRS = [(i, i ^ 1) for i in range(Z * Y * CORES)]


def over_all(value, join):
    value = join(value, swap(value, "dp", CORE_PAIRS))
    value = join(value, swap(value, "mp", MP_PAIRS))
    for bit in (2, 4, 8):
        pairs = [(i, i ^ bit) for i in range(Z * Y * CORES)]
        value = join(value, swap(value, "dp", pairs))
    return value


def joined(arrays):
    return jnp.concatenate(arrays, axis=1)


def norm_rows_of(stream):
    center = stream - jnp.mean(stream, axis=-1, keepdims=True)
    inverse = lax.rsqrt(jnp.mean(center * center, axis=-1, keepdims=True) + EPSILON)
    return center * inverse, inverse


def norm_back(stream, gain, grad):
    rows, inverse = norm_rows_of(stream)
    scaled = grad * gain
    back = inverse * (
        scaled
        - jnp.mean(scaled, axis=-1, keepdims=True)
        - rows * jnp.mean(scaled * rows, axis=-1, keepdims=True)
    )
    return back, jnp.sum(grad * rows, axis=0), jnp.sum(grad, axis=0)


def clip_per_device(
    inputs,
    text_states,
    cotangent,
    norm_params,
    self_query_key,
    self_value,
    self_output,
    cross_query,
    cross_key_value,
    cross_output,
    hidden_in,
    hidden_out,
):
    dp, mp = lax.axis_index("dp"), lax.axis_index("mp")
    z = dp // (Y * CORES)
    rows, width = self_value.shape
    both = range(2)

    def shard_of(pieces):
        return jnp.concatenate([rounded(p).reshape(rows, -1) for p in pieces], axis=1)

    def gathered(shard):
        whole = lax.all_gather(shard, ("mp", "dp"), axis=0, tiled=True)
        return whole.reshape(2, D, shard.shape[1])

    def other_half(array):
        return rounded(lax.dynamic_index_in_dim(array, 1 - mp, 0, keepdims=False))

    def whole_clip(array, got, kind):
        own = lax.dynamic_index_in_dim(array, mp, 0, keepdims=False).astype(kind)
        got = got.astype(kind)
        return jnp.where(
            mp == 0, jnp.concatenate([own, got], axis=0), jnp.concatenate([got, own], axis=0)
        )

    def other_frames(array):
        count = array.shape[0] // 2
        return rounded(lax.dynamic_slice_in_dim(array, (1 - mp) * count, count, 0))

    def own_frames(array, got):
        count = array.shape[0] // 2
        own = lax.dynamic_slice_in_dim(array, mp * count, count, 0)
        got = got.astype(f32)
        return jnp.where(mp == 0, jnp.stack([own, got]), jnp.stack([got, own]))

    norms_padded = jnp.pad(norm_params, ((0, 0), (0, LANES - norm_params.shape[1])))
    hidden = hidden_in.shape[1]
    self_shard = shard_of([self_query_key, self_value, self_output, norms_padded])
    cross_shard = shard_of([cross_query, cross_key_value, cross_output, hidden_in])
    sent = (other_half(inputs), other_half(text_states))
    self_shard, cross_shard, sent = lax.optimization_barrier((self_shard, cross_shard, sent))
    cross_all = gathered(cross_shard)
    self_all, (got_inputs, got_text) = gather_now(16, self_shard, sent)
    self_all = self_all.reshape(2, D, self_shard.shape[1])
    out_all = gathered(rounded(hidden_out))
    norms = self_all[0, :, 4 * width : 4 * width + norm_params.shape[1]].astype(f32).T
    self_o = [self_all[m, :, 3 * width : 4 * width] for m in both]
    cross_q = [cross_all[m, :, :width] for m in both]
    cross_kv = [cross_all[m, :, width : 3 * width] for m in both]
    cross_o = [cross_all[m, :, 3 * width : 4 * width] for m in both]
    in_w = [cross_all[m, :, 4 * width :] for m in both]

    def times(array, matrix):
        return dotf(array, matrix, NN)

    def times_turned(arrays, matrices):
        return dotf(arrays[0], matrices[0], NT) + dotf(arrays[1], matrices[1], NT)

    stream = whole_clip(inputs, got_inputs, f32)
    states = whole_clip(text_states, got_text, bf16)
    normed_self = rounded(norm_rows_of(stream)[0] * norms[0] + norms[1])
    qkv = project_both(normed_self, self_all, 0, 3 * width)
    qkv, cotangent = lax.optimization_barrier((qkv, cotangent))
    upstream = whole_clip(cotangent, swap(other_half(cotangent), "mp", MP_PAIRS), f32)
    mixed_self, lse, self_peaks = self_attend(qkv, width)
    after_self = unproject_both(0, [], halves_of(mixed_self), self_all, 3 * width, width, stream)
    normed_cross = rounded(norm_rows_of(after_self)[0] * norms[2] + norms[3])
    queries = project_both(normed_cross, cross_all, 0, width)
    text_kv = jnp.stack([rounded(times(states, cross_kv[m])) for m in both])
    mixed_cross, cross_peaks = cross_attend(queries, text_kv, width)
    after_cross = unproject_both(0, [], halves_of(mixed_cross), cross_all, 3 * width, width, after_self)
    normed_hidden = rounded(norm_rows_of(after_cross)[0] * norms[4] + norms[5])
    upward = [times(normed_hidden, in_w[m]) for m in both]
    activated, pulls = zip(*[jax.vjp(gelu_exact, up) for up in upward])
    activated = [rounded(a) for a in activated]

    branch = rounded(upstream)
    hidden_grad = weight_grad_whole(branch, activated, 512, 2 * hidden, hidden)
    def peaks_of(peaks):
        return peaks[:, :, :2, 0].reshape(2, -1)

    tops = over_all(jnp.stack([peaks_of(self_peaks), peaks_of(cross_peaks)]), jnp.maximum)
    tops = lax.dynamic_index_in_dim(tops, mp, 1, keepdims=False)
    factors = CLIP_LIMIT / jnp.maximum(tops, CLIP_LIMIT)
    root_scales = jnp.repeat(jnp.sqrt(factors), D // HEADS, axis=1)
    clipped = (
        self_query_key * root_scales[0][None, None, :],
        cross_query * root_scales[1][None, :],
        cross_key_value[:, 0] * root_scales[1][None, :],
    )
    out_all, hidden_grad, clipped = lax.optimization_barrier((out_all, hidden_grad, clipped))
    grad_up = [rounded(pulls[m](times(branch, out_all[m]))[0]) for m in both]
    hidden_grad = weight_grad_whole(normed_hidden, grad_up, 512, 2 * hidden, 0, hidden_grad)
    grad_up, hidden_grad = lax.optimization_barrier((grad_up, hidden_grad))
    shard_hidden = lax.psum_scatter(
        hidden_grad.reshape(2 * D, 2 * hidden), ("mp", "dp"), scatter_dimension=0, tiled=True
    ).astype(f32)
    grad_normed = unproject_both(
        0, [], [(a, m, 0) for m, a in enumerate(grad_up)], cross_all, 4 * width, hidden
    )
    back, gain_three, bias_three = norm_back(after_cross, norms[4], grad_normed)
    grad_stream = upstream + back

    branch_cross = rounded(grad_stream)
    grad_mixed = project_both(branch_cross, cross_all, 3 * width, width)
    dq, dk, dv = cross_attend_back(queries, text_kv, grad_mixed, width)
    grad_normed = unproject_both(0, [], halves_of(dq), cross_all, 0, width)
    back, gain_two, bias_two = norm_back(after_self, norms[2], grad_normed)
    dkv = [joined([dk[m], dv[m]]) for m in both]
    grad_text = times_turned(dkv, cross_kv)
    swap_text = Holder(other_frames(grad_text))
    grad_stream = grad_stream + back
    branch_self = rounded(grad_stream)
    group_pair = exchanged_grad(1, [], [normed_cross, states], [(0, [dq]), (1, [dk]), (1, [dv])], rows)
    group_out = exchanged_grad(
        2, [], [branch_cross, branch_self], [(0, [mixed_cross]), (1, [mixed_self])], rows
    )
    grad_mixed = project_both(branch_self, self_all, 3 * width, width)
    pairs = width // LANES
    cut = 2 * pairs // 3
    early = self_attend_back(
        3, [("x1", group_pair), ("y1", group_pair)], qkv, grad_mixed, lse, width, 0, cut
    )
    activated, early = lax.optimization_barrier((activated, early))
    output = unproject_both(
        4, [("x1", group_out), ("y1", group_out)], [(a, m, 0) for m, a in enumerate(activated)], out_all, 0, hidden, after_cross
    )
    swap_output = Holder(other_frames(output))
    group_early = exchanged_grad(
        5, [("x0", swap_text), ("x2", group_pair), ("y2", group_pair)], [normed_self], [(0, list(early))], rows
    )
    late = self_attend_back(
        6,
        [
            ("x2", group_out),
            ("y2", group_out),
            ("za", group_pair),
            ("zb", group_pair),
            ("x0", swap_output),
        ],
        qkv,
        grad_mixed,
        lse,
        width,
        cut,
        pairs,
    )
    group_late = exchanged_grad(
        7, [("x1", group_early), ("y1", group_early)], [normed_self], [(0, list(late))], rows
    )
    pieces = []
    for half in both:
        for part, arrays in enumerate((early, late)):
            pieces += [(a, half, i * width + part * cut * LANES) for i, a in enumerate(arrays)]
    grad_normed = unproject_both(
        8,
        [
            ("x1", group_late),
            ("y1", group_late),
            ("x2", group_early),
            ("y2", group_early),
            ("za", group_out),
            ("zb", group_out),
        ],
        pieces,
        self_all,
        0,
        3 * width,
    )
    back, gain_one, bias_one = norm_back(stream, norms[0], grad_normed)
    norm_grads = jnp.stack([gain_one, bias_one, gain_two, bias_two, gain_three, bias_three])
    grad_inputs = grad_stream + back
    sent = other_frames(grad_inputs)
    swaps_inputs = [Holder(sent[: sent.shape[0] // 2]), Holder(sent[sent.shape[0] // 2 :])]
    norm_grads = relay(
        9,
        [
            ("x2", group_late),
            ("y2", group_late),
            ("za", group_early),
            ("zb", group_early),
            ("x0", swaps_inputs[0]),
            ("total", group_pair),
            ("total", group_out),
        ],
        jnp.pad(norm_grads, ((0, 2), (0, 0))),
    )[:6]
    last_hop(10, [("za", group_late), ("zb", group_late), ("x0", swaps_inputs[1]), ("total", group_early)])
    grad_inputs = own_frames(grad_inputs, jnp.concatenate([h.got() for h in swaps_inputs]))
    grad_text = own_frames(grad_text, swap_text.got())
    output = own_frames(output, swap_output.got())
    shard_pair, shard_outs = group_pair.arrays["total"], group_out.arrays["total"]
    halves = [group_early.arrays["total"], group_late.result(z)]
    sizes = [cut * LANES, width - cut * LANES]
    shard_self = [
        joined([h[:, i * n : (i + 1) * n] for h, n in zip(halves, sizes)]) for i in range(3)
    ]

    shard_norms = lax.dynamic_slice_in_dim(norm_grads, dp * rows, rows, 1).T

    return (
        output,
        grad_inputs,
        grad_text,
        shard_norms,
        jnp.stack(shard_self[:2], axis=1),
        shard_self[2],
        shard_outs[:, width:],
        shard_pair[:, :width],
        shard_pair[:, width:].reshape(rows, 2, width),
        shard_outs[:, :width],
        shard_hidden[:, :hidden],
        shard_hidden[:, hidden:],
        factors,
        *clipped,
    )


def solution(mesh):
    in_specs = (
        P("dp", "mp", None),
        P("dp", "mp", None),
        P("dp", "mp", None),
        P("dp", None),
        P("dp", None, "mp"),
        P("dp", "mp"),
        P("dp", "mp"),
        P("dp", "mp"),
        P("dp", None, "mp"),
        P("dp", "mp"),
        P("dp", "mp"),
        P("dp", "mp"),
    )
    out_specs = (
        P("dp", "mp", None),
        P("dp", "mp", None),
        P("dp", "mp", None),
        P("dp", None),
        P("dp", None, "mp"),
        P("dp", "mp"),
        P("dp", "mp"),
        P("dp", "mp"),
        P("dp", None, "mp"),
        P("dp", "mp"),
        P("dp", "mp"),
        P("dp", "mp"),
        P(None, "mp"),
        P("dp", None, "mp"),
        P("dp", "mp"),
        P("dp", "mp"),
    )
    by_clip = mesh.shape["mp"] == 2 and mesh.shape["dp"] == 16
    return jax.shard_map(
        clip_per_device if by_clip else per_device, mesh=mesh, in_specs=in_specs, out_specs=out_specs, check_vma=False
    )
```

```python
import functools
import math

import jax
import jax.numpy as jnp
from jax import lax
from jax.experimental import pallas as pl
from jax.experimental.pallas import tpu as pltpu
from jax.sharding import PartitionSpec as P

D = 1536
HEADS = 24


EPSILON = 1e-05
CLIP_LIMIT = 7.0
MASKED = -1e30


def layer_norm(stream_rows, gain_row, bias_row):
    center = stream_rows - jnp.mean(stream_rows, axis=-1, keepdims=True)
    spread = jnp.mean(center * center, axis=-1, keepdims=True)
    return center * lax.rsqrt(spread + EPSILON) * gain_row + bias_row


def gelu_exact(values):
    return 0.5 * values * (1.0 + lax.erf(values * 2.0 ** (-0.5)))


def rounded(values):
    return values.astype(jnp.bfloat16)


def project(array, matrix):
    return jnp.einsum("cld,de->cle", array, matrix, preferred_element_type=jnp.float32)


def unproject(array, matrix):
    return jnp.einsum("cle,de->cld", array, matrix, preferred_element_type=jnp.float32)


def outer_sum(left, right):
    return jnp.einsum("cld,cle->de", left, right, preferred_element_type=jnp.float32)


def widen(values):
    return lax.all_gather(values, "mp", axis=1, tiled=True)


def settle(partial_sum):
    return lax.psum_scatter(
        partial_sum.astype(jnp.bfloat16), "mp", scatter_dimension=1, tiled=True
    ).astype(jnp.float32)


def widen_grad(values):
    return lax.all_gather(values, "mp", axis=1, tiled=True)


def settle_grad(partial_sum):
    return lax.psum_scatter(
        partial_sum.astype(jnp.bfloat16), "mp", scatter_dimension=1, tiled=True
    ).astype(jnp.float32)


def self_forward(queries, keys_all, values_all):
    frame_count, head_count, head_width = (queries.shape[1], queries.shape[2], queries.shape[3])
    block_rows = min(512, frame_count)
    block_count = frame_count // block_rows
    scaling = head_width ** (-0.5)
    row_ids = jnp.arange(block_rows)
    col_ids = jnp.arange(frame_count)

    def per_clip(triple):
        clip_queries, clip_keys, clip_values = triple

        def per_block(block_index):
            offset = block_index * block_rows
            block_queries = lax.dynamic_slice_in_dim(clip_queries, offset, block_rows, 0)
            scores = (
                jnp.einsum(
                    "qhe,khe->hqk", block_queries, clip_keys, preferred_element_type=jnp.float32
                )
                * scaling
            )
            allowed = col_ids[None, :] <= (offset + row_ids)[:, None]
            scores = jnp.where(allowed[None], scores, MASKED)
            highest = jnp.max(scores, axis=2, keepdims=True)
            exponents = jnp.exp(scores - highest)
            row_sums = jnp.sum(exponents, axis=2, keepdims=True)
            mixed = jnp.einsum(
                "hqk,khe->qhe",
                rounded(exponents / row_sums),
                clip_values,
                preferred_element_type=jnp.float32,
            )
            return (
                mixed,
                (highest + jnp.log(row_sums))[:, :, 0],
                jnp.max(highest[:, :, 0], axis=1),
            )

        mixed, log_sums, block_peaks = lax.map(per_block, jnp.arange(block_count))
        return (
            mixed.reshape(frame_count, head_count, head_width),
            log_sums,
            jnp.max(block_peaks, axis=0),
        )

    mixed, log_sums, clip_peaks = lax.map(per_clip, (queries, keys_all, values_all))
    return (mixed, log_sums, jnp.max(clip_peaks, axis=0))


def self_backward(queries, keys_all, values_all, log_sums, grad_mixed):
    frame_count, head_count, head_width = (queries.shape[1], queries.shape[2], queries.shape[3])
    block_rows = min(512, frame_count)
    block_count = frame_count // block_rows
    scaling = head_width ** (-0.5)
    row_ids = jnp.arange(block_rows)
    col_ids = jnp.arange(frame_count)

    def per_clip(bundle):
        clip_queries, clip_keys, clip_values, clip_logs, clip_grads = bundle

        def per_block(carried, block_index):
            grad_keys, grad_values = carried
            offset = block_index * block_rows
            block_queries = lax.dynamic_slice_in_dim(clip_queries, offset, block_rows, 0)
            block_grads = lax.dynamic_slice_in_dim(clip_grads, offset, block_rows, 0)
            scores = (
                jnp.einsum(
                    "qhe,khe->hqk", block_queries, clip_keys, preferred_element_type=jnp.float32
                )
                * scaling
            )
            allowed = col_ids[None, :] <= (offset + row_ids)[:, None]
            scores = jnp.where(allowed[None], scores, MASKED)
            weights = jnp.exp(scores - clip_logs[block_index][:, :, None])
            grad_values = grad_values + jnp.einsum(
                "hqk,qhe->khe", rounded(weights), block_grads, preferred_element_type=jnp.float32
            )
            grad_weights = jnp.einsum(
                "qhe,khe->hqk", block_grads, clip_values, preferred_element_type=jnp.float32
            )
            centered = grad_weights - jnp.sum(weights * grad_weights, axis=2, keepdims=True)
            grad_scores = rounded(weights * centered)
            grad_queries = (
                jnp.einsum(
                    "hqk,khe->qhe", grad_scores, clip_keys, preferred_element_type=jnp.float32
                )
                * scaling
            )
            grad_keys = (
                grad_keys
                + jnp.einsum(
                    "hqk,qhe->khe", grad_scores, block_queries, preferred_element_type=jnp.float32
                )
                * scaling
            )
            return ((grad_keys, grad_values), grad_queries)

        zero_keys = jnp.zeros(clip_keys.shape, jnp.float32)
        (grad_keys, grad_values), grad_queries = lax.scan(
            per_block, (zero_keys, zero_keys), jnp.arange(block_count)
        )
        return (grad_queries.reshape(frame_count, head_count, head_width), grad_keys, grad_values)

    return lax.map(per_clip, (queries, keys_all, values_all, log_sums, grad_mixed))


def cross_forward(queries, keys_all, values_all):
    scaling = queries.shape[3] ** (-0.5)
    scores = (
        jnp.einsum("clhe,cshe->chls", queries, keys_all, preferred_element_type=jnp.float32)
        * scaling
    )
    highest = jnp.max(scores, axis=3, keepdims=True)
    exponents = jnp.exp(scores - highest)
    weights = exponents / jnp.sum(exponents, axis=3, keepdims=True)
    mixed = jnp.einsum(
        "chls,cshe->clhe", rounded(weights), values_all, preferred_element_type=jnp.float32
    )
    return (mixed, weights, jnp.max(highest, axis=(0, 2, 3)))


def cross_backward(queries, keys_all, values_all, weights, grad_mixed):
    scaling = queries.shape[3] ** (-0.5)
    grad_values = jnp.einsum(
        "chls,clhe->cshe", rounded(weights), grad_mixed, preferred_element_type=jnp.float32
    )
    grad_weights = jnp.einsum(
        "clhe,cshe->chls", grad_mixed, values_all, preferred_element_type=jnp.float32
    )
    centered = grad_weights - jnp.sum(weights * grad_weights, axis=3, keepdims=True)
    grad_scores = rounded(weights * centered)
    grad_queries = (
        jnp.einsum("chls,cshe->clhe", grad_scores, keys_all, preferred_element_type=jnp.float32)
        * scaling
    )
    grad_keys = (
        jnp.einsum("chls,clhe->cshe", grad_scores, queries, preferred_element_type=jnp.float32)
        * scaling
    )
    return (grad_queries, grad_keys, grad_values)


def per_device(
    inputs,
    text_states,
    cotangent,
    norm_params,
    self_query_key,
    self_value,
    self_output,
    cross_query,
    cross_key_value,
    cross_output,
    hidden_in,
    hidden_out,
):
    (
        full_norms,
        full_query_key,
        full_value,
        full_output,
        full_cross_query,
        full_cross_pair,
        full_cross_output,
        full_hidden_in,
        full_hidden_out,
    ) = (
        lax.all_gather(rounded(norm_params), "dp", axis=0, tiled=True),
        lax.all_gather(rounded(self_query_key), "dp", axis=0, tiled=True),
        lax.all_gather(rounded(self_value), "dp", axis=0, tiled=True),
        lax.all_gather(rounded(self_output), "dp", axis=0, tiled=True),
        lax.all_gather(rounded(cross_query), "dp", axis=0, tiled=True),
        lax.all_gather(rounded(cross_key_value), "dp", axis=0, tiled=True),
        lax.all_gather(rounded(cross_output), "dp", axis=0, tiled=True),
        lax.all_gather(rounded(hidden_in), "dp", axis=0, tiled=True),
        lax.all_gather(rounded(hidden_out), "dp", axis=0, tiled=True),
    )
    norm_rows = full_norms.astype(jnp.float32)
    head_width = D // HEADS
    head_count = full_value.shape[1] // head_width

    def split_heads(array):
        return array.reshape(array.shape[0], array.shape[1], head_count, head_width)

    def merge_heads(array):
        return array.reshape(array.shape[0], array.shape[1], head_count * head_width)

    normed, pull_self = jax.vjp(layer_norm, inputs, norm_rows[:, 0], norm_rows[:, 1])
    normed_self = widen(rounded(normed))
    query_key_rows = jnp.einsum(
        "cld,dte->clte", normed_self, full_query_key, preferred_element_type=jnp.float32
    )
    queries = rounded(query_key_rows[:, :, 0])
    self_keys = rounded(query_key_rows[:, :, 1])
    values = rounded(project(normed_self, full_value))
    mixed, log_sums, self_peaks = self_forward(
        split_heads(queries), split_heads(self_keys), split_heads(values)
    )
    mixed_self = rounded(merge_heads(mixed))
    after_self = inputs + settle(unproject(mixed_self, full_output))
    normed, pull_cross = jax.vjp(layer_norm, after_self, norm_rows[:, 2], norm_rows[:, 3])
    normed_cross = widen(rounded(normed))
    cross_queries = rounded(project(normed_cross, full_cross_query))
    states = lax.all_gather(rounded(text_states), "mp", axis=1, tiled=True)
    key_value_rows = jnp.einsum(
        "csd,dte->cste", states, full_cross_pair, preferred_element_type=jnp.float32
    )
    cross_keys = rounded(key_value_rows[:, :, 0])
    cross_values = rounded(key_value_rows[:, :, 1])
    attended, cross_weights, cross_peaks = cross_forward(
        split_heads(cross_queries), split_heads(cross_keys), split_heads(cross_values)
    )
    mixed_cross = rounded(merge_heads(attended))
    after_cross = after_self + settle(unproject(mixed_cross, full_cross_output))
    normed, pull_hidden = jax.vjp(layer_norm, after_cross, norm_rows[:, 4], norm_rows[:, 5])
    normed_hidden = widen(rounded(normed))
    upward = project(normed_hidden, full_hidden_in)
    activated, pull_gelu = jax.vjp(gelu_exact, upward)
    activated = rounded(activated)
    output = after_cross + settle(unproject(activated, full_hidden_out))
    self_top, cross_top = lax.pmax((self_peaks, cross_peaks), "dp")
    grad_branch = widen_grad(rounded(cotangent))
    grad_hidden_out = outer_sum(grad_branch, activated)
    grad_upward = rounded(pull_gelu(project(grad_branch, full_hidden_out))[0])
    grad_hidden_in = outer_sum(normed_hidden, grad_upward)
    grad_normed = settle_grad(unproject(grad_upward, full_hidden_in))
    back_stream, grad_gain_three, grad_bias_three = pull_hidden(grad_normed)
    grad_stream = cotangent + back_stream
    grad_branch = widen_grad(rounded(grad_stream))
    grad_cross_output = outer_sum(grad_branch, mixed_cross)
    grad_attended = rounded(project(grad_branch, full_cross_output))
    grad_queries, grad_keys, grad_values = cross_backward(
        split_heads(cross_queries),
        split_heads(cross_keys),
        split_heads(cross_values),
        cross_weights,
        split_heads(grad_attended),
    )
    grad_queries = rounded(merge_heads(grad_queries))
    grad_pair = rounded(jnp.stack([merge_heads(grad_keys), merge_heads(grad_values)], axis=2))
    grad_cross_query = outer_sum(normed_cross, grad_queries)
    grad_cross_pair = jnp.einsum(
        "csd,cste->dte", states, grad_pair, preferred_element_type=jnp.float32
    )
    grad_text = lax.psum_scatter(
        jnp.einsum(
            "cste,dte->csd", grad_pair, full_cross_pair, preferred_element_type=jnp.float32
        ).astype(jnp.bfloat16),
        "mp",
        scatter_dimension=1,
        tiled=True,
    ).astype(jnp.float32)
    grad_normed = settle_grad(unproject(grad_queries, full_cross_query))
    back_stream, grad_gain_two, grad_bias_two = pull_cross(grad_normed)
    grad_stream = grad_stream + back_stream
    grad_branch = widen_grad(rounded(grad_stream))
    grad_self_output = outer_sum(grad_branch, mixed_self)
    grad_mixed = rounded(project(grad_branch, full_output))
    grad_queries, grad_keys, grad_values = self_backward(
        split_heads(queries),
        split_heads(self_keys),
        split_heads(values),
        log_sums,
        split_heads(grad_mixed),
    )
    grad_pair = rounded(jnp.stack([merge_heads(grad_queries), merge_heads(grad_keys)], axis=2))
    grad_values = rounded(merge_heads(grad_values))
    grad_self_pair = jnp.einsum(
        "cld,clte->dte", normed_self, grad_pair, preferred_element_type=jnp.float32
    )
    grad_self_value = outer_sum(normed_self, grad_values)
    grad_normed = settle_grad(
        jnp.einsum("clte,dte->cld", grad_pair, full_query_key, preferred_element_type=jnp.float32)
        + unproject(grad_values, full_value)
    )
    back_stream, grad_gain_one, grad_bias_one = pull_self(grad_normed)
    grad_inputs = grad_stream + back_stream
    grad_norm_rows = lax.psum(
        jnp.stack(
            [
                grad_gain_one,
                grad_bias_one,
                grad_gain_two,
                grad_bias_two,
                grad_gain_three,
                grad_bias_three,
            ],
            axis=1,
        ).astype(jnp.bfloat16),
        "mp",
    )
    (
        shard_norms,
        shard_self_pair,
        shard_self_value,
        shard_self_output,
        shard_cross_query,
        shard_cross_pair,
        shard_cross_output,
        shard_hidden_in,
        shard_hidden_out,
    ) = (
        lax.psum_scatter(grad_norm_rows, "dp", scatter_dimension=0, tiled=True).astype(jnp.float32),
        lax.psum_scatter(
            grad_self_pair.astype(jnp.bfloat16), "dp", scatter_dimension=0, tiled=True
        ).astype(jnp.float32),
        lax.psum_scatter(
            grad_self_value.astype(jnp.bfloat16), "dp", scatter_dimension=0, tiled=True
        ).astype(jnp.float32),
        lax.psum_scatter(
            grad_self_output.astype(jnp.bfloat16), "dp", scatter_dimension=0, tiled=True
        ).astype(jnp.float32),
        lax.psum_scatter(
            grad_cross_query.astype(jnp.bfloat16), "dp", scatter_dimension=0, tiled=True
        ).astype(jnp.float32),
        lax.psum_scatter(
            grad_cross_pair.astype(jnp.bfloat16), "dp", scatter_dimension=0, tiled=True
        ).astype(jnp.float32),
        lax.psum_scatter(
            grad_cross_output.astype(jnp.bfloat16), "dp", scatter_dimension=0, tiled=True
        ).astype(jnp.float32),
        lax.psum_scatter(
            grad_hidden_in.astype(jnp.bfloat16), "dp", scatter_dimension=0, tiled=True
        ).astype(jnp.float32),
        lax.psum_scatter(
            grad_hidden_out.astype(jnp.bfloat16), "dp", scatter_dimension=0, tiled=True
        ).astype(jnp.float32),
    )
    factors = CLIP_LIMIT / jnp.maximum(jnp.stack([self_top, cross_top]), CLIP_LIMIT)
    root_scales = jnp.repeat(jnp.sqrt(factors), head_width, axis=1)
    clipped_self = self_query_key * root_scales[0][None, None, :]
    clipped_query = cross_query * root_scales[1][None, :]
    clipped_key = cross_key_value[:, 0] * root_scales[1][None, :]
    return (
        output,
        grad_inputs,
        grad_text,
        shard_norms,
        shard_self_pair,
        shard_self_value,
        shard_self_output,
        shard_cross_query,
        shard_cross_pair,
        shard_cross_output,
        shard_hidden_in,
        shard_hidden_out,
        factors,
        clipped_self,
        clipped_query,
        clipped_key,
    )


NT = (((1,), (1,)), ((), ()))
TN = (((0,), (0,)), ((), ()))
NN = (((1,), (0,)), ((), ()))
f32 = jnp.float32
bf16 = jnp.bfloat16
LANES = 128
MESH = pl.DeviceIdType.MESH
Z, Y, CORES = 4, 2, 2


def dotf(a, b, dims):
    return lax.dot_general(a, b, dims, preferred_element_type=f32)


def head_masks():
    lane = lax.broadcasted_iota(jnp.int32, (1, LANES), 1)
    return [lane < 64, lane >= 64]


def self_forward_kernel(rows_at_once, q_ref, k_ref, v_ref, o_ref, lse_ref, peak_ref):
    frames, size = q_ref.shape[0], rows_at_once
    masks = head_masks()
    key_row = lax.broadcasted_iota(jnp.int32, (size, size), 0)
    query_col = lax.broadcasted_iota(jnp.int32, (size, size), 1)
    allowed = key_row <= query_col
    zero = jnp.zeros((), bf16)
    peaks = [None, None]
    values = [jnp.where(mask, v_ref[...], zero) for mask in masks]
    for block in range(frames // size):
        first = block * size
        rows = slice(first, first + size)
        q = q_ref[rows, :] * jnp.asarray(0.125, bf16)
        mixed = None
        for h in range(2):
            qh = jnp.where(masks[h], q, zero)
            diagonal = jnp.where(allowed, dotf(k_ref[rows, :], qh, NT), MASKED)
            top = jnp.max(diagonal, axis=0, keepdims=True)
            if first:
                full = dotf(k_ref[0:first, :], qh, NT)
                top = jnp.maximum(top, jnp.max(full, axis=0, keepdims=True))
            diagonal = jnp.exp(diagonal - top)
            total = jnp.sum(diagonal, axis=0, keepdims=True)
            part = dotf(diagonal.astype(bf16), values[h][rows, :], TN)
            if first:
                full = jnp.exp(full - top)
                total = total + jnp.sum(full, axis=0, keepdims=True)
                part = part + dotf(full.astype(bf16), values[h][0:first, :], TN)
            lse_ref[h : h + 1, rows] = top + jnp.log(total)
            part = part * (1.0 / total).reshape(size, 1)
            mixed = part if mixed is None else mixed + part
            peaks[h] = top if peaks[h] is None else jnp.maximum(peaks[h], top)
        o_ref[rows, :] = mixed.astype(bf16)
    for h in range(2):
        peak_ref[h : h + 1, :] = jnp.broadcast_to(
            jnp.max(peaks[h], axis=1, keepdims=True), (1, LANES)
        )


def self_attend(qkv, width):
    frames, pairs = qkv.shape[1], width // LANES
    at = lambda offset: pl.BlockSpec((None, frames, LANES), lambda m, i: (m, 0, offset + i))
    stat = lambda n: pl.BlockSpec((None, None, 8, n), lambda m, i: (m, i, 0, 0))
    return pl.pallas_call(
        functools.partial(self_forward_kernel, 512),
        grid=(2, pairs),
        out_shape=(
            jax.ShapeDtypeStruct((2, frames, width), bf16),
            jax.ShapeDtypeStruct((2, pairs, 8, frames), f32),
            jax.ShapeDtypeStruct((2, pairs, 8, LANES), f32),
        ),
        in_specs=[at(0), at(pairs), at(2 * pairs)],
        out_specs=(at(0), stat(frames), stat(LANES)),
        compiler_params=pltpu.CompilerParams(vmem_limit_bytes=40 << 20),
        cost_estimate=pl.CostEstimate(
            flops=16 * frames * frames * width,
            bytes_accessed=16 * frames * width,
            transcendentals=0,
        ),
    )(qkv, qkv, qkv)


def self_backward_kernel(
    rows_at_once, q_ref, k_ref, v_ref, g_ref, lse_ref, dq_ref, dk_ref, dv_ref, dk_sum, dv_sum
):
    frames, size = q_ref.shape[0], rows_at_once
    masks = head_masks()
    key_row = lax.broadcasted_iota(jnp.int32, (size, size), 0)
    query_col = lax.broadcasted_iota(jnp.int32, (size, size), 1)
    allowed = key_row <= query_col
    zero = jnp.zeros((), bf16)
    keys = [jnp.where(mask, k_ref[...], zero) for mask in masks]
    blocks = frames // size
    for block in reversed(range(blocks)):
        first = block * size
        spans = [(slice(first, first + size), True)]
        if first:
            spans.append((slice(0, first), False))
        rows = spans[0][0]
        q = q_ref[rows, :] * jnp.asarray(0.125, bf16)
        g = g_ref[rows, :]
        dq = None
        dk, dv = [None] * len(spans), [None] * len(spans)
        for h in range(2):
            qh, gh = jnp.where(masks[h], q, zero), jnp.where(masks[h], g, zero)
            lse = lse_ref[h : h + 1, rows]
            weights, grads, center = [], [], None
            for span, masked in spans:
                scores = dotf(k_ref[span, :], qh, NT)
                if masked:
                    scores = jnp.where(allowed, scores, MASKED)
                weights.append(jnp.exp(scores - lse))
                grads.append(dotf(v_ref[span, :], gh, NT))
                part = jnp.sum(weights[-1] * grads[-1], axis=0, keepdims=True)
                center = part if center is None else center + part
            for i, (span, _) in enumerate(spans):
                ds = (weights[i] * (grads[i] - center)).astype(bf16)
                a = dotf(weights[i].astype(bf16), gh, NN)
                b = dotf(ds, qh, NN)
                c = dotf(ds, keys[h][span, :], TN)
                dv[i] = a if dv[i] is None else dv[i] + a
                dk[i] = b if dk[i] is None else dk[i] + b
                dq = c if dq is None else dq + c
        dq_ref[rows, :] = (dq * 0.125).astype(bf16)
        for i, (span, _) in enumerate(spans):
            if block == blocks - 1:
                dk_sum[span, :] = dk[i]
                dv_sum[span, :] = dv[i]
            else:
                dk_sum[span, :] += dk[i]
                dv_sum[span, :] += dv[i]
    dk_ref[...] = dk_sum[...].astype(bf16)
    dv_ref[...] = dv_sum[...].astype(bf16)


class Hop:
    def __init__(self, kind, group):
        self.kind, self.group = kind, group
        rows, width = group.rows // 2, group.width
        self.chunk = (rows, width)
        self.count = {"x1": 8, "y1": 8, "y2": 4, "x2": 4, "za": 3, "zb": 3}[kind]
        self.lead = {"x1": (Z, Y), "y1": (2, Z), "y2": (Z,), "x2": (Z,), "za": (3,), "zb": (3,)}[kind]
        self.names = {
            "x1": ["own", "there"],
            "y1": ["own", "there"],
            "y2": ["own", "there", "x1"],
            "x2": ["own", "there", "y1"],
            "za": ["own", "there", "x1", "y2"],
            "zb": ["own", "there", "y1", "x2"],
        }[kind]

    def shape(self):
        return jax.ShapeDtypeStruct(self.lead + self.chunk, bf16)

    def scratch(self):
        return [
            pltpu.VMEM((self.count, len(self.names)) + self.chunk, bf16),
            pltpu.VMEM((self.count,) + self.chunk, bf16),
            pltpu.SemaphoreType.DMA((self.count, len(self.names))),
            pltpu.SemaphoreType.DMA((self.count,)),
            pltpu.SemaphoreType.DMA((self.count,)),
        ]

    def bind(self, sources, target, scratch):
        self.sources, self.target = sources, target
        self.loads, self.sent, self.load_sem, self.send_sem, self.recv_sem = scratch

    def index(self, t):
        half = self.chunk[0]
        low, high = pl.ds(0, half), pl.ds(half, half)
        if self.kind == "x1":
            at = (1, t // 2, t % 2, low)
            return [at, at], (t // 2, t % 2)
        if self.kind == "y1":
            at = (t // 4, t % 4, 1, high)
            return [at, at], (t // 4, t % 4)
        if self.kind == "y2":
            at = (0, t, 1, low)
            return [at, at, (t, 1)], (t,)
        if self.kind == "x2":
            at = (1, t, 0, high)
            return [at, at, (1, t)], (t,)
        z = (lax.axis_index("dp") // (Y * CORES) + t + 1) % Z
        if self.kind == "za":
            at = (0, z, 0, low)
            return [at, at, (z, 0), (z,)], (t,)
        at = (0, z, 0, high)
        return [at, at, (0, z), (z,)], (t,)

    def partner(self, t):
        dp, mp = lax.axis_index("dp"), lax.axis_index("mp")
        if self.kind in ("x1", "x2"):
            return (dp, 1 - mp)
        if self.kind in ("y1", "y2"):
            return (dp + CORES - 2 * CORES * ((dp // CORES) % Y), mp)
        group = Y * CORES
        return (((dp // group + t + 1) % Z) * group + dp % group, mp)

    def partners(self):
        return [self.partner(t) for t in range(3 if self.kind in ("za", "zb") else 1)]

    def load(self, t):
        return [
            pltpu.make_async_copy(source.at[at], self.loads.at[t, i], self.load_sem.at[t, i])
            for i, (source, at) in enumerate(zip(self.sources, self.index(t)[0]))
        ]

    def send(self, t):
        return pltpu.make_async_remote_copy(
            src_ref=self.sent.at[t],
            dst_ref=self.target.at[self.index(t)[1]],
            send_sem=self.send_sem.at[t],
            recv_sem=self.recv_sem.at[t],
            device_id=self.partner(t),
            device_id_type=MESH,
        )

    def begin(self):
        for t in range(self.count):
            for copy in self.load(t):
                copy.start()

    def each(self, steps):
        return self.count if steps < 3 else -(-self.count // 2)

    def work(self, step, steps, j):
        t = step * self.each(steps) + j

        @pl.when(t < self.count)
        def _():
            for copy in self.load(t):
                copy.wait()
            total = self.loads[t, 0].astype(f32)
            for i in range(1, len(self.names)):
                total = total + self.loads[t, i].astype(f32)
            self.sent[t] = total.astype(bf16)
            self.send(t).start()

    def finish(self):
        for t in range(self.count):
            self.send(t).wait()


class Swap:
    kind, names = "x0", ["sent"]

    def __init__(self, holder):
        self.group = holder

    def shape(self):
        sent = self.group.arrays["sent"]
        return jax.ShapeDtypeStruct(sent.shape, sent.dtype)

    def scratch(self):
        return [pltpu.SemaphoreType.DMA((1,)), pltpu.SemaphoreType.DMA((1,))]

    def bind(self, sources, target, scratch):
        self.source, self.target = sources[0], target
        self.send_sem, self.recv_sem = scratch

    def partners(self):
        return [(lax.axis_index("dp"), 1 - lax.axis_index("mp"))]

    def copy(self):
        return pltpu.make_async_remote_copy(
            src_ref=self.source,
            dst_ref=self.target,
            send_sem=self.send_sem.at[0],
            recv_sem=self.recv_sem.at[0],
            device_id=self.partners()[0],
            device_id_type=MESH,
        )

    def each(self, steps):
        return 1

    def begin(self):
        pass

    def work(self, step, steps, j):
        @pl.when(step == 0)
        def _():
            self.copy().start()

    def finish(self):
        self.copy().wait()


class Total:
    kind = "total"
    names = ["own", "there", "x1", "y2", "y1", "x2", "za", "zb"]

    def __init__(self, group):
        self.group = group
        low = group.rows // 2
        self.low, self.high = pl.ds(0, low), pl.ds(low, group.rows - low)

    def shape(self):
        return jax.ShapeDtypeStruct((self.group.rows, self.group.width), f32)

    def scratch(self):
        half, width = self.group.rows // 2, self.group.width
        return [
            pltpu.VMEM((2, 7, half, width), bf16),
            pltpu.VMEM((2 * half, width), f32),
            pltpu.SemaphoreType.DMA((2, 7)),
            pltpu.SemaphoreType.DMA(()),
        ]

    def bind(self, sources, target, scratch):
        self.sources, self.target = dict(zip(self.names, sources)), target
        self.terms, self.sum, self.load_sem, self.store_sem = scratch

    def partners(self):
        return []

    def loads(self):
        z = lax.axis_index("dp") // (Y * CORES)
        a = self.sources
        low = [a["own"].at[0, z, 0, self.low], a["there"].at[0, z, 0, self.low], a["x1"].at[z, 0]]
        low += [a["y2"].at[z]] + [a["za"].at[k] for k in range(3)]
        high = [a["own"].at[0, z, 0, self.high], a["there"].at[0, z, 0, self.high]]
        high += [a["y1"].at[0, z], a["x2"].at[z]] + [a["zb"].at[k] for k in range(3)]
        return [
            pltpu.make_async_copy(source, self.terms.at[p, i], self.load_sem.at[p, i])
            for p, part in enumerate((low, high))
            for i, source in enumerate(part)
        ]

    def each(self, steps):
        return 0

    def begin(self):
        for copy in self.loads():
            copy.start()

    def finish(self):
        for copy in self.loads():
            copy.wait()
        half = self.group.rows // 2
        for p in range(2):
            total = self.terms[p, 0].astype(f32)
            for i in range(1, 7):
                total = total + self.terms[p, i].astype(f32)
            self.sum[p * half : (p + 1) * half, :] = total
        copy = pltpu.make_async_copy(self.sum, self.target, self.store_sem)
        copy.start()
        copy.wait()


class Holder:
    def __init__(self, sent):
        self.arrays = {"sent": sent}

    def got(self):
        return self.arrays["x0"]


class Group:
    def __init__(self, own, there):
        self.arrays = {"own": own, "there": there}
        self.rows, self.width = own.shape[3], own.shape[4]

    def result(self, z):
        a = self.arrays
        half = self.rows // 2
        take = lambda array, at=0: lax.dynamic_index_in_dim(array, z, at, keepdims=False)
        total = take(a["own"][0, :, 0]).astype(f32) + take(a["there"][0, :, 0]).astype(f32)
        low = take(a["x1"][:, 0]).astype(f32) + take(a["y2"]).astype(f32)
        high = take(a["y1"][0]).astype(f32) + take(a["x2"]).astype(f32)
        for k in range(3):
            low = low + a["za"][k].astype(f32)
            high = high + a["zb"][k].astype(f32)
        return total + jnp.concatenate([low, high], axis=0)


def meet(partners):
    barrier = pltpu.get_barrier_semaphore()
    for partner in partners:
        pl.semaphore_signal(barrier, inc=1, device_id=partner, device_id_type=MESH)
    pl.semaphore_wait(barrier, len(partners))


def core_partner():
    dp = lax.axis_index("dp")
    return (dp + 1 - 2 * (dp % CORES), lax.axis_index("mp"))


def hosted(body, number, grid, args, in_specs, out_shape, out_specs, scratch, plan, flops, core=False, near=False, after=(), closing=None):
    special = {"x0": Swap, "total": Total}
    hops = [special[k](group) if k in special else Hop(k, group) for k, group in (*plan, *after)]
    made = {(id(hop.group), hop.kind): k for k, hop in enumerate(hops)}
    arrays, places = [], {}
    for hop in hops:
        for name in hop.names:
            key = (id(hop.group), name)
            if key not in places and key not in made:
                places[key] = len(arrays)
                arrays.append(hop.group.arrays[name])
    steps = 1
    for n in grid:
        steps *= n
    kinds = set(hop.kind[0] for hop in hops if hop.kind != "total")

    def kernel(*refs):
        counts = [len(args), len(arrays), len(out_shape), len(hops), len(scratch)]
        parts, at = [], 0
        for n in counts:
            parts.append(refs[at : at + n])
            at += n
        for k, hop in enumerate(hops):
            keys = [(id(hop.group), name) for name in hop.names]
            sources = [parts[3][made[key]] if key in made else parts[1][places[key]] for key in keys]
            taken = len(hop.scratch())
            hop.bind(sources, parts[3][k], refs[at : at + taken])
            at += taken
        first, last = hops[: len(plan)], hops[len(plan) :]
        step = 0
        for axis, n in enumerate(grid):
            step = step * n + pl.program_id(axis)

        @pl.when(step == 0)
        def _():
            partners = [core_partner()] if core else []
            if near:
                dp, mp = lax.axis_index("dp"), lax.axis_index("mp")
                partners += [(dp, 1 - mp), (dp + CORES - 2 * CORES * ((dp // CORES) % Y), mp)]
            for kind in sorted(kinds):
                partners += [hop for hop in hops if hop.kind[0] == kind][0].partners()
            if partners:
                meet(partners)
            for hop in first:
                hop.begin()

        for j in range(max([hop.each(steps) for hop in first], default=0)):
            for hop in first:
                if j < hop.each(steps):
                    hop.work(step, steps, j)
        body(*parts[0], *parts[2], *parts[4])

        @pl.when(step == steps - 1)
        def _():
            left = sorted(first, key=lambda hop: hop.kind != "total")
            if last:
                for hop in first:
                    if hop.kind in ("x2", "y2"):
                        hop.finish()
                        left.remove(hop)
                for hop in last:
                    if hop.kind != "total":
                        hop.begin()
                        for j in range(hop.count):
                            hop.work(0, 1, j)
            if closing is not None:
                closing(*parts[0], *parts[2], *parts[4])
            for hop in left:
                hop.finish()
            for hop in last:
                if hop.kind == "total":
                    hop.begin()
            for hop in last:
                hop.finish()

    hbm = pl.BlockSpec(memory_space=pl.ANY)
    extra = [s for hop in hops for s in hop.scratch()]
    outs = pl.pallas_call(
        kernel,
        grid=grid,
        in_specs=list(in_specs) + [hbm] * len(arrays),
        out_specs=tuple(out_specs) + (hbm,) * len(hops),
        out_shape=tuple(out_shape) + tuple(hop.shape() for hop in hops),
        scratch_shapes=list(scratch) + extra,
        compiler_params=pltpu.CompilerParams(
            vmem_limit_bytes=56 << 20,
            **(dict(collective_id=number, has_side_effects=True) if hops or core else {}),
        ),
        cost_estimate=pl.CostEstimate(flops=flops, bytes_accessed=flops // 500, transcendentals=0),
    )(*args, *arrays)
    for hop, array in zip(hops, outs[len(out_shape) :]):
        hop.group.arrays[hop.kind] = array
    return outs[: len(out_shape)]


def self_attend_back(number, plan, qkv, grad, lse, width, begin, end):
    frames, pairs = qkv.shape[1], width // LANES
    at = lambda offset: pl.BlockSpec((None, frames, LANES), lambda m, i: (m, 0, offset + i))
    out = jax.ShapeDtypeStruct((2, frames, (end - begin) * LANES), bf16)
    return hosted(
        functools.partial(self_backward_kernel, 256),
        number,
        (2, end - begin),
        [qkv, qkv, qkv, grad, lse],
        [
            at(begin),
            at(pairs + begin),
            at(2 * pairs + begin),
            at(begin),
            pl.BlockSpec((None, None, 8, frames), lambda m, i: (m, begin + i, 0, 0)),
        ],
        [out] * 3,
        [at(0)] * 3,
        [pltpu.VMEM((frames, LANES), f32)] * 2,
        plan,
        16 * frames * frames * LANES * (end - begin),
    )


def half_spec(array, half):
    if array.ndim == 2:
        return pl.BlockSpec(array.shape, lambda *grid: (0, 0), pipeline_mode=pl.Buffered(1))
    return pl.BlockSpec(
        (None,) + array.shape[1:], lambda *grid: (half, 0, 0), pipeline_mode=pl.Buffered(1)
    )


def exchanged_grad(number, plan, xs, tiles, rows):
    depth = xs[0].shape[1]
    specs = [pl.BlockSpec(x.shape, lambda j, m: (0, 0), pipeline_mode=pl.Buffered(1)) for x in xs]
    args, halves = list(xs), []
    for _, arrays in tiles:
        halves.append([])
        for half in range(2):
            halves[-1].append(range(len(args), len(args) + len(arrays)))
            args += arrays
            specs += [half_spec(array, half) for array in arrays]
    tile = sum(array.shape[2] for array in tiles[0][1])
    count = len(tiles)
    steps = 2 * count
    longest = max(x.shape[0] for x in xs)
    shape = jax.ShapeDtypeStruct((2, Z, Y, rows, count * tile), bf16)
    hbm = pl.BlockSpec(memory_space=pl.ANY)

    def body(*refs):
        own_ref, there_ref = refs[len(args) : len(args) + 2]
        turned, own, other, own_sem, send_sem, recv_sem = refs[len(args) + 2 :]
        dp, mp = lax.axis_index("dp"), lax.axis_index("mp")
        core, across = dp % CORES, (dp // CORES) % Y
        j, m = pl.program_id(0), pl.program_id(1)
        step = 2 * j + m

        def place(step):
            column = (step // 2) * tile
            column = column if isinstance(column, int) else pl.multiple_of(column, LANES)
            every = slice(None)
            return ((step + mp) % 2, every, every, every, pl.ds(column, tile))

        def kept(step):
            slot = step % 2
            return pltpu.make_async_copy(own.at[slot], own_ref.at[place(step)], own_sem.at[slot])

        def sent(step):
            return pltpu.make_async_remote_copy(
                src_ref=other.at[step % 2],
                dst_ref=there_ref.at[place(step)],
                send_sem=send_sem.at[step],
                recv_sem=recv_sem.at[step],
                device_id=core_partner(),
                device_id_type=MESH,
            )

        @pl.when(step >= 2)
        def _():
            kept(step - 2).wait()
            sent(step - 2).wait_send()

        for k, (source, _) in enumerate(tiles):
            frames = xs[source].shape[0]

            if k == 0 or tiles[k - 1][0] != source:

                @pl.when((j == k) & (m == 0))
                def _(source=source, frames=frames):
                    turned[:, 0:frames] = refs[source][...].T

            for half in range(2):

                @pl.when((j == k) & (m == half))
                def _(k=k, half=half, frames=frames):
                    pieces = [refs[i][...] for i in halves[k][half]]
                    y = pieces[0] if len(pieces) == 1 else jnp.concatenate(pieces, axis=1)
                    for z in range(Z):
                        span = slice(z * Y * CORES * rows, (z + 1) * Y * CORES * rows)
                        part = dotf(turned[span, 0:frames], y, NN).astype(bf16)
                        for i in range(Y):
                            first = part[2 * i * rows : (2 * i + 1) * rows]
                            second = part[(2 * i + 1) * rows : (2 * i + 2) * rows]
                            own[m, z, (i + across) % 2] = jnp.where(core == 0, first, second)
                            other[m, z, (i + across) % 2] = jnp.where(core == 0, second, first)

        kept(step).start()
        sent(step).start()

        @pl.when(step == steps - 1)
        def _():
            for t in (steps - 2, steps - 1):
                kept(t).wait()
                sent(t).wait_send()
            for t in range(steps):
                sent(t).wait_recv()

    outs = hosted(
        body,
        number,
        (count, 2),
        args,
        specs,
        [shape, shape],
        [hbm, hbm],
        [
            pltpu.VMEM((depth, longest), bf16),
            pltpu.VMEM((2, Z, Y, rows, tile), bf16),
            pltpu.VMEM((2, Z, Y, rows, tile), bf16),
            pltpu.SemaphoreType.DMA((2,)),
            pltpu.SemaphoreType.DMA((steps,)),
            pltpu.SemaphoreType.DMA((steps,)),
        ],
        plan,
        4 * longest * depth * count * tile,
        core=True,
    )
    return Group(*outs)


def gather_kernel(parts, swaps, *refs):
    shard_ref, sent_refs = refs[0], refs[1 : 1 + swaps]
    whole_ref, got_refs = refs[1 + swaps], refs[2 + swaps : 2 + 2 * swaps]
    own_sem, swap_send, swap_recv, send_sem, recv_sem = refs[2 + 2 * swaps :]
    dp, x = lax.axis_index("dp"), lax.axis_index("mp")
    group = Y * CORES
    z, rest = dp // group, dp % group
    across = rest + CORES - 2 * CORES * (rest // CORES)
    rows, columns = shard_ref.shape
    x_peer, y_peer, core_peer = (dp, 1 - x), (z * group + across, x), core_partner()
    z_peers = [(((z + k) % Z) * group + rest, x) for k in range(1, Z)]
    cut = 5 * rows // 6
    low, high, every = pl.ds(0, cut), pl.ds(cut, rows - cut), slice(None)
    meet([x_peer, y_peer, core_peer] + z_peers)
    started = []

    def send(part, slot, source, at, peer):
        copy = pltpu.make_async_remote_copy(
            src_ref=source,
            dst_ref=whole_ref.at[at],
            send_sem=send_sem.at[part, slot],
            recv_sem=recv_sem.at[part, slot],
            device_id=peer,
            device_id_type=MESH,
        )
        copy.start()
        started.append(copy)
        return copy

    def pass_on(part, slot, at, peer):
        return send(part, slot, whole_ref.at[at], at, peer)

    def columns_of(part):
        begin, end = parts[part]
        return pl.ds(begin, end - begin)

    swapped = []
    for i in range(swaps):
        copy = pltpu.make_async_remote_copy(
            src_ref=sent_refs[i],
            dst_ref=got_refs[i],
            send_sem=swap_send.at[i],
            recv_sem=swap_recv.at[i],
            device_id=x_peer,
            device_id_type=MESH,
        )
        copy.start()
        swapped.append(copy)
    own = pltpu.make_async_copy(shard_ref, whole_ref.at[x, z, rest], own_sem)
    own.start()
    along, over, turned, late = {}, {}, {}, []
    for part in range(len(parts)):
        cut = columns_of(part)
        at = (x, z, rest, every, cut)
        along[part] = [
            send(part, k, shard_ref.at[every, cut], at, peer) for k, peer in enumerate(z_peers)
        ]
        late.append(send(part, 3, shard_ref.at[every, cut], at, core_peer))
    own.wait()

    def first(part):
        cut = columns_of(part)
        for copy in along[part]:
            copy.wait_recv()
        over[part] = [
            pass_on(part, 4, (x, every, rest, low, cut), x_peer),
            pass_on(part, 5, (x, every, rest, high, cut), y_peer),
        ]
        for k in range(1, Z):
            late.append(pass_on(part, 5 + k, (x, (z + k) % Z, rest, every, cut), core_peer))

    def second(part):
        cut = columns_of(part)
        for copy in over[part]:
            copy.wait_recv()
        turned[part] = [
            pass_on(part, 9, (0, every, rest, low, cut), y_peer),
            pass_on(part, 10, (x, every, rest, high, cut), x_peer),
            pass_on(part, 11, (1, every, rest, low, cut), y_peer),
            pass_on(part, 12, (x, every, across, high, cut), x_peer),
        ]
        late.append(pass_on(part, 13, (1 - x, every, rest, low, cut), core_peer))
        late.append(pass_on(part, 14, (x, every, across, high, cut), core_peer))

    def third(part):
        cut = columns_of(part)
        for copy in turned[part]:
            copy.wait_recv()
        late.append(pass_on(part, 15, (0, every, across, low, cut), core_peer))
        late.append(pass_on(part, 16, (1, every, across, low, cut), core_peer))
        late.append(pass_on(part, 17, (1 - x, every, rest, high, cut), core_peer))
        late.append(pass_on(part, 18, (1 - x, every, across, high, cut), core_peer))

    first(0)
    for part in range(len(parts)):
        second(part)
        if part + 1 < len(parts):
            first(part + 1)
        if part:
            third(part - 1)
    third(len(parts) - 1)
    for copy in late:
        copy.wait_recv()
    for copy in started:
        copy.wait_send()
    for copy in swapped:
        copy.wait()


def gather_now(number, shard, swaps):
    rows, columns = shard.shape
    tiles = columns // LANES
    cuts = [0, tiles // 3 * LANES, 2 * tiles // 3 * LANES, columns]
    parts = list(zip(cuts[:-1], cuts[1:]))
    hbm = pl.BlockSpec(memory_space=pl.ANY)
    outs = pl.pallas_call(
        functools.partial(gather_kernel, parts, len(swaps)),
        in_specs=[hbm] * (1 + len(swaps)),
        out_specs=(hbm,) * (1 + len(swaps)),
        out_shape=(jax.ShapeDtypeStruct((2, Z, Y * CORES, rows, columns), shard.dtype),)
        + tuple(jax.ShapeDtypeStruct(a.shape, a.dtype) for a in swaps),
        scratch_shapes=[
            pltpu.SemaphoreType.DMA(()),
            pltpu.SemaphoreType.DMA((len(swaps),)),
            pltpu.SemaphoreType.DMA((len(swaps),)),
            pltpu.SemaphoreType.DMA((len(parts), 19)),
            pltpu.SemaphoreType.DMA((len(parts), 19)),
        ],
        compiler_params=pltpu.CompilerParams(collective_id=number, has_side_effects=True),
        cost_estimate=pl.CostEstimate(flops=10**9, bytes_accessed=10**8, transcendentals=0),
    )(shard, *swaps)
    return outs[0], outs[1:]


def project_kernel(x_ref, w_ref, o_ref):
    step = x_ref.shape[0] // 4
    for i in range(4):
        rows = slice(i * step, (i + 1) * step)
        o_ref[rows, :] = dotf(x_ref[rows, :], w_ref[...], NN).astype(o_ref.dtype)


def project_both(x, whole, begin, width, tile=768):
    (frames, depth), first = x.shape, begin // tile
    return pl.pallas_call(
        project_kernel,
        grid=(2, width // tile),
        in_specs=[
            pl.BlockSpec((frames, depth), lambda m, j: (0, 0)),
            pl.BlockSpec((None, depth, tile), lambda m, j: (m, 0, first + j)),
        ],
        out_specs=pl.BlockSpec((None, frames, tile), lambda m, j: (m, 0, j)),
        out_shape=jax.ShapeDtypeStruct((2, frames, width), bf16),
        compiler_params=pltpu.CompilerParams(vmem_limit_bytes=40 << 20),
        cost_estimate=pl.CostEstimate(
            flops=4 * frames * depth * width,
            bytes_accessed=4 * (frames + depth) * width,
            transcendentals=0,
        ),
    )(x, whole)


def unproject_both(number, plan, pieces, whole, begin, width, base=None):
    frames, depth, tile = pieces[0][0].shape[-2], whole.shape[1], 512 if width < 1024 else 256
    first, direct = begin // width, len(pieces) == 2
    bases = [] if base is None else [base]

    def body(*refs):
        n = len(pieces)
        w_refs, refs_left = refs[n : n + 2], refs[n + 2 :]
        o_ref = refs_left[len(bases)]

        if not direct:
            joint = refs_left[-1]

            @pl.when(pl.program_id(0) == 0)
            def _():
                for ref, (_, half, column) in zip(refs, pieces):
                    joint[half, :, column : column + ref.shape[1]] = ref[...]

        for i in range(4):
            rows = slice(i * frames // 4, (i + 1) * frames // 4)
            ys = [refs[m][rows, :] if direct else joint[m, rows, :] for m in range(2)]
            total = dotf(ys[0], w_refs[0][...], NT) + dotf(ys[1], w_refs[1][...], NT)
            o_ref[rows, :] = refs_left[0][rows, :] + total if bases else total

    weights = lambda m: pl.BlockSpec((None, tile, width), lambda j: (m, j, first))
    across = pl.BlockSpec((frames, tile), lambda j: (0, j))
    return hosted(
        body,
        number,
        (depth // tile,),
        [p[0] for p in pieces] + [whole, whole] + bases,
        [half_spec(array, half) for array, half, _ in pieces] + [weights(0), weights(1)] + [across] * len(bases),
        [jax.ShapeDtypeStruct((frames, depth), f32)],
        [across],
        [] if direct else [pltpu.VMEM((2, frames, width), bf16)],
        plan,
        4 * frames * depth * width,
    )[0]


def halves_of(array):
    return [(array, 0, 0), (array, 1, 0)]


def norm_back_last(number, plan, after, stream, grad, gain, passed, others):
    frames, depth = stream.shape
    steps = 8
    size, half = frames // steps, steps // 2

    def swapped(got_ref, sent, send_sem, recv_sem, t):
        return pltpu.make_async_remote_copy(
            src_ref=sent.at[t],
            dst_ref=got_ref.at[t],
            send_sem=send_sem.at[t],
            recv_sem=recv_sem.at[t],
            device_id=(lax.axis_index("dp"), 1 - lax.axis_index("mp")),
            device_id_type=MESH,
        )

    def body(stream_ref, grad_ref, gain_ref, passed_ref, others_ref, o_ref, got_ref, total_ref, *scratch):
        sent, send_sem, recv_sem, sums = scratch[:4]
        step = pl.program_id(0)
        rows, inverse = norm_rows_of(stream_ref[...])
        grads = grad_ref[...]
        scaled = grads * gain_ref[...]
        products = jnp.mean(scaled * rows, axis=-1, keepdims=True)
        back = inverse * (scaled - jnp.mean(scaled, axis=-1, keepdims=True) - rows * products)
        total = passed_ref[...] + back
        o_ref[...] = total

        @pl.when(step == 0)
        def _():
            sums[0] = others_ref[...]

        sums[0, 0:1, :] += jnp.sum(grads * rows, axis=0, keepdims=True)
        sums[0, 1:2, :] += jnp.sum(grads, axis=0, keepdims=True)

        @pl.when(step // half == 1 - lax.axis_index("mp"))
        def _():
            sent[step % half] = total.astype(bf16)
            swapped(got_ref, sent, send_sem, recv_sem, step % half).start()

    def closing(stream_ref, grad_ref, gain_ref, passed_ref, others_ref, o_ref, got_ref, total_ref, *scratch):
        sent, swap_send, swap_recv, sums, got, send_sem, recv_sem = scratch
        dp, mp = lax.axis_index("dp"), lax.axis_index("mp")
        group = Y * CORES
        z, rest = dp // group, dp % group
        partners = [core_partner(), (dp + CORES - 2 * CORES * ((dp // CORES) % Y), mp)]
        partners.append(((z + 1 - 2 * (z % 2)) * group + rest, mp))
        partners.append((((z + 2) % Z) * group + rest, mp))
        partners.append((dp, 1 - mp))
        for i, partner in enumerate(partners):
            copy = pltpu.make_async_remote_copy(
                src_ref=sums.at[i],
                dst_ref=got.at[i],
                send_sem=send_sem.at[i],
                recv_sem=recv_sem.at[i],
                device_id=partner,
                device_id_type=MESH,
            )
            copy.start()
            copy.wait()
            sums[i + 1] = sums[i] + got[i]
        total_ref[...] = sums[5]
        for t in range(half):
            swapped(got_ref, sent, swap_send, swap_recv, t).wait()

    block = pl.BlockSpec((size, depth), lambda i: (i, 0))
    hbm = pl.BlockSpec(memory_space=pl.ANY)
    sums = pl.BlockSpec((8, depth), lambda i: (0, 0))
    total, got, sums = hosted(
        body,
        number,
        (steps,),
        [stream, grad, gain, passed, others],
        [block, block, pl.BlockSpec((1, depth), lambda i: (0, 0)), block, sums],
        [
            jax.ShapeDtypeStruct((frames, depth), f32),
            jax.ShapeDtypeStruct((half, size, depth), bf16),
            jax.ShapeDtypeStruct((8, depth), f32),
        ],
        [block, hbm, sums],
        [
            pltpu.VMEM((half, size, depth), bf16),
            pltpu.SemaphoreType.DMA((half,)),
            pltpu.SemaphoreType.DMA((half,)),
            pltpu.VMEM((6, 8, depth), f32),
            pltpu.VMEM((5, 8, depth), f32),
            pltpu.SemaphoreType.DMA((5,)),
            pltpu.SemaphoreType.DMA((5,)),
        ],
        plan,
        10**9,
        core=True,
        after=after,
        closing=closing,
    )
    return total, got.reshape(frames // 2, depth), sums


def pair_rows(array, masks):
    zero = jnp.zeros((), bf16)
    return jnp.concatenate([jnp.where(mask, array, zero) for mask in masks], axis=0)


def cross_weights_of(q, keys, masks):
    scores = dotf(q * jnp.asarray(0.125, bf16), keys, NT)
    tops = [jnp.max(jnp.where(mask, scores, MASKED), axis=1, keepdims=True) for mask in masks]
    exponents = jnp.exp(scores - jnp.where(masks[0], tops[0], tops[1]))
    sums = [jnp.sum(jnp.where(mask, exponents, 0.0), axis=1, keepdims=True) for mask in masks]
    return exponents * jnp.where(masks[0], 1.0 / sums[0], 1.0 / sums[1]), tops


def cross_forward_kernel(q_ref, k_ref, v_ref, o_ref, peak_ref):
    masks = head_masks()
    weights, tops = cross_weights_of(q_ref[...], pair_rows(k_ref[...], masks), masks)
    o_ref[...] = dotf(weights.astype(bf16), pair_rows(v_ref[...], masks), NN).astype(bf16)
    for h in range(2):
        peak_ref[h : h + 1, :] = jnp.broadcast_to(
            jnp.max(tops[h], axis=0, keepdims=True), (1, LANES)
        )


def cross_specs(frames, text, pairs):
    at = lambda n, offset: pl.BlockSpec((None, n, LANES), lambda m, i: (m, 0, offset + i))
    return at(frames, 0), at(text, 0), at(text, pairs)


def cross_attend(q, kv, width):
    frames, text, pairs = q.shape[1], kv.shape[1], width // LANES
    long, keys, values = cross_specs(frames, text, pairs)
    return pl.pallas_call(
        cross_forward_kernel,
        grid=(2, pairs),
        out_shape=(
            jax.ShapeDtypeStruct((2, frames, width), bf16),
            jax.ShapeDtypeStruct((2, pairs, 8, LANES), f32),
        ),
        in_specs=[long, keys, values],
        out_specs=(long, pl.BlockSpec((None, None, 8, LANES), lambda m, i: (m, i, 0, 0))),
        compiler_params=pltpu.CompilerParams(vmem_limit_bytes=32 << 20),
        cost_estimate=pl.CostEstimate(
            flops=32 * frames * LANES * width, bytes_accessed=8 * frames * width, transcendentals=0
        ),
    )(q, kv, kv)


def cross_backward_kernel(q_ref, k_ref, v_ref, g_ref, dq_ref, dk_ref, dv_ref):
    masks = head_masks()
    text = k_ref.shape[0]
    keys, values = pair_rows(k_ref[...], masks), pair_rows(v_ref[...], masks)
    q, g = q_ref[...], g_ref[...]
    weights, _ = cross_weights_of(q, keys, masks)
    grads = dotf(g, values, NT)
    products = weights * grads
    centers = [jnp.sum(jnp.where(mask, products, 0.0), axis=1, keepdims=True) for mask in masks]
    ds = (weights * (grads - jnp.where(masks[0], centers[0], centers[1]))).astype(bf16)
    dq_ref[...] = (dotf(ds, keys, NN) * 0.125).astype(bf16)
    dk = dotf(ds, q, TN) * 0.125
    dv = dotf(weights.astype(bf16), g, TN)
    dk_ref[...] = jnp.where(masks[0], dk[:text], dk[text:]).astype(bf16)
    dv_ref[...] = jnp.where(masks[0], dv[:text], dv[text:]).astype(bf16)


def cross_attend_back(q, kv, grad, width):
    frames, text, pairs = q.shape[1], kv.shape[1], width // LANES
    long, keys, values = cross_specs(frames, text, pairs)
    return pl.pallas_call(
        cross_backward_kernel,
        grid=(2, pairs),
        out_shape=(
            jax.ShapeDtypeStruct((2, frames, width), bf16),
            jax.ShapeDtypeStruct((2, text, width), bf16),
            jax.ShapeDtypeStruct((2, text, width), bf16),
        ),
        in_specs=[long, keys, values, long],
        out_specs=(long, keys, keys),
        compiler_params=pltpu.CompilerParams(vmem_limit_bytes=32 << 20),
        cost_estimate=pl.CostEstimate(
            flops=64 * frames * LANES * width, bytes_accessed=12 * frames * width, transcendentals=0
        ),
    )(q, kv, kv, grad)


def weight_grad_whole_kernel(x_ref, y0_ref, y1_ref, *refs):
    half, tile = pl.program_id(0), pl.program_id(1)
    o_ref, turned = refs[-2:]

    @pl.when((half == 0) & (tile == 0))
    def _():
        turned[...] = x_ref[...].T

    for m, y_ref in enumerate((y0_ref, y1_ref)):

        @pl.when(half == m)
        def _(y_ref=y_ref):
            step = o_ref.shape[0] // 4
            for i in range(4):
                rows = slice(i * step, (i + 1) * step)
                o_ref[rows, :] = dotf(turned[rows, :], y_ref[...], NN).astype(bf16)


def weight_grad_whole(x, ys, tile, columns, begin, into=None):
    frames, depth = x.shape
    width = ys[0].shape[1]
    tiles, first = width // tile, begin // tile
    given = [] if into is None else [into]
    return pl.pallas_call(
        weight_grad_whole_kernel,
        grid=(2, tiles),
        in_specs=[
            pl.BlockSpec((frames, depth), lambda m, j: (0, 0)),
            pl.BlockSpec((frames, tile), lambda m, j: (0, jnp.where(m == 0, j, tiles - 1))),
            pl.BlockSpec((frames, tile), lambda m, j: (0, jnp.where(m == 0, 0, j))),
        ]
        + [pl.BlockSpec(memory_space=pl.ANY)] * len(given),
        out_specs=pl.BlockSpec((None, depth, tile), lambda m, j: (m, 0, first + j)),
        scratch_shapes=[pltpu.VMEM((depth, frames), bf16)],
        out_shape=jax.ShapeDtypeStruct((2, depth, columns), bf16),
        input_output_aliases={3: 0} if given else {},
        compiler_params=pltpu.CompilerParams(vmem_limit_bytes=40 << 20),
        cost_estimate=pl.CostEstimate(
            flops=4 * frames * depth * width,
            bytes_accessed=4 * (depth + frames) * width + 2 * frames * depth,
            transcendentals=0,
        ),
    )(x, *ys, *given)


def swap(values, axis_name, pairs):
    return lax.ppermute(values, axis_name, pairs)


MP_PAIRS = [(0, 1), (1, 0)]
CORE_PAIRS = [(i, i ^ 1) for i in range(Z * Y * CORES)]


def over_all(value, join):
    value = join(value, swap(value, "dp", CORE_PAIRS))
    value = join(value, swap(value, "mp", MP_PAIRS))
    for bit in (2, 4, 8):
        pairs = [(i, i ^ bit) for i in range(Z * Y * CORES)]
        value = join(value, swap(value, "dp", pairs))
    return value


def joined(arrays):
    return jnp.concatenate(arrays, axis=1)


def norm_rows_of(stream):
    center = stream - jnp.mean(stream, axis=-1, keepdims=True)
    inverse = lax.rsqrt(jnp.mean(center * center, axis=-1, keepdims=True) + EPSILON)
    return center * inverse, inverse


def norm_back(stream, gain, grad):
    rows, inverse = norm_rows_of(stream)
    scaled = grad * gain
    back = inverse * (
        scaled
        - jnp.mean(scaled, axis=-1, keepdims=True)
        - rows * jnp.mean(scaled * rows, axis=-1, keepdims=True)
    )
    return back, jnp.sum(grad * rows, axis=0), jnp.sum(grad, axis=0)


def clip_per_device(
    inputs,
    text_states,
    cotangent,
    norm_params,
    self_query_key,
    self_value,
    self_output,
    cross_query,
    cross_key_value,
    cross_output,
    hidden_in,
    hidden_out,
):
    dp, mp = lax.axis_index("dp"), lax.axis_index("mp")
    z = dp // (Y * CORES)
    rows, width = self_value.shape
    both = range(2)

    def shard_of(pieces):
        return jnp.concatenate([rounded(p).reshape(rows, -1) for p in pieces], axis=1)

    def gathered(shard):
        whole = lax.all_gather(shard, ("mp", "dp"), axis=0, tiled=True)
        return whole.reshape(2, D, shard.shape[1])

    def other_half(array):
        return rounded(lax.dynamic_index_in_dim(array, 1 - mp, 0, keepdims=False))

    def whole_clip(array, got, kind):
        own = lax.dynamic_index_in_dim(array, mp, 0, keepdims=False).astype(kind)
        got = got.astype(kind)
        return jnp.where(
            mp == 0, jnp.concatenate([own, got], axis=0), jnp.concatenate([got, own], axis=0)
        )

    def other_frames(array):
        count = array.shape[0] // 2
        return rounded(lax.dynamic_slice_in_dim(array, (1 - mp) * count, count, 0))

    def own_frames(array, got):
        count = array.shape[0] // 2
        own = lax.dynamic_slice_in_dim(array, mp * count, count, 0)
        got = got.astype(f32)
        return jnp.where(mp == 0, jnp.stack([own, got]), jnp.stack([got, own]))

    norms_padded = jnp.pad(norm_params, ((0, 0), (0, LANES - norm_params.shape[1])))
    hidden = hidden_in.shape[1]
    self_shard = shard_of([self_query_key, self_value, self_output, norms_padded])
    cross_shard = shard_of([cross_query, cross_key_value, cross_output, hidden_in])
    sent = (other_half(inputs), other_half(text_states))
    self_shard, cross_shard, sent = lax.optimization_barrier((self_shard, cross_shard, sent))
    cross_all = gathered(cross_shard)
    self_all, (got_inputs, got_text) = gather_now(16, self_shard, sent)
    self_all = self_all.reshape(2, D, self_shard.shape[1])
    out_all = gathered(rounded(hidden_out))
    norms = self_all[0, :, 4 * width : 4 * width + norm_params.shape[1]].astype(f32).T
    self_o = [self_all[m, :, 3 * width : 4 * width] for m in both]
    cross_q = [cross_all[m, :, :width] for m in both]
    cross_kv = [cross_all[m, :, width : 3 * width] for m in both]
    cross_o = [cross_all[m, :, 3 * width : 4 * width] for m in both]
    in_w = [cross_all[m, :, 4 * width :] for m in both]

    def times(array, matrix):
        return dotf(array, matrix, NN)

    def times_turned(arrays, matrices):
        return dotf(arrays[0], matrices[0], NT) + dotf(arrays[1], matrices[1], NT)

    stream = whole_clip(inputs, got_inputs, f32)
    states = whole_clip(text_states, got_text, bf16)
    normed_self = rounded(norm_rows_of(stream)[0] * norms[0] + norms[1])
    qkv = project_both(normed_self, self_all, 0, 3 * width)
    qkv, cotangent = lax.optimization_barrier((qkv, cotangent))
    upstream = whole_clip(cotangent, swap(other_half(cotangent), "mp", MP_PAIRS), f32)
    mixed_self, lse, self_peaks = self_attend(qkv, width)
    after_self = unproject_both(0, [], halves_of(mixed_self), self_all, 3 * width, width, stream)
    normed_cross = rounded(norm_rows_of(after_self)[0] * norms[2] + norms[3])
    queries = project_both(normed_cross, cross_all, 0, width)
    text_kv = jnp.stack([rounded(times(states, cross_kv[m])) for m in both])
    mixed_cross, cross_peaks = cross_attend(queries, text_kv, width)
    after_cross = unproject_both(0, [], halves_of(mixed_cross), cross_all, 3 * width, width, after_self)
    normed_hidden = rounded(norm_rows_of(after_cross)[0] * norms[4] + norms[5])
    upward = [times(normed_hidden, in_w[m]) for m in both]
    activated, pulls = zip(*[jax.vjp(gelu_exact, up) for up in upward])
    activated = [rounded(a) for a in activated]

    branch = rounded(upstream)
    hidden_grad = weight_grad_whole(branch, activated, 512, 2 * hidden, hidden)
    def peaks_of(peaks):
        return peaks[:, :, :2, 0].reshape(2, -1)

    tops = over_all(jnp.stack([peaks_of(self_peaks), peaks_of(cross_peaks)]), jnp.maximum)
    tops = lax.dynamic_index_in_dim(tops, mp, 1, keepdims=False)
    factors = CLIP_LIMIT / jnp.maximum(tops, CLIP_LIMIT)
    root_scales = jnp.repeat(jnp.sqrt(factors), D // HEADS, axis=1)
    clipped = (
        self_query_key * root_scales[0][None, None, :],
        cross_query * root_scales[1][None, :],
        cross_key_value[:, 0] * root_scales[1][None, :],
    )
    out_all, hidden_grad, clipped = lax.optimization_barrier((out_all, hidden_grad, clipped))
    grad_up = [rounded(pulls[m](times(branch, out_all[m]))[0]) for m in both]
    hidden_grad = weight_grad_whole(normed_hidden, grad_up, 512, 2 * hidden, 0, hidden_grad)
    grad_up, hidden_grad = lax.optimization_barrier((grad_up, hidden_grad))
    shard_hidden = lax.psum_scatter(
        hidden_grad.reshape(2 * D, 2 * hidden), ("mp", "dp"), scatter_dimension=0, tiled=True
    ).astype(f32)
    grad_normed = unproject_both(
        0, [], [(a, m, 0) for m, a in enumerate(grad_up)], cross_all, 4 * width, hidden
    )
    back, gain_three, bias_three = norm_back(after_cross, norms[4], grad_normed)
    grad_stream = upstream + back

    branch_cross = rounded(grad_stream)
    grad_mixed = project_both(branch_cross, cross_all, 3 * width, width)
    dq, dk, dv = cross_attend_back(queries, text_kv, grad_mixed, width)
    grad_normed = unproject_both(0, [], halves_of(dq), cross_all, 0, width)
    back, gain_two, bias_two = norm_back(after_self, norms[2], grad_normed)
    dkv = [joined([dk[m], dv[m]]) for m in both]
    grad_text = times_turned(dkv, cross_kv)
    swap_text = Holder(other_frames(grad_text))
    grad_stream = grad_stream + back
    branch_self = rounded(grad_stream)
    group_pair = exchanged_grad(1, [], [normed_cross, states], [(0, [dq]), (1, [dk]), (1, [dv])], rows)
    group_out = exchanged_grad(
        2, [], [branch_cross, branch_self], [(0, [mixed_cross]), (1, [mixed_self])], rows
    )
    grad_mixed = project_both(branch_self, self_all, 3 * width, width)
    pairs = width // LANES
    cut = 2 * pairs // 3
    early = self_attend_back(
        3, [("x1", group_pair), ("y1", group_pair)], qkv, grad_mixed, lse, width, 0, cut
    )
    activated, early = lax.optimization_barrier((activated, early))
    output = unproject_both(
        4, [("x1", group_out), ("y1", group_out)], [(a, m, 0) for m, a in enumerate(activated)], out_all, 0, hidden, after_cross
    )
    swap_output = Holder(other_frames(output))
    group_early = exchanged_grad(
        5, [("x0", swap_text), ("x2", group_pair), ("y2", group_pair)], [normed_self], [(0, list(early))], rows
    )
    late = self_attend_back(
        6,
        [
            ("x2", group_out),
            ("y2", group_out),
            ("za", group_pair),
            ("zb", group_pair),
            ("x0", swap_output),
        ],
        qkv,
        grad_mixed,
        lse,
        width,
        cut,
        pairs,
    )
    group_late = exchanged_grad(
        7, [("x1", group_early), ("y1", group_early)], [normed_self], [(0, list(late))], rows
    )
    pieces = []
    for half in both:
        for part, arrays in enumerate((early, late)):
            pieces += [(a, half, i * width + part * cut * LANES) for i, a in enumerate(arrays)]
    grad_normed = unproject_both(
        8,
        [
            ("x1", group_late),
            ("y1", group_late),
            ("x2", group_early),
            ("y2", group_early),
            ("za", group_out),
            ("zb", group_out),
        ],
        pieces,
        self_all,
        0,
        3 * width,
    )
    grad_inputs, got_inputs, norm_grads = norm_back_last(
        9,
        [
            ("x2", group_late),
            ("y2", group_late),
            ("za", group_early),
            ("zb", group_early),
            ("total", group_pair),
            ("total", group_out),
        ],
        [("za", group_late), ("zb", group_late), ("total", group_early)],
        stream,
        grad_normed,
        norms[0:1],
        grad_stream,
        jnp.pad(jnp.stack([gain_two, bias_two, gain_three, bias_three]), ((2, 2), (0, 0))),
    )
    norm_grads = norm_grads[:6]
    grad_inputs = own_frames(grad_inputs, got_inputs)
    grad_text = own_frames(grad_text, swap_text.got())
    output = own_frames(output, swap_output.got())
    shard_pair, shard_outs = group_pair.arrays["total"], group_out.arrays["total"]
    halves = [group_early.arrays["total"], group_late.result(z)]
    sizes = [cut * LANES, width - cut * LANES]
    shard_self = [
        joined([h[:, i * n : (i + 1) * n] for h, n in zip(halves, sizes)]) for i in range(3)
    ]

    shard_norms = lax.dynamic_slice_in_dim(norm_grads, dp * rows, rows, 1).T

    return (
        output,
        grad_inputs,
        grad_text,
        shard_norms,
        jnp.stack(shard_self[:2], axis=1),
        shard_self[2],
        shard_outs[:, width:],
        shard_pair[:, :width],
        shard_pair[:, width:].reshape(rows, 2, width),
        shard_outs[:, :width],
        shard_hidden[:, :hidden],
        shard_hidden[:, hidden:],
        factors,
        *clipped,
    )


def solution(mesh):
    in_specs = (
        P("dp", "mp", None),
        P("dp", "mp", None),
        P("dp", "mp", None),
        P("dp", None),
        P("dp", None, "mp"),
        P("dp", "mp"),
        P("dp", "mp"),
        P("dp", "mp"),
        P("dp", None, "mp"),
        P("dp", "mp"),
        P("dp", "mp"),
        P("dp", "mp"),
    )
    out_specs = (
        P("dp", "mp", None),
        P("dp", "mp", None),
        P("dp", "mp", None),
        P("dp", None),
        P("dp", None, "mp"),
        P("dp", "mp"),
        P("dp", "mp"),
        P("dp", "mp"),
        P("dp", None, "mp"),
        P("dp", "mp"),
        P("dp", "mp"),
        P("dp", "mp"),
        P(None, "mp"),
        P("dp", None, "mp"),
        P("dp", "mp"),
        P("dp", "mp"),
    )
    by_clip = mesh.shape["mp"] == 2 and mesh.shape["dp"] == 16
    return jax.shard_map(
        clip_per_device if by_clip else per_device, mesh=mesh, in_specs=in_specs, out_specs=out_specs, check_vma=False
    )
```

```python
import functools
import math

import jax
import jax.numpy as jnp
from jax import lax
from jax.experimental import pallas as pl
from jax.experimental.pallas import tpu as pltpu
from jax.sharding import PartitionSpec as P

D = 1536
HEADS = 24


EPSILON = 1e-05
CLIP_LIMIT = 7.0
MASKED = -1e30


def layer_norm(stream_rows, gain_row, bias_row):
    center = stream_rows - jnp.mean(stream_rows, axis=-1, keepdims=True)
    spread = jnp.mean(center * center, axis=-1, keepdims=True)
    return center * lax.rsqrt(spread + EPSILON) * gain_row + bias_row


def gelu_exact(values):
    return 0.5 * values * (1.0 + lax.erf(values * 2.0 ** (-0.5)))


def rounded(values):
    return values.astype(jnp.bfloat16)


def project(array, matrix):
    return jnp.einsum("cld,de->cle", array, matrix, preferred_element_type=jnp.float32)


def unproject(array, matrix):
    return jnp.einsum("cle,de->cld", array, matrix, preferred_element_type=jnp.float32)


def outer_sum(left, right):
    return jnp.einsum("cld,cle->de", left, right, preferred_element_type=jnp.float32)


def widen(values):
    return lax.all_gather(values, "mp", axis=1, tiled=True)


def settle(partial_sum):
    return lax.psum_scatter(
        partial_sum.astype(jnp.bfloat16), "mp", scatter_dimension=1, tiled=True
    ).astype(jnp.float32)


def widen_grad(values):
    return lax.all_gather(values, "mp", axis=1, tiled=True)


def settle_grad(partial_sum):
    return lax.psum_scatter(
        partial_sum.astype(jnp.bfloat16), "mp", scatter_dimension=1, tiled=True
    ).astype(jnp.float32)


def self_forward(queries, keys_all, values_all):
    frame_count, head_count, head_width = (queries.shape[1], queries.shape[2], queries.shape[3])
    block_rows = min(512, frame_count)
    block_count = frame_count // block_rows
    scaling = head_width ** (-0.5)
    row_ids = jnp.arange(block_rows)
    col_ids = jnp.arange(frame_count)

    def per_clip(triple):
        clip_queries, clip_keys, clip_values = triple

        def per_block(block_index):
            offset = block_index * block_rows
            block_queries = lax.dynamic_slice_in_dim(clip_queries, offset, block_rows, 0)
            scores = (
                jnp.einsum(
                    "qhe,khe->hqk", block_queries, clip_keys, preferred_element_type=jnp.float32
                )
                * scaling
            )
            allowed = col_ids[None, :] <= (offset + row_ids)[:, None]
            scores = jnp.where(allowed[None], scores, MASKED)
            highest = jnp.max(scores, axis=2, keepdims=True)
            exponents = jnp.exp(scores - highest)
            row_sums = jnp.sum(exponents, axis=2, keepdims=True)
            mixed = jnp.einsum(
                "hqk,khe->qhe",
                rounded(exponents / row_sums),
                clip_values,
                preferred_element_type=jnp.float32,
            )
            return (
                mixed,
                (highest + jnp.log(row_sums))[:, :, 0],
                jnp.max(highest[:, :, 0], axis=1),
            )

        mixed, log_sums, block_peaks = lax.map(per_block, jnp.arange(block_count))
        return (
            mixed.reshape(frame_count, head_count, head_width),
            log_sums,
            jnp.max(block_peaks, axis=0),
        )

    mixed, log_sums, clip_peaks = lax.map(per_clip, (queries, keys_all, values_all))
    return (mixed, log_sums, jnp.max(clip_peaks, axis=0))


def self_backward(queries, keys_all, values_all, log_sums, grad_mixed):
    frame_count, head_count, head_width = (queries.shape[1], queries.shape[2], queries.shape[3])
    block_rows = min(512, frame_count)
    block_count = frame_count // block_rows
    scaling = head_width ** (-0.5)
    row_ids = jnp.arange(block_rows)
    col_ids = jnp.arange(frame_count)

    def per_clip(bundle):
        clip_queries, clip_keys, clip_values, clip_logs, clip_grads = bundle

        def per_block(carried, block_index):
            grad_keys, grad_values = carried
            offset = block_index * block_rows
            block_queries = lax.dynamic_slice_in_dim(clip_queries, offset, block_rows, 0)
            block_grads = lax.dynamic_slice_in_dim(clip_grads, offset, block_rows, 0)
            scores = (
                jnp.einsum(
                    "qhe,khe->hqk", block_queries, clip_keys, preferred_element_type=jnp.float32
                )
                * scaling
            )
            allowed = col_ids[None, :] <= (offset + row_ids)[:, None]
            scores = jnp.where(allowed[None], scores, MASKED)
            weights = jnp.exp(scores - clip_logs[block_index][:, :, None])
            grad_values = grad_values + jnp.einsum(
                "hqk,qhe->khe", rounded(weights), block_grads, preferred_element_type=jnp.float32
            )
            grad_weights = jnp.einsum(
                "qhe,khe->hqk", block_grads, clip_values, preferred_element_type=jnp.float32
            )
            centered = grad_weights - jnp.sum(weights * grad_weights, axis=2, keepdims=True)
            grad_scores = rounded(weights * centered)
            grad_queries = (
                jnp.einsum(
                    "hqk,khe->qhe", grad_scores, clip_keys, preferred_element_type=jnp.float32
                )
                * scaling
            )
            grad_keys = (
                grad_keys
                + jnp.einsum(
                    "hqk,qhe->khe", grad_scores, block_queries, preferred_element_type=jnp.float32
                )
                * scaling
            )
            return ((grad_keys, grad_values), grad_queries)

        zero_keys = jnp.zeros(clip_keys.shape, jnp.float32)
        (grad_keys, grad_values), grad_queries = lax.scan(
            per_block, (zero_keys, zero_keys), jnp.arange(block_count)
        )
        return (grad_queries.reshape(frame_count, head_count, head_width), grad_keys, grad_values)

    return lax.map(per_clip, (queries, keys_all, values_all, log_sums, grad_mixed))


def cross_forward(queries, keys_all, values_all):
    scaling = queries.shape[3] ** (-0.5)
    scores = (
        jnp.einsum("clhe,cshe->chls", queries, keys_all, preferred_element_type=jnp.float32)
        * scaling
    )
    highest = jnp.max(scores, axis=3, keepdims=True)
    exponents = jnp.exp(scores - highest)
    weights = exponents / jnp.sum(exponents, axis=3, keepdims=True)
    mixed = jnp.einsum(
        "chls,cshe->clhe", rounded(weights), values_all, preferred_element_type=jnp.float32
    )
    return (mixed, weights, jnp.max(highest, axis=(0, 2, 3)))


def cross_backward(queries, keys_all, values_all, weights, grad_mixed):
    scaling = queries.shape[3] ** (-0.5)
    grad_values = jnp.einsum(
        "chls,clhe->cshe", rounded(weights), grad_mixed, preferred_element_type=jnp.float32
    )
    grad_weights = jnp.einsum(
        "clhe,cshe->chls", grad_mixed, values_all, preferred_element_type=jnp.float32
    )
    centered = grad_weights - jnp.sum(weights * grad_weights, axis=3, keepdims=True)
    grad_scores = rounded(weights * centered)
    grad_queries = (
        jnp.einsum("chls,cshe->clhe", grad_scores, keys_all, preferred_element_type=jnp.float32)
        * scaling
    )
    grad_keys = (
        jnp.einsum("chls,clhe->cshe", grad_scores, queries, preferred_element_type=jnp.float32)
        * scaling
    )
    return (grad_queries, grad_keys, grad_values)


def per_device(
    inputs,
    text_states,
    cotangent,
    norm_params,
    self_query_key,
    self_value,
    self_output,
    cross_query,
    cross_key_value,
    cross_output,
    hidden_in,
    hidden_out,
):
    (
        full_norms,
        full_query_key,
        full_value,
        full_output,
        full_cross_query,
        full_cross_pair,
        full_cross_output,
        full_hidden_in,
        full_hidden_out,
    ) = (
        lax.all_gather(rounded(norm_params), "dp", axis=0, tiled=True),
        lax.all_gather(rounded(self_query_key), "dp", axis=0, tiled=True),
        lax.all_gather(rounded(self_value), "dp", axis=0, tiled=True),
        lax.all_gather(rounded(self_output), "dp", axis=0, tiled=True),
        lax.all_gather(rounded(cross_query), "dp", axis=0, tiled=True),
        lax.all_gather(rounded(cross_key_value), "dp", axis=0, tiled=True),
        lax.all_gather(rounded(cross_output), "dp", axis=0, tiled=True),
        lax.all_gather(rounded(hidden_in), "dp", axis=0, tiled=True),
        lax.all_gather(rounded(hidden_out), "dp", axis=0, tiled=True),
    )
    norm_rows = full_norms.astype(jnp.float32)
    head_width = D // HEADS
    head_count = full_value.shape[1] // head_width

    def split_heads(array):
        return array.reshape(array.shape[0], array.shape[1], head_count, head_width)

    def merge_heads(array):
        return array.reshape(array.shape[0], array.shape[1], head_count * head_width)

    normed, pull_self = jax.vjp(layer_norm, inputs, norm_rows[:, 0], norm_rows[:, 1])
    normed_self = widen(rounded(normed))
    query_key_rows = jnp.einsum(
        "cld,dte->clte", normed_self, full_query_key, preferred_element_type=jnp.float32
    )
    queries = rounded(query_key_rows[:, :, 0])
    self_keys = rounded(query_key_rows[:, :, 1])
    values = rounded(project(normed_self, full_value))
    mixed, log_sums, self_peaks = self_forward(
        split_heads(queries), split_heads(self_keys), split_heads(values)
    )
    mixed_self = rounded(merge_heads(mixed))
    after_self = inputs + settle(unproject(mixed_self, full_output))
    normed, pull_cross = jax.vjp(layer_norm, after_self, norm_rows[:, 2], norm_rows[:, 3])
    normed_cross = widen(rounded(normed))
    cross_queries = rounded(project(normed_cross, full_cross_query))
    states = lax.all_gather(rounded(text_states), "mp", axis=1, tiled=True)
    key_value_rows = jnp.einsum(
        "csd,dte->cste", states, full_cross_pair, preferred_element_type=jnp.float32
    )
    cross_keys = rounded(key_value_rows[:, :, 0])
    cross_values = rounded(key_value_rows[:, :, 1])
    attended, cross_weights, cross_peaks = cross_forward(
        split_heads(cross_queries), split_heads(cross_keys), split_heads(cross_values)
    )
    mixed_cross = rounded(merge_heads(attended))
    after_cross = after_self + settle(unproject(mixed_cross, full_cross_output))
    normed, pull_hidden = jax.vjp(layer_norm, after_cross, norm_rows[:, 4], norm_rows[:, 5])
    normed_hidden = widen(rounded(normed))
    upward = project(normed_hidden, full_hidden_in)
    activated, pull_gelu = jax.vjp(gelu_exact, upward)
    activated = rounded(activated)
    output = after_cross + settle(unproject(activated, full_hidden_out))
    self_top, cross_top = lax.pmax((self_peaks, cross_peaks), "dp")
    grad_branch = widen_grad(rounded(cotangent))
    grad_hidden_out = outer_sum(grad_branch, activated)
    grad_upward = rounded(pull_gelu(project(grad_branch, full_hidden_out))[0])
    grad_hidden_in = outer_sum(normed_hidden, grad_upward)
    grad_normed = settle_grad(unproject(grad_upward, full_hidden_in))
    back_stream, grad_gain_three, grad_bias_three = pull_hidden(grad_normed)
    grad_stream = cotangent + back_stream
    grad_branch = widen_grad(rounded(grad_stream))
    grad_cross_output = outer_sum(grad_branch, mixed_cross)
    grad_attended = rounded(project(grad_branch, full_cross_output))
    grad_queries, grad_keys, grad_values = cross_backward(
        split_heads(cross_queries),
        split_heads(cross_keys),
        split_heads(cross_values),
        cross_weights,
        split_heads(grad_attended),
    )
    grad_queries = rounded(merge_heads(grad_queries))
    grad_pair = rounded(jnp.stack([merge_heads(grad_keys), merge_heads(grad_values)], axis=2))
    grad_cross_query = outer_sum(normed_cross, grad_queries)
    grad_cross_pair = jnp.einsum(
        "csd,cste->dte", states, grad_pair, preferred_element_type=jnp.float32
    )
    grad_text = lax.psum_scatter(
        jnp.einsum(
            "cste,dte->csd", grad_pair, full_cross_pair, preferred_element_type=jnp.float32
        ).astype(jnp.bfloat16),
        "mp",
        scatter_dimension=1,
        tiled=True,
    ).astype(jnp.float32)
    grad_normed = settle_grad(unproject(grad_queries, full_cross_query))
    back_stream, grad_gain_two, grad_bias_two = pull_cross(grad_normed)
    grad_stream = grad_stream + back_stream
    grad_branch = widen_grad(rounded(grad_stream))
    grad_self_output = outer_sum(grad_branch, mixed_self)
    grad_mixed = rounded(project(grad_branch, full_output))
    grad_queries, grad_keys, grad_values = self_backward(
        split_heads(queries),
        split_heads(self_keys),
        split_heads(values),
        log_sums,
        split_heads(grad_mixed),
    )
    grad_pair = rounded(jnp.stack([merge_heads(grad_queries), merge_heads(grad_keys)], axis=2))
    grad_values = rounded(merge_heads(grad_values))
    grad_self_pair = jnp.einsum(
        "cld,clte->dte", normed_self, grad_pair, preferred_element_type=jnp.float32
    )
    grad_self_value = outer_sum(normed_self, grad_values)
    grad_normed = settle_grad(
        jnp.einsum("clte,dte->cld", grad_pair, full_query_key, preferred_element_type=jnp.float32)
        + unproject(grad_values, full_value)
    )
    back_stream, grad_gain_one, grad_bias_one = pull_self(grad_normed)
    grad_inputs = grad_stream + back_stream
    grad_norm_rows = lax.psum(
        jnp.stack(
            [
                grad_gain_one,
                grad_bias_one,
                grad_gain_two,
                grad_bias_two,
                grad_gain_three,
                grad_bias_three,
            ],
            axis=1,
        ).astype(jnp.bfloat16),
        "mp",
    )
    (
        shard_norms,
        shard_self_pair,
        shard_self_value,
        shard_self_output,
        shard_cross_query,
        shard_cross_pair,
        shard_cross_output,
        shard_hidden_in,
        shard_hidden_out,
    ) = (
        lax.psum_scatter(grad_norm_rows, "dp", scatter_dimension=0, tiled=True).astype(jnp.float32),
        lax.psum_scatter(
            grad_self_pair.astype(jnp.bfloat16), "dp", scatter_dimension=0, tiled=True
        ).astype(jnp.float32),
        lax.psum_scatter(
            grad_self_value.astype(jnp.bfloat16), "dp", scatter_dimension=0, tiled=True
        ).astype(jnp.float32),
        lax.psum_scatter(
            grad_self_output.astype(jnp.bfloat16), "dp", scatter_dimension=0, tiled=True
        ).astype(jnp.float32),
        lax.psum_scatter(
            grad_cross_query.astype(jnp.bfloat16), "dp", scatter_dimension=0, tiled=True
        ).astype(jnp.float32),
        lax.psum_scatter(
            grad_cross_pair.astype(jnp.bfloat16), "dp", scatter_dimension=0, tiled=True
        ).astype(jnp.float32),
        lax.psum_scatter(
            grad_cross_output.astype(jnp.bfloat16), "dp", scatter_dimension=0, tiled=True
        ).astype(jnp.float32),
        lax.psum_scatter(
            grad_hidden_in.astype(jnp.bfloat16), "dp", scatter_dimension=0, tiled=True
        ).astype(jnp.float32),
        lax.psum_scatter(
            grad_hidden_out.astype(jnp.bfloat16), "dp", scatter_dimension=0, tiled=True
        ).astype(jnp.float32),
    )
    factors = CLIP_LIMIT / jnp.maximum(jnp.stack([self_top, cross_top]), CLIP_LIMIT)
    root_scales = jnp.repeat(jnp.sqrt(factors), head_width, axis=1)
    clipped_self = self_query_key * root_scales[0][None, None, :]
    clipped_query = cross_query * root_scales[1][None, :]
    clipped_key = cross_key_value[:, 0] * root_scales[1][None, :]
    return (
        output,
        grad_inputs,
        grad_text,
        shard_norms,
        shard_self_pair,
        shard_self_value,
        shard_self_output,
        shard_cross_query,
        shard_cross_pair,
        shard_cross_output,
        shard_hidden_in,
        shard_hidden_out,
        factors,
        clipped_self,
        clipped_query,
        clipped_key,
    )


NT = (((1,), (1,)), ((), ()))
TN = (((0,), (0,)), ((), ()))
NN = (((1,), (0,)), ((), ()))
f32 = jnp.float32
bf16 = jnp.bfloat16
LANES = 128
MESH = pl.DeviceIdType.MESH
Z, Y, CORES = 4, 2, 2


def dotf(a, b, dims):
    return lax.dot_general(a, b, dims, preferred_element_type=f32)


def head_masks():
    lane = lax.broadcasted_iota(jnp.int32, (1, LANES), 1)
    return [lane < 64, lane >= 64]


def self_forward_kernel(rows_at_once, q_ref, k_ref, v_ref, o_ref, lse_ref, peak_ref):
    frames, size = q_ref.shape[0], rows_at_once
    masks = head_masks()
    key_row = lax.broadcasted_iota(jnp.int32, (size, size), 0)
    query_col = lax.broadcasted_iota(jnp.int32, (size, size), 1)
    allowed = key_row <= query_col
    zero = jnp.zeros((), bf16)
    peaks = [None, None]
    values = [jnp.where(mask, v_ref[...], zero) for mask in masks]
    for block in range(frames // size):
        first = block * size
        rows = slice(first, first + size)
        q = q_ref[rows, :] * jnp.asarray(0.125, bf16)
        mixed = None
        for h in range(2):
            qh = jnp.where(masks[h], q, zero)
            diagonal = jnp.where(allowed, dotf(k_ref[rows, :], qh, NT), MASKED)
            top = jnp.max(diagonal, axis=0, keepdims=True)
            if first:
                full = dotf(k_ref[0:first, :], qh, NT)
                top = jnp.maximum(top, jnp.max(full, axis=0, keepdims=True))
            diagonal = jnp.exp(diagonal - top)
            total = jnp.sum(diagonal, axis=0, keepdims=True)
            part = dotf(diagonal.astype(bf16), values[h][rows, :], TN)
            if first:
                full = jnp.exp(full - top)
                total = total + jnp.sum(full, axis=0, keepdims=True)
                part = part + dotf(full.astype(bf16), values[h][0:first, :], TN)
            lse_ref[h : h + 1, rows] = top + jnp.log(total)
            part = part * (1.0 / total).reshape(size, 1)
            mixed = part if mixed is None else mixed + part
            peaks[h] = top if peaks[h] is None else jnp.maximum(peaks[h], top)
        o_ref[rows, :] = mixed.astype(bf16)
    for h in range(2):
        peak_ref[h : h + 1, :] = jnp.broadcast_to(
            jnp.max(peaks[h], axis=1, keepdims=True), (1, LANES)
        )


def self_attend(qkv, width):
    frames, pairs = qkv.shape[1], width // LANES
    at = lambda offset: pl.BlockSpec((None, frames, LANES), lambda m, i: (m, 0, offset + i))
    stat = lambda n: pl.BlockSpec((None, None, 8, n), lambda m, i: (m, i, 0, 0))
    return pl.pallas_call(
        functools.partial(self_forward_kernel, 512),
        grid=(2, pairs),
        out_shape=(
            jax.ShapeDtypeStruct((2, frames, width), bf16),
            jax.ShapeDtypeStruct((2, pairs, 8, frames), f32),
            jax.ShapeDtypeStruct((2, pairs, 8, LANES), f32),
        ),
        in_specs=[at(0), at(pairs), at(2 * pairs)],
        out_specs=(at(0), stat(frames), stat(LANES)),
        compiler_params=pltpu.CompilerParams(vmem_limit_bytes=40 << 20),
        cost_estimate=pl.CostEstimate(
            flops=16 * frames * frames * width,
            bytes_accessed=16 * frames * width,
            transcendentals=0,
        ),
    )(qkv, qkv, qkv)


def self_backward_kernel(
    rows_at_once, q_ref, k_ref, v_ref, g_ref, lse_ref, dq_ref, dk_ref, dv_ref, dk_sum, dv_sum
):
    frames, size = q_ref.shape[0], rows_at_once
    masks = head_masks()
    key_row = lax.broadcasted_iota(jnp.int32, (size, size), 0)
    query_col = lax.broadcasted_iota(jnp.int32, (size, size), 1)
    allowed = key_row <= query_col
    zero = jnp.zeros((), bf16)
    keys = [jnp.where(mask, k_ref[...], zero) for mask in masks]
    blocks = frames // size
    for block in reversed(range(blocks)):
        first = block * size
        spans = [(slice(first, first + size), True)]
        if first:
            spans.append((slice(0, first), False))
        rows = spans[0][0]
        q = q_ref[rows, :] * jnp.asarray(0.125, bf16)
        g = g_ref[rows, :]
        dq = None
        dk, dv = [None] * len(spans), [None] * len(spans)
        for h in range(2):
            qh, gh = jnp.where(masks[h], q, zero), jnp.where(masks[h], g, zero)
            lse = lse_ref[h : h + 1, rows]
            weights, grads, center = [], [], None
            for span, masked in spans:
                scores = dotf(k_ref[span, :], qh, NT)
                if masked:
                    scores = jnp.where(allowed, scores, MASKED)
                weights.append(jnp.exp(scores - lse))
                grads.append(dotf(v_ref[span, :], gh, NT))
                part = jnp.sum(weights[-1] * grads[-1], axis=0, keepdims=True)
                center = part if center is None else center + part
            for i, (span, _) in enumerate(spans):
                ds = (weights[i] * (grads[i] - center)).astype(bf16)
                a = dotf(weights[i].astype(bf16), gh, NN)
                b = dotf(ds, qh, NN)
                c = dotf(ds, keys[h][span, :], TN)
                dv[i] = a if dv[i] is None else dv[i] + a
                dk[i] = b if dk[i] is None else dk[i] + b
                dq = c if dq is None else dq + c
        dq_ref[rows, :] = (dq * 0.125).astype(bf16)
        for i, (span, _) in enumerate(spans):
            if block == blocks - 1:
                dk_sum[span, :] = dk[i]
                dv_sum[span, :] = dv[i]
            else:
                dk_sum[span, :] += dk[i]
                dv_sum[span, :] += dv[i]
    dk_ref[...] = dk_sum[...].astype(bf16)
    dv_ref[...] = dv_sum[...].astype(bf16)


class Hop:
    def __init__(self, kind, group):
        self.kind, self.group = kind, group
        rows, width = group.rows // 2, group.width
        self.chunk = (rows, width)
        self.count = {"x1": 8, "y1": 8, "y2": 4, "x2": 4, "za": 3, "zb": 3}[kind]
        self.lead = {"x1": (Z, Y), "y1": (2, Z), "y2": (Z,), "x2": (Z,), "za": (3,), "zb": (3,)}[kind]
        self.names = {
            "x1": ["own", "there"],
            "y1": ["own", "there"],
            "y2": ["own", "there", "x1"],
            "x2": ["own", "there", "y1"],
            "za": ["own", "there", "x1", "y2"],
            "zb": ["own", "there", "y1", "x2"],
        }[kind]

    def shape(self):
        return jax.ShapeDtypeStruct(self.lead + self.chunk, bf16)

    def scratch(self):
        return [
            pltpu.VMEM((self.count, len(self.names)) + self.chunk, bf16),
            pltpu.VMEM((self.count,) + self.chunk, bf16),
            pltpu.SemaphoreType.DMA((self.count, len(self.names))),
            pltpu.SemaphoreType.DMA((self.count,)),
            pltpu.SemaphoreType.DMA((self.count,)),
        ]

    def bind(self, sources, target, scratch):
        self.sources, self.target = sources, target
        self.loads, self.sent, self.load_sem, self.send_sem, self.recv_sem = scratch

    def index(self, t):
        half = self.chunk[0]
        low, high = pl.ds(0, half), pl.ds(half, half)
        if self.kind == "x1":
            at = (1, t // 2, t % 2, low)
            return [at, at], (t // 2, t % 2)
        if self.kind == "y1":
            at = (t // 4, t % 4, 1, high)
            return [at, at], (t // 4, t % 4)
        if self.kind == "y2":
            at = (0, t, 1, low)
            return [at, at, (t, 1)], (t,)
        if self.kind == "x2":
            at = (1, t, 0, high)
            return [at, at, (1, t)], (t,)
        z = (lax.axis_index("dp") // (Y * CORES) + t + 1) % Z
        if self.kind == "za":
            at = (0, z, 0, low)
            return [at, at, (z, 0), (z,)], (t,)
        at = (0, z, 0, high)
        return [at, at, (0, z), (z,)], (t,)

    def partner(self, t):
        dp, mp = lax.axis_index("dp"), lax.axis_index("mp")
        if self.kind in ("x1", "x2"):
            return (dp, 1 - mp)
        if self.kind in ("y1", "y2"):
            return (dp + CORES - 2 * CORES * ((dp // CORES) % Y), mp)
        group = Y * CORES
        return (((dp // group + t + 1) % Z) * group + dp % group, mp)

    def partners(self):
        return [self.partner(t) for t in range(3 if self.kind in ("za", "zb") else 1)]

    def load(self, t):
        return [
            pltpu.make_async_copy(source.at[at], self.loads.at[t, i], self.load_sem.at[t, i])
            for i, (source, at) in enumerate(zip(self.sources, self.index(t)[0]))
        ]

    def send(self, t):
        return pltpu.make_async_remote_copy(
            src_ref=self.sent.at[t],
            dst_ref=self.target.at[self.index(t)[1]],
            send_sem=self.send_sem.at[t],
            recv_sem=self.recv_sem.at[t],
            device_id=self.partner(t),
            device_id_type=MESH,
        )

    def begin(self):
        for t in range(self.count):
            for copy in self.load(t):
                copy.start()

    def each(self, steps):
        return self.count if steps < 3 else -(-self.count // 2)

    def work(self, step, steps, j):
        t = step * self.each(steps) + j

        @pl.when(t < self.count)
        def _():
            for copy in self.load(t):
                copy.wait()
            total = self.loads[t, 0].astype(f32)
            for i in range(1, len(self.names)):
                total = total + self.loads[t, i].astype(f32)
            self.sent[t] = total.astype(bf16)
            self.send(t).start()

    def finish(self):
        for t in range(self.count):
            self.send(t).wait()


class Swap:
    kind, names = "x0", ["sent"]

    def __init__(self, holder):
        self.group = holder

    def shape(self):
        sent = self.group.arrays["sent"]
        return jax.ShapeDtypeStruct(sent.shape, sent.dtype)

    def scratch(self):
        return [pltpu.SemaphoreType.DMA((1,)), pltpu.SemaphoreType.DMA((1,))]

    def bind(self, sources, target, scratch):
        self.source, self.target = sources[0], target
        self.send_sem, self.recv_sem = scratch

    def partners(self):
        return [(lax.axis_index("dp"), 1 - lax.axis_index("mp"))]

    def copy(self):
        return pltpu.make_async_remote_copy(
            src_ref=self.source,
            dst_ref=self.target,
            send_sem=self.send_sem.at[0],
            recv_sem=self.recv_sem.at[0],
            device_id=self.partners()[0],
            device_id_type=MESH,
        )

    def each(self, steps):
        return 1

    def begin(self):
        pass

    def work(self, step, steps, j):
        @pl.when(step == 0)
        def _():
            self.copy().start()

    def finish(self):
        self.copy().wait()


class Total:
    kind = "total"
    names = ["own", "there", "x1", "y2", "y1", "x2", "za", "zb"]

    def __init__(self, group):
        self.group = group
        low = group.rows // 2
        self.low, self.high = pl.ds(0, low), pl.ds(low, group.rows - low)

    def shape(self):
        return jax.ShapeDtypeStruct((self.group.rows, self.group.width), f32)

    def scratch(self):
        half, width = self.group.rows // 2, self.group.width
        return [
            pltpu.VMEM((2, 7, half, width), bf16),
            pltpu.VMEM((2 * half, width), f32),
            pltpu.SemaphoreType.DMA((2, 7)),
            pltpu.SemaphoreType.DMA(()),
        ]

    def bind(self, sources, target, scratch):
        self.sources, self.target = dict(zip(self.names, sources)), target
        self.terms, self.sum, self.load_sem, self.store_sem = scratch

    def partners(self):
        return []

    def loads(self):
        z = lax.axis_index("dp") // (Y * CORES)
        a = self.sources
        low = [a["own"].at[0, z, 0, self.low], a["there"].at[0, z, 0, self.low], a["x1"].at[z, 0]]
        low += [a["y2"].at[z]] + [a["za"].at[k] for k in range(3)]
        high = [a["own"].at[0, z, 0, self.high], a["there"].at[0, z, 0, self.high]]
        high += [a["y1"].at[0, z], a["x2"].at[z]] + [a["zb"].at[k] for k in range(3)]
        return [
            pltpu.make_async_copy(source, self.terms.at[p, i], self.load_sem.at[p, i])
            for p, part in enumerate((low, high))
            for i, source in enumerate(part)
        ]

    def each(self, steps):
        return 0

    def begin(self):
        for copy in self.loads():
            copy.start()

    def finish(self):
        for copy in self.loads():
            copy.wait()
        half = self.group.rows // 2
        for p in range(2):
            total = self.terms[p, 0].astype(f32)
            for i in range(1, 7):
                total = total + self.terms[p, i].astype(f32)
            self.sum[p * half : (p + 1) * half, :] = total
        copy = pltpu.make_async_copy(self.sum, self.target, self.store_sem)
        copy.start()
        copy.wait()


class Holder:
    def __init__(self, sent):
        self.arrays = {"sent": sent}

    def got(self):
        return self.arrays["x0"]


class Group:
    def __init__(self, own, there):
        self.arrays = {"own": own, "there": there}
        self.rows, self.width = own.shape[3], own.shape[4]

    def result(self, z):
        a = self.arrays
        half = self.rows // 2
        take = lambda array, at=0: lax.dynamic_index_in_dim(array, z, at, keepdims=False)
        total = take(a["own"][0, :, 0]).astype(f32) + take(a["there"][0, :, 0]).astype(f32)
        low = take(a["x1"][:, 0]).astype(f32) + take(a["y2"]).astype(f32)
        high = take(a["y1"][0]).astype(f32) + take(a["x2"]).astype(f32)
        for k in range(3):
            low = low + a["za"][k].astype(f32)
            high = high + a["zb"][k].astype(f32)
        return total + jnp.concatenate([low, high], axis=0)


def meet(partners):
    barrier = pltpu.get_barrier_semaphore()
    for partner in partners:
        pl.semaphore_signal(barrier, inc=1, device_id=partner, device_id_type=MESH)
    pl.semaphore_wait(barrier, len(partners))


def core_partner():
    dp = lax.axis_index("dp")
    return (dp + 1 - 2 * (dp % CORES), lax.axis_index("mp"))


def hosted(body, number, grid, args, in_specs, out_shape, out_specs, scratch, plan, flops, core=False, near=False, after=(), closing=None):
    special = {"x0": Swap, "total": Total}
    hops = [special[k](group) if k in special else Hop(k, group) for k, group in (*plan, *after)]
    made = {(id(hop.group), hop.kind): k for k, hop in enumerate(hops)}
    arrays, places = [], {}
    for hop in hops:
        for name in hop.names:
            key = (id(hop.group), name)
            if key not in places and key not in made:
                places[key] = len(arrays)
                arrays.append(hop.group.arrays[name])
    steps = 1
    for n in grid:
        steps *= n
    kinds = set(hop.kind[0] for hop in hops if hop.kind != "total")

    def kernel(*refs):
        counts = [len(args), len(arrays), len(out_shape), len(hops), len(scratch)]
        parts, at = [], 0
        for n in counts:
            parts.append(refs[at : at + n])
            at += n
        for k, hop in enumerate(hops):
            keys = [(id(hop.group), name) for name in hop.names]
            sources = [parts[3][made[key]] if key in made else parts[1][places[key]] for key in keys]
            taken = len(hop.scratch())
            hop.bind(sources, parts[3][k], refs[at : at + taken])
            at += taken
        first, last = hops[: len(plan)], hops[len(plan) :]
        step = 0
        for axis, n in enumerate(grid):
            step = step * n + pl.program_id(axis)

        @pl.when(step == 0)
        def _():
            partners = [core_partner()] if core else []
            if near:
                dp, mp = lax.axis_index("dp"), lax.axis_index("mp")
                partners += [(dp, 1 - mp), (dp + CORES - 2 * CORES * ((dp // CORES) % Y), mp)]
            for kind in sorted(kinds):
                partners += [hop for hop in hops if hop.kind[0] == kind][0].partners()
            if partners:
                meet(partners)
            for hop in first:
                hop.begin()

        for j in range(max([hop.each(steps) for hop in first], default=0)):
            for hop in first:
                if j < hop.each(steps):
                    hop.work(step, steps, j)
        body(*parts[0], *parts[2], *parts[4])

        @pl.when(step == steps - 1)
        def _():
            left = sorted(first, key=lambda hop: hop.kind != "total")
            if last:
                for hop in first:
                    if hop.kind in ("x2", "y2"):
                        hop.finish()
                        left.remove(hop)
                for hop in last:
                    if hop.kind != "total":
                        hop.begin()
                        for j in range(hop.count):
                            hop.work(0, 1, j)
            if last:
                for hop in [hop for hop in left if hop.kind == "total"]:
                    hop.finish()
                    left.remove(hop)
            if closing is not None:
                closing(*parts[0], *parts[2], *parts[4])
            for hop in left:
                hop.finish()
            for hop in last:
                if hop.kind == "total":
                    hop.begin()
            for hop in last:
                hop.finish()

    hbm = pl.BlockSpec(memory_space=pl.ANY)
    extra = [s for hop in hops for s in hop.scratch()]
    outs = pl.pallas_call(
        kernel,
        grid=grid,
        in_specs=list(in_specs) + [hbm] * len(arrays),
        out_specs=tuple(out_specs) + (hbm,) * len(hops),
        out_shape=tuple(out_shape) + tuple(hop.shape() for hop in hops),
        scratch_shapes=list(scratch) + extra,
        compiler_params=pltpu.CompilerParams(
            vmem_limit_bytes=56 << 20,
            **(dict(collective_id=number, has_side_effects=True) if hops or core else {}),
        ),
        cost_estimate=pl.CostEstimate(flops=flops, bytes_accessed=flops // 500, transcendentals=0),
    )(*args, *arrays)
    for hop, array in zip(hops, outs[len(out_shape) :]):
        hop.group.arrays[hop.kind] = array
    return outs[: len(out_shape)]


def self_attend_back(number, plan, qkv, grad, lse, width, begin, end):
    frames, pairs = qkv.shape[1], width // LANES
    at = lambda offset: pl.BlockSpec((None, frames, LANES), lambda m, i: (m, 0, offset + i))
    out = jax.ShapeDtypeStruct((2, frames, (end - begin) * LANES), bf16)
    return hosted(
        functools.partial(self_backward_kernel, 256),
        number,
        (2, end - begin),
        [qkv, qkv, qkv, grad, lse],
        [
            at(begin),
            at(pairs + begin),
            at(2 * pairs + begin),
            at(begin),
            pl.BlockSpec((None, None, 8, frames), lambda m, i: (m, begin + i, 0, 0)),
        ],
        [out] * 3,
        [at(0)] * 3,
        [pltpu.VMEM((frames, LANES), f32)] * 2,
        plan,
        16 * frames * frames * LANES * (end - begin),
    )


def half_spec(array, half):
    if array.ndim == 2:
        return pl.BlockSpec(array.shape, lambda *grid: (0, 0), pipeline_mode=pl.Buffered(1))
    return pl.BlockSpec(
        (None,) + array.shape[1:], lambda *grid: (half, 0, 0), pipeline_mode=pl.Buffered(1)
    )


def exchanged_grad(number, plan, xs, tiles, rows):
    depth = xs[0].shape[1]
    specs = [pl.BlockSpec(x.shape, lambda j, m: (0, 0), pipeline_mode=pl.Buffered(1)) for x in xs]
    args, halves = list(xs), []
    for _, arrays in tiles:
        halves.append([])
        for half in range(2):
            halves[-1].append(range(len(args), len(args) + len(arrays)))
            args += arrays
            specs += [half_spec(array, half) for array in arrays]
    tile = sum(array.shape[2] for array in tiles[0][1])
    count = len(tiles)
    steps = 2 * count
    longest = max(x.shape[0] for x in xs)
    shape = jax.ShapeDtypeStruct((2, Z, Y, rows, count * tile), bf16)
    hbm = pl.BlockSpec(memory_space=pl.ANY)

    def body(*refs):
        own_ref, there_ref = refs[len(args) : len(args) + 2]
        turned, own, other, own_sem, send_sem, recv_sem = refs[len(args) + 2 :]
        dp, mp = lax.axis_index("dp"), lax.axis_index("mp")
        core, across = dp % CORES, (dp // CORES) % Y
        j, m = pl.program_id(0), pl.program_id(1)
        step = 2 * j + m

        def place(step):
            column = (step // 2) * tile
            column = column if isinstance(column, int) else pl.multiple_of(column, LANES)
            every = slice(None)
            return ((step + mp) % 2, every, every, every, pl.ds(column, tile))

        def kept(step):
            slot = step % 2
            return pltpu.make_async_copy(own.at[slot], own_ref.at[place(step)], own_sem.at[slot])

        def sent(step):
            return pltpu.make_async_remote_copy(
                src_ref=other.at[step % 2],
                dst_ref=there_ref.at[place(step)],
                send_sem=send_sem.at[step],
                recv_sem=recv_sem.at[step],
                device_id=core_partner(),
                device_id_type=MESH,
            )

        @pl.when(step >= 2)
        def _():
            kept(step - 2).wait()
            sent(step - 2).wait_send()

        for k, (source, _) in enumerate(tiles):
            frames = xs[source].shape[0]

            if k == 0 or tiles[k - 1][0] != source:

                @pl.when((j == k) & (m == 0))
                def _(source=source, frames=frames):
                    turned[:, 0:frames] = refs[source][...].T

            for half in range(2):

                @pl.when((j == k) & (m == half))
                def _(k=k, half=half, frames=frames):
                    pieces = [refs[i][...] for i in halves[k][half]]
                    y = pieces[0] if len(pieces) == 1 else jnp.concatenate(pieces, axis=1)
                    for z in range(Z):
                        span = slice(z * Y * CORES * rows, (z + 1) * Y * CORES * rows)
                        part = dotf(turned[span, 0:frames], y, NN).astype(bf16)
                        for i in range(Y):
                            first = part[2 * i * rows : (2 * i + 1) * rows]
                            second = part[(2 * i + 1) * rows : (2 * i + 2) * rows]
                            own[m, z, (i + across) % 2] = jnp.where(core == 0, first, second)
                            other[m, z, (i + across) % 2] = jnp.where(core == 0, second, first)

        kept(step).start()
        sent(step).start()

        @pl.when(step == steps - 1)
        def _():
            for t in (steps - 2, steps - 1):
                kept(t).wait()
                sent(t).wait_send()
            for t in range(steps):
                sent(t).wait_recv()

    outs = hosted(
        body,
        number,
        (count, 2),
        args,
        specs,
        [shape, shape],
        [hbm, hbm],
        [
            pltpu.VMEM((depth, longest), bf16),
            pltpu.VMEM((2, Z, Y, rows, tile), bf16),
            pltpu.VMEM((2, Z, Y, rows, tile), bf16),
            pltpu.SemaphoreType.DMA((2,)),
            pltpu.SemaphoreType.DMA((steps,)),
            pltpu.SemaphoreType.DMA((steps,)),
        ],
        plan,
        4 * longest * depth * count * tile,
        core=True,
    )
    return Group(*outs)


def gather_kernel(parts, swaps, *refs):
    shard_ref, sent_refs = refs[0], refs[1 : 1 + swaps]
    whole_ref, got_refs = refs[1 + swaps], refs[2 + swaps : 2 + 2 * swaps]
    own_sem, swap_send, swap_recv, send_sem, recv_sem = refs[2 + 2 * swaps :]
    dp, x = lax.axis_index("dp"), lax.axis_index("mp")
    group = Y * CORES
    z, rest = dp // group, dp % group
    across = rest + CORES - 2 * CORES * (rest // CORES)
    rows, columns = shard_ref.shape
    x_peer, y_peer, core_peer = (dp, 1 - x), (z * group + across, x), core_partner()
    z_peers = [(((z + k) % Z) * group + rest, x) for k in range(1, Z)]
    cut = 5 * rows // 6
    low, high, every = pl.ds(0, cut), pl.ds(cut, rows - cut), slice(None)
    meet([x_peer, y_peer, core_peer] + z_peers)
    started = []

    def send(part, slot, source, at, peer):
        copy = pltpu.make_async_remote_copy(
            src_ref=source,
            dst_ref=whole_ref.at[at],
            send_sem=send_sem.at[part, slot],
            recv_sem=recv_sem.at[part, slot],
            device_id=peer,
            device_id_type=MESH,
        )
        copy.start()
        started.append(copy)
        return copy

    def pass_on(part, slot, at, peer):
        return send(part, slot, whole_ref.at[at], at, peer)

    def columns_of(part):
        begin, end = parts[part]
        return pl.ds(begin, end - begin)

    swapped = []
    for i in range(swaps):
        copy = pltpu.make_async_remote_copy(
            src_ref=sent_refs[i],
            dst_ref=got_refs[i],
            send_sem=swap_send.at[i],
            recv_sem=swap_recv.at[i],
            device_id=x_peer,
            device_id_type=MESH,
        )
        copy.start()
        swapped.append(copy)
    own = pltpu.make_async_copy(shard_ref, whole_ref.at[x, z, rest], own_sem)
    own.start()
    along, over, turned, late = {}, {}, {}, []
    for part in range(len(parts)):
        cut = columns_of(part)
        at = (x, z, rest, every, cut)
        along[part] = [
            send(part, k, shard_ref.at[every, cut], at, peer) for k, peer in enumerate(z_peers)
        ]
        late.append(send(part, 3, shard_ref.at[every, cut], at, core_peer))
    own.wait()

    def first(part):
        cut = columns_of(part)
        for copy in along[part]:
            copy.wait_recv()
        over[part] = [
            pass_on(part, 4, (x, every, rest, low, cut), x_peer),
            pass_on(part, 5, (x, every, rest, high, cut), y_peer),
        ]
        for k in range(1, Z):
            late.append(pass_on(part, 5 + k, (x, (z + k) % Z, rest, every, cut), core_peer))

    def second(part):
        cut = columns_of(part)
        for copy in over[part]:
            copy.wait_recv()
        turned[part] = [
            pass_on(part, 9, (0, every, rest, low, cut), y_peer),
            pass_on(part, 10, (x, every, rest, high, cut), x_peer),
            pass_on(part, 11, (1, every, rest, low, cut), y_peer),
            pass_on(part, 12, (x, every, across, high, cut), x_peer),
        ]
        late.append(pass_on(part, 13, (1 - x, every, rest, low, cut), core_peer))
        late.append(pass_on(part, 14, (x, every, across, high, cut), core_peer))

    def third(part):
        cut = columns_of(part)
        for copy in turned[part]:
            copy.wait_recv()
        late.append(pass_on(part, 15, (0, every, across, low, cut), core_peer))
        late.append(pass_on(part, 16, (1, every, across, low, cut), core_peer))
        late.append(pass_on(part, 17, (1 - x, every, rest, high, cut), core_peer))
        late.append(pass_on(part, 18, (1 - x, every, across, high, cut), core_peer))

    first(0)
    for part in range(len(parts)):
        second(part)
        if part + 1 < len(parts):
            first(part + 1)
        if part:
            third(part - 1)
    third(len(parts) - 1)
    for copy in late:
        copy.wait_recv()
    for copy in started:
        copy.wait_send()
    for copy in swapped:
        copy.wait()


def gather_now(number, shard, swaps):
    rows, columns = shard.shape
    tiles = columns // LANES
    cuts = [0, tiles // 3 * LANES, 2 * tiles // 3 * LANES, columns]
    parts = list(zip(cuts[:-1], cuts[1:]))
    hbm = pl.BlockSpec(memory_space=pl.ANY)
    outs = pl.pallas_call(
        functools.partial(gather_kernel, parts, len(swaps)),
        in_specs=[hbm] * (1 + len(swaps)),
        out_specs=(hbm,) * (1 + len(swaps)),
        out_shape=(jax.ShapeDtypeStruct((2, Z, Y * CORES, rows, columns), shard.dtype),)
        + tuple(jax.ShapeDtypeStruct(a.shape, a.dtype) for a in swaps),
        scratch_shapes=[
            pltpu.SemaphoreType.DMA(()),
            pltpu.SemaphoreType.DMA((len(swaps),)),
            pltpu.SemaphoreType.DMA((len(swaps),)),
            pltpu.SemaphoreType.DMA((len(parts), 19)),
            pltpu.SemaphoreType.DMA((len(parts), 19)),
        ],
        compiler_params=pltpu.CompilerParams(collective_id=number, has_side_effects=True),
        cost_estimate=pl.CostEstimate(flops=10**9, bytes_accessed=10**8, transcendentals=0),
    )(shard, *swaps)
    return outs[0], outs[1:]


def project_kernel(x_ref, w_ref, o_ref):
    step = x_ref.shape[0] // 4
    for i in range(4):
        rows = slice(i * step, (i + 1) * step)
        o_ref[rows, :] = dotf(x_ref[rows, :], w_ref[...], NN).astype(o_ref.dtype)


def project_both(x, whole, begin, width, tile=768):
    (frames, depth), first = x.shape, begin // tile
    return pl.pallas_call(
        project_kernel,
        grid=(2, width // tile),
        in_specs=[
            pl.BlockSpec((frames, depth), lambda m, j: (0, 0)),
            pl.BlockSpec((None, depth, tile), lambda m, j: (m, 0, first + j)),
        ],
        out_specs=pl.BlockSpec((None, frames, tile), lambda m, j: (m, 0, j)),
        out_shape=jax.ShapeDtypeStruct((2, frames, width), bf16),
        compiler_params=pltpu.CompilerParams(vmem_limit_bytes=40 << 20),
        cost_estimate=pl.CostEstimate(
            flops=4 * frames * depth * width,
            bytes_accessed=4 * (frames + depth) * width,
            transcendentals=0,
        ),
    )(x, whole)


def unproject_both(number, plan, pieces, whole, begin, width, base=None):
    frames, depth, tile = pieces[0][0].shape[-2], whole.shape[1], 512 if width < 1024 else 256
    first, direct = begin // width, len(pieces) == 2
    bases = [] if base is None else [base]

    def body(*refs):
        n = len(pieces)
        w_refs, refs_left = refs[n : n + 2], refs[n + 2 :]
        o_ref = refs_left[len(bases)]

        if not direct:
            joint = refs_left[-1]

            @pl.when(pl.program_id(0) == 0)
            def _():
                for ref, (_, half, column) in zip(refs, pieces):
                    joint[half, :, column : column + ref.shape[1]] = ref[...]

        for i in range(4):
            rows = slice(i * frames // 4, (i + 1) * frames // 4)
            ys = [refs[m][rows, :] if direct else joint[m, rows, :] for m in range(2)]
            total = dotf(ys[0], w_refs[0][...], NT) + dotf(ys[1], w_refs[1][...], NT)
            o_ref[rows, :] = refs_left[0][rows, :] + total if bases else total

    weights = lambda m: pl.BlockSpec((None, tile, width), lambda j: (m, j, first))
    across = pl.BlockSpec((frames, tile), lambda j: (0, j))
    return hosted(
        body,
        number,
        (depth // tile,),
        [p[0] for p in pieces] + [whole, whole] + bases,
        [half_spec(array, half) for array, half, _ in pieces] + [weights(0), weights(1)] + [across] * len(bases),
        [jax.ShapeDtypeStruct((frames, depth), f32)],
        [across],
        [] if direct else [pltpu.VMEM((2, frames, width), bf16)],
        plan,
        4 * frames * depth * width,
    )[0]


def halves_of(array):
    return [(array, 0, 0), (array, 1, 0)]


def norm_back_last(number, plan, after, stream, grad, gain, passed, others):
    frames, depth = stream.shape
    steps = 8
    size, half = frames // steps, steps // 2

    def swapped(got_ref, sent, send_sem, recv_sem, t):
        return pltpu.make_async_remote_copy(
            src_ref=sent.at[t],
            dst_ref=got_ref.at[t],
            send_sem=send_sem.at[t],
            recv_sem=recv_sem.at[t],
            device_id=(lax.axis_index("dp"), 1 - lax.axis_index("mp")),
            device_id_type=MESH,
        )

    def body(stream_ref, grad_ref, gain_ref, passed_ref, others_ref, o_ref, got_ref, total_ref, *scratch):
        sent, send_sem, recv_sem, sums = scratch[:4]
        step = pl.program_id(0)
        rows, inverse = norm_rows_of(stream_ref[...])
        grads = grad_ref[...]
        scaled = grads * gain_ref[...]
        products = jnp.mean(scaled * rows, axis=-1, keepdims=True)
        back = inverse * (scaled - jnp.mean(scaled, axis=-1, keepdims=True) - rows * products)
        total = passed_ref[...] + back
        o_ref[...] = total

        @pl.when(step == 0)
        def _():
            sums[0] = others_ref[...]

        sums[0, 0:1, :] += jnp.sum(grads * rows, axis=0, keepdims=True)
        sums[0, 1:2, :] += jnp.sum(grads, axis=0, keepdims=True)

        @pl.when(step // half == 1 - lax.axis_index("mp"))
        def _():
            sent[step % half] = total.astype(bf16)
            swapped(got_ref, sent, send_sem, recv_sem, step % half).start()

    def closing(stream_ref, grad_ref, gain_ref, passed_ref, others_ref, o_ref, got_ref, total_ref, *scratch):
        sent, swap_send, swap_recv, sums, got, send_sem, recv_sem = scratch
        dp, mp = lax.axis_index("dp"), lax.axis_index("mp")
        group = Y * CORES
        z, rest = dp // group, dp % group
        partners = [core_partner(), (dp + CORES - 2 * CORES * ((dp // CORES) % Y), mp)]
        partners.append(((z + 1 - 2 * (z % 2)) * group + rest, mp))
        partners.append((((z + 2) % Z) * group + rest, mp))
        partners.append((dp, 1 - mp))
        for i, partner in enumerate(partners):
            copy = pltpu.make_async_remote_copy(
                src_ref=sums.at[i],
                dst_ref=got.at[i],
                send_sem=send_sem.at[i],
                recv_sem=recv_sem.at[i],
                device_id=partner,
                device_id_type=MESH,
            )
            copy.start()
            copy.wait()
            sums[i + 1] = sums[i] + got[i]
        total_ref[...] = sums[5]
        for t in range(half):
            swapped(got_ref, sent, swap_send, swap_recv, t).wait()

    block = pl.BlockSpec((size, depth), lambda i: (i, 0))
    hbm = pl.BlockSpec(memory_space=pl.ANY)
    sums = pl.BlockSpec((8, depth), lambda i: (0, 0))
    total, got, sums = hosted(
        body,
        number,
        (steps,),
        [stream, grad, gain, passed, others],
        [block, block, pl.BlockSpec((1, depth), lambda i: (0, 0)), block, sums],
        [
            jax.ShapeDtypeStruct((frames, depth), f32),
            jax.ShapeDtypeStruct((half, size, depth), bf16),
            jax.ShapeDtypeStruct((8, depth), f32),
        ],
        [block, hbm, sums],
        [
            pltpu.VMEM((half, size, depth), bf16),
            pltpu.SemaphoreType.DMA((half,)),
            pltpu.SemaphoreType.DMA((half,)),
            pltpu.VMEM((6, 8, depth), f32),
            pltpu.VMEM((5, 8, depth), f32),
            pltpu.SemaphoreType.DMA((5,)),
            pltpu.SemaphoreType.DMA((5,)),
        ],
        plan,
        10**9,
        core=True,
        after=after,
        closing=closing,
    )
    return total, got.reshape(frames // 2, depth), sums


def pair_rows(array, masks):
    zero = jnp.zeros((), bf16)
    return jnp.concatenate([jnp.where(mask, array, zero) for mask in masks], axis=0)


def cross_weights_of(q, keys, masks):
    scores = dotf(q * jnp.asarray(0.125, bf16), keys, NT)
    tops = [jnp.max(jnp.where(mask, scores, MASKED), axis=1, keepdims=True) for mask in masks]
    exponents = jnp.exp(scores - jnp.where(masks[0], tops[0], tops[1]))
    sums = [jnp.sum(jnp.where(mask, exponents, 0.0), axis=1, keepdims=True) for mask in masks]
    return exponents * jnp.where(masks[0], 1.0 / sums[0], 1.0 / sums[1]), tops


def cross_forward_kernel(q_ref, k_ref, v_ref, o_ref, peak_ref):
    masks = head_masks()
    weights, tops = cross_weights_of(q_ref[...], pair_rows(k_ref[...], masks), masks)
    o_ref[...] = dotf(weights.astype(bf16), pair_rows(v_ref[...], masks), NN).astype(bf16)
    for h in range(2):
        peak_ref[h : h + 1, :] = jnp.broadcast_to(
            jnp.max(tops[h], axis=0, keepdims=True), (1, LANES)
        )


def cross_specs(frames, text, pairs):
    at = lambda n, offset: pl.BlockSpec((None, n, LANES), lambda m, i: (m, 0, offset + i))
    return at(frames, 0), at(text, 0), at(text, pairs)


def cross_attend(q, kv, width):
    frames, text, pairs = q.shape[1], kv.shape[1], width // LANES
    long, keys, values = cross_specs(frames, text, pairs)
    return pl.pallas_call(
        cross_forward_kernel,
        grid=(2, pairs),
        out_shape=(
            jax.ShapeDtypeStruct((2, frames, width), bf16),
            jax.ShapeDtypeStruct((2, pairs, 8, LANES), f32),
        ),
        in_specs=[long, keys, values],
        out_specs=(long, pl.BlockSpec((None, None, 8, LANES), lambda m, i: (m, i, 0, 0))),
        compiler_params=pltpu.CompilerParams(vmem_limit_bytes=32 << 20),
        cost_estimate=pl.CostEstimate(
            flops=32 * frames * LANES * width, bytes_accessed=8 * frames * width, transcendentals=0
        ),
    )(q, kv, kv)


def cross_backward_kernel(q_ref, k_ref, v_ref, g_ref, dq_ref, dk_ref, dv_ref):
    masks = head_masks()
    text = k_ref.shape[0]
    keys, values = pair_rows(k_ref[...], masks), pair_rows(v_ref[...], masks)
    q, g = q_ref[...], g_ref[...]
    weights, _ = cross_weights_of(q, keys, masks)
    grads = dotf(g, values, NT)
    products = weights * grads
    centers = [jnp.sum(jnp.where(mask, products, 0.0), axis=1, keepdims=True) for mask in masks]
    ds = (weights * (grads - jnp.where(masks[0], centers[0], centers[1]))).astype(bf16)
    dq_ref[...] = (dotf(ds, keys, NN) * 0.125).astype(bf16)
    dk = dotf(ds, q, TN) * 0.125
    dv = dotf(weights.astype(bf16), g, TN)
    dk_ref[...] = jnp.where(masks[0], dk[:text], dk[text:]).astype(bf16)
    dv_ref[...] = jnp.where(masks[0], dv[:text], dv[text:]).astype(bf16)


def cross_attend_back(q, kv, grad, width):
    frames, text, pairs = q.shape[1], kv.shape[1], width // LANES
    long, keys, values = cross_specs(frames, text, pairs)
    return pl.pallas_call(
        cross_backward_kernel,
        grid=(2, pairs),
        out_shape=(
            jax.ShapeDtypeStruct((2, frames, width), bf16),
            jax.ShapeDtypeStruct((2, text, width), bf16),
            jax.ShapeDtypeStruct((2, text, width), bf16),
        ),
        in_specs=[long, keys, values, long],
        out_specs=(long, keys, keys),
        compiler_params=pltpu.CompilerParams(vmem_limit_bytes=32 << 20),
        cost_estimate=pl.CostEstimate(
            flops=64 * frames * LANES * width, bytes_accessed=12 * frames * width, transcendentals=0
        ),
    )(q, kv, kv, grad)


def weight_grad_whole_kernel(x_ref, y0_ref, y1_ref, *refs):
    half, tile = pl.program_id(0), pl.program_id(1)
    o_ref, turned = refs[-2:]

    @pl.when((half == 0) & (tile == 0))
    def _():
        turned[...] = x_ref[...].T

    for m, y_ref in enumerate((y0_ref, y1_ref)):

        @pl.when(half == m)
        def _(y_ref=y_ref):
            step = o_ref.shape[0] // 4
            for i in range(4):
                rows = slice(i * step, (i + 1) * step)
                o_ref[rows, :] = dotf(turned[rows, :], y_ref[...], NN).astype(bf16)


def weight_grad_whole(x, ys, tile, columns, begin, into=None):
    frames, depth = x.shape
    width = ys[0].shape[1]
    tiles, first = width // tile, begin // tile
    given = [] if into is None else [into]
    return pl.pallas_call(
        weight_grad_whole_kernel,
        grid=(2, tiles),
        in_specs=[
            pl.BlockSpec((frames, depth), lambda m, j: (0, 0)),
            pl.BlockSpec((frames, tile), lambda m, j: (0, jnp.where(m == 0, j, tiles - 1))),
            pl.BlockSpec((frames, tile), lambda m, j: (0, jnp.where(m == 0, 0, j))),
        ]
        + [pl.BlockSpec(memory_space=pl.ANY)] * len(given),
        out_specs=pl.BlockSpec((None, depth, tile), lambda m, j: (m, 0, first + j)),
        scratch_shapes=[pltpu.VMEM((depth, frames), bf16)],
        out_shape=jax.ShapeDtypeStruct((2, depth, columns), bf16),
        input_output_aliases={3: 0} if given else {},
        compiler_params=pltpu.CompilerParams(vmem_limit_bytes=40 << 20),
        cost_estimate=pl.CostEstimate(
            flops=4 * frames * depth * width,
            bytes_accessed=4 * (depth + frames) * width + 2 * frames * depth,
            transcendentals=0,
        ),
    )(x, *ys, *given)


def swap(values, axis_name, pairs):
    return lax.ppermute(values, axis_name, pairs)


MP_PAIRS = [(0, 1), (1, 0)]
CORE_PAIRS = [(i, i ^ 1) for i in range(Z * Y * CORES)]


def over_all(value, join):
    value = join(value, swap(value, "dp", CORE_PAIRS))
    value = join(value, swap(value, "mp", MP_PAIRS))
    for bit in (2, 4, 8):
        pairs = [(i, i ^ bit) for i in range(Z * Y * CORES)]
        value = join(value, swap(value, "dp", pairs))
    return value


def joined(arrays):
    return jnp.concatenate(arrays, axis=1)


def norm_rows_of(stream):
    center = stream - jnp.mean(stream, axis=-1, keepdims=True)
    inverse = lax.rsqrt(jnp.mean(center * center, axis=-1, keepdims=True) + EPSILON)
    return center * inverse, inverse


def norm_back(stream, gain, grad):
    rows, inverse = norm_rows_of(stream)
    scaled = grad * gain
    back = inverse * (
        scaled
        - jnp.mean(scaled, axis=-1, keepdims=True)
        - rows * jnp.mean(scaled * rows, axis=-1, keepdims=True)
    )
    return back, jnp.sum(grad * rows, axis=0), jnp.sum(grad, axis=0)


def clip_per_device(
    inputs,
    text_states,
    cotangent,
    norm_params,
    self_query_key,
    self_value,
    self_output,
    cross_query,
    cross_key_value,
    cross_output,
    hidden_in,
    hidden_out,
):
    dp, mp = lax.axis_index("dp"), lax.axis_index("mp")
    z = dp // (Y * CORES)
    rows, width = self_value.shape
    both = range(2)

    def shard_of(pieces):
        return jnp.concatenate([rounded(p).reshape(rows, -1) for p in pieces], axis=1)

    def gathered(shard):
        whole = lax.all_gather(shard, ("mp", "dp"), axis=0, tiled=True)
        return whole.reshape(2, D, shard.shape[1])

    def other_half(array):
        return rounded(lax.dynamic_index_in_dim(array, 1 - mp, 0, keepdims=False))

    def whole_clip(array, got, kind):
        own = lax.dynamic_index_in_dim(array, mp, 0, keepdims=False).astype(kind)
        got = got.astype(kind)
        return jnp.where(
            mp == 0, jnp.concatenate([own, got], axis=0), jnp.concatenate([got, own], axis=0)
        )

    def other_frames(array):
        count = array.shape[0] // 2
        return rounded(lax.dynamic_slice_in_dim(array, (1 - mp) * count, count, 0))

    def own_frames(array, got):
        count = array.shape[0] // 2
        own = lax.dynamic_slice_in_dim(array, mp * count, count, 0)
        got = got.astype(f32)
        return jnp.where(mp == 0, jnp.stack([own, got]), jnp.stack([got, own]))

    norms_padded = jnp.pad(norm_params, ((0, 0), (0, LANES - norm_params.shape[1])))
    hidden = hidden_in.shape[1]
    self_shard = shard_of([self_query_key, self_value, self_output, norms_padded])
    cross_shard = shard_of([cross_query, cross_key_value, cross_output, hidden_in])
    sent = (other_half(inputs), other_half(text_states))
    self_shard, cross_shard, sent = lax.optimization_barrier((self_shard, cross_shard, sent))
    cross_all = gathered(cross_shard)
    self_all, (got_inputs, got_text) = gather_now(16, self_shard, sent)
    self_all = self_all.reshape(2, D, self_shard.shape[1])
    out_all = gathered(rounded(hidden_out))
    norms = self_all[0, :, 4 * width : 4 * width + norm_params.shape[1]].astype(f32).T
    self_o = [self_all[m, :, 3 * width : 4 * width] for m in both]
    cross_q = [cross_all[m, :, :width] for m in both]
    cross_kv = [cross_all[m, :, width : 3 * width] for m in both]
    cross_o = [cross_all[m, :, 3 * width : 4 * width] for m in both]
    in_w = [cross_all[m, :, 4 * width :] for m in both]

    def times(array, matrix):
        return dotf(array, matrix, NN)

    def times_turned(arrays, matrices):
        return dotf(arrays[0], matrices[0], NT) + dotf(arrays[1], matrices[1], NT)

    stream = whole_clip(inputs, got_inputs, f32)
    states = whole_clip(text_states, got_text, bf16)
    normed_self = rounded(norm_rows_of(stream)[0] * norms[0] + norms[1])
    qkv = project_both(normed_self, self_all, 0, 3 * width)
    qkv, cotangent = lax.optimization_barrier((qkv, cotangent))
    upstream = whole_clip(cotangent, swap(other_half(cotangent), "mp", MP_PAIRS), f32)
    mixed_self, lse, self_peaks = self_attend(qkv, width)
    after_self = unproject_both(0, [], halves_of(mixed_self), self_all, 3 * width, width, stream)
    normed_cross = rounded(norm_rows_of(after_self)[0] * norms[2] + norms[3])
    queries = project_both(normed_cross, cross_all, 0, width)
    text_kv = jnp.stack([rounded(times(states, cross_kv[m])) for m in both])
    mixed_cross, cross_peaks = cross_attend(queries, text_kv, width)
    after_cross = unproject_both(0, [], halves_of(mixed_cross), cross_all, 3 * width, width, after_self)
    normed_hidden = rounded(norm_rows_of(after_cross)[0] * norms[4] + norms[5])
    upward = [times(normed_hidden, in_w[m]) for m in both]
    activated, pulls = zip(*[jax.vjp(gelu_exact, up) for up in upward])
    activated = [rounded(a) for a in activated]

    branch = rounded(upstream)
    hidden_grad = weight_grad_whole(branch, activated, 512, 2 * hidden, hidden)
    def peaks_of(peaks):
        return peaks[:, :, :2, 0].reshape(2, -1)

    tops = over_all(jnp.stack([peaks_of(self_peaks), peaks_of(cross_peaks)]), jnp.maximum)
    tops = lax.dynamic_index_in_dim(tops, mp, 1, keepdims=False)
    factors = CLIP_LIMIT / jnp.maximum(tops, CLIP_LIMIT)
    root_scales = jnp.repeat(jnp.sqrt(factors), D // HEADS, axis=1)
    clipped = (
        self_query_key * root_scales[0][None, None, :],
        cross_query * root_scales[1][None, :],
        cross_key_value[:, 0] * root_scales[1][None, :],
    )
    out_all, hidden_grad, clipped = lax.optimization_barrier((out_all, hidden_grad, clipped))
    grad_up = [rounded(pulls[m](times(branch, out_all[m]))[0]) for m in both]
    hidden_grad = weight_grad_whole(normed_hidden, grad_up, 512, 2 * hidden, 0, hidden_grad)
    grad_up, hidden_grad = lax.optimization_barrier((grad_up, hidden_grad))
    shard_hidden = lax.psum_scatter(
        hidden_grad.reshape(2 * D, 2 * hidden), ("mp", "dp"), scatter_dimension=0, tiled=True
    ).astype(f32)
    grad_normed = unproject_both(
        0, [], [(a, m, 0) for m, a in enumerate(grad_up)], cross_all, 4 * width, hidden
    )
    back, gain_three, bias_three = norm_back(after_cross, norms[4], grad_normed)
    grad_stream = upstream + back

    branch_cross = rounded(grad_stream)
    grad_mixed = project_both(branch_cross, cross_all, 3 * width, width)
    dq, dk, dv = cross_attend_back(queries, text_kv, grad_mixed, width)
    grad_normed = unproject_both(0, [], halves_of(dq), cross_all, 0, width)
    back, gain_two, bias_two = norm_back(after_self, norms[2], grad_normed)
    dkv = [joined([dk[m], dv[m]]) for m in both]
    grad_text = times_turned(dkv, cross_kv)
    swap_text = Holder(other_frames(grad_text))
    grad_stream = grad_stream + back
    branch_self = rounded(grad_stream)
    group_pair = exchanged_grad(1, [], [normed_cross, states], [(0, [dq]), (1, [dk]), (1, [dv])], rows)
    group_out = exchanged_grad(
        2, [], [branch_cross, branch_self], [(0, [mixed_cross]), (1, [mixed_self])], rows
    )
    grad_mixed = project_both(branch_self, self_all, 3 * width, width)
    pairs = width // LANES
    cut = 2 * pairs // 3
    early = self_attend_back(
        3, [("x1", group_pair), ("y1", group_pair)], qkv, grad_mixed, lse, width, 0, cut
    )
    activated, early = lax.optimization_barrier((activated, early))
    output = unproject_both(
        4, [("x1", group_out), ("y1", group_out)], [(a, m, 0) for m, a in enumerate(activated)], out_all, 0, hidden, after_cross
    )
    swap_output = Holder(other_frames(output))
    group_early = exchanged_grad(
        5, [("x0", swap_text), ("x2", group_pair), ("y2", group_pair)], [normed_self], [(0, list(early))], rows
    )
    late = self_attend_back(
        6,
        [
            ("x2", group_out),
            ("y2", group_out),
            ("za", group_pair),
            ("zb", group_pair),
            ("x0", swap_output),
        ],
        qkv,
        grad_mixed,
        lse,
        width,
        cut,
        pairs,
    )
    group_late = exchanged_grad(
        7, [("x1", group_early), ("y1", group_early)], [normed_self], [(0, list(late))], rows
    )
    pieces = []
    for half in both:
        for part, arrays in enumerate((early, late)):
            pieces += [(a, half, i * width + part * cut * LANES) for i, a in enumerate(arrays)]
    grad_normed = unproject_both(
        8,
        [
            ("x1", group_late),
            ("y1", group_late),
            ("x2", group_early),
            ("y2", group_early),
            ("za", group_out),
            ("zb", group_out),
        ],
        pieces,
        self_all,
        0,
        3 * width,
    )
    grad_inputs, got_inputs, norm_grads = norm_back_last(
        9,
        [
            ("x2", group_late),
            ("y2", group_late),
            ("za", group_early),
            ("zb", group_early),
            ("total", group_pair),
            ("total", group_out),
        ],
        [("za", group_late), ("zb", group_late), ("total", group_early)],
        stream,
        grad_normed,
        norms[0:1],
        grad_stream,
        jnp.pad(jnp.stack([gain_two, bias_two, gain_three, bias_three]), ((2, 2), (0, 0))),
    )
    norm_grads = norm_grads[:6]
    grad_inputs = own_frames(grad_inputs, got_inputs)
    grad_text = own_frames(grad_text, swap_text.got())
    output = own_frames(output, swap_output.got())
    shard_pair, shard_outs = group_pair.arrays["total"], group_out.arrays["total"]
    halves = [group_early.arrays["total"], group_late.result(z)]
    sizes = [cut * LANES, width - cut * LANES]
    shard_self = [
        joined([h[:, i * n : (i + 1) * n] for h, n in zip(halves, sizes)]) for i in range(3)
    ]

    shard_norms = lax.dynamic_slice_in_dim(norm_grads, dp * rows, rows, 1).T

    return (
        output,
        grad_inputs,
        grad_text,
        shard_norms,
        jnp.stack(shard_self[:2], axis=1),
        shard_self[2],
        shard_outs[:, width:],
        shard_pair[:, :width],
        shard_pair[:, width:].reshape(rows, 2, width),
        shard_outs[:, :width],
        shard_hidden[:, :hidden],
        shard_hidden[:, hidden:],
        factors,
        *clipped,
    )


def solution(mesh):
    in_specs = (
        P("dp", "mp", None),
        P("dp", "mp", None),
        P("dp", "mp", None),
        P("dp", None),
        P("dp", None, "mp"),
        P("dp", "mp"),
        P("dp", "mp"),
        P("dp", "mp"),
        P("dp", None, "mp"),
        P("dp", "mp"),
        P("dp", "mp"),
        P("dp", "mp"),
    )
    out_specs = (
        P("dp", "mp", None),
        P("dp", "mp", None),
        P("dp", "mp", None),
        P("dp", None),
        P("dp", None, "mp"),
        P("dp", "mp"),
        P("dp", "mp"),
        P("dp", "mp"),
        P("dp", None, "mp"),
        P("dp", "mp"),
        P("dp", "mp"),
        P("dp", "mp"),
        P(None, "mp"),
        P("dp", None, "mp"),
        P("dp", "mp"),
        P("dp", "mp"),
    )
    by_clip = mesh.shape["mp"] == 2 and mesh.shape["dp"] == 16
    return jax.shard_map(
        clip_per_device if by_clip else per_device, mesh=mesh, in_specs=in_specs, out_specs=out_specs, check_vma=False
    )
```
